128 devices in a mesh: grp: 4 (over z), sub: 32 (over y, x, core).
Axes of the slice: x: 4, y: 4, z: 4, core: 2. Of those that a mesh axis runs over, the one named last changes fastest.
Arguments:
- points: bfloat16 [524288, 256], P(('grp', 'sub'))
- weights: bfloat16 [64, 524288], P(None, ('grp', 'sub')), may hold values from -6 to 6
- near: int32 [1024, 8], replicated, may hold values from 0 to 1023, as said below
- counts: int32 [1024], replicated, may hold values from 2 to 8, as said below
- skel_leaf: int32 [1024, 256], P(('grp', 'sub')), may hold values from 0 to 511, as said below
- skel_local: int32 [896, 256], P(('grp', 'sub')), may hold values from 0 to 511, as said below
- skel_upper: int32 [126, 256], replicated, may hold values from 0 to 511, as said below
Outputs:
- spread: float32 [64, 524288], P(None, ('grp', 'sub'))
The draws below stay inside these ranges and needn't reach their ends.
Inputs may be any that keep to these rules, and one draw needn't show every extreme that they name: `near`: slot 0 of a leaf's row is the leaf itself; the other entries of a row are different leaves of other devices with the same index of grp. All slots of the rows of one device name at most one leaf of any other device. `counts`: the live slots over the leaves of one device number at most 48, and exactly 48 on one device. `skel_leaf`: the entries of a row are different. `skel_local`: the entries of a row are different. `skel_upper`: the entries of a row are different.
All inputs are finite; a program needn't handle non-finite values.
Results may differ from the reference program's by a relative error of at most 0.0023.
Values may be sent and summed in bfloat16 or wider, within the bound.
No kernel may reach another device: no remote copies, remote signals or barrier semaphores. Data moves between devices by JAX's collectives and lax.ppermute only.
A program may use at most 128 MiB of HBM per device.

```python
import math
import jax
import jax.numpy as jnp
from jax import lax

D = 256
C = 64
P_SIZE = 512
S = 256
NEAR = 8
LD = 8
LEAVES = 1024
POINTS = 524288
LOCAL = 896
UPPER = 126
N_GRP = 4
N_SUB = 32


def draw_points(key, part):
    values = jax.random.normal(key, (POINTS, D), jnp.float32)
    return (values * (1.0 / D ** 0.5)).astype(jnp.bfloat16)


def draw_near(key, part):
    device_count = LEAVES // LD
    shift_key, pick_key = jax.random.split(key)
    shifts = jax.random.randint(shift_key, (device_count,), 0, N_SUB - 1)
    picks = jax.random.randint(pick_key, (device_count, N_SUB), 0, LD)
    leaf_ids = jnp.arange(LEAVES, dtype=jnp.int32)
    owners = leaf_ids // LD
    within = leaf_ids % LD
    groups = owners // N_SUB
    members = owners % N_SUB
    ahead = jnp.arange(1, NEAR, dtype=jnp.int32)
    offsets = 1 + (shifts[owners][:, None] + within[:, None] * (NEAR - 1) + ahead[None, :] - 1) % (N_SUB - 1)
    partners = (members[:, None] + offsets) % N_SUB
    chosen = picks[owners[:, None], partners]
    remote = (groups[:, None] * N_SUB + partners) * LD + chosen
    return jnp.concatenate([leaf_ids[:, None], remote], axis=1).astype(jnp.int32)


def draw_counts(key, part):
    device_count = LEAVES // LD
    busy_key, base_key, pair_key = jax.random.split(key, 3)
    busiest = jax.random.randint(busy_key, (), 0, device_count)
    base = jax.random.randint(base_key, (LEAVES,), 2, 5)
    swing = jax.random.randint(pair_key, (LEAVES // 2,), -2, 3)
    swing = jnp.where(jnp.arange(LEAVES // 2) % (LD // 2) == 0, 2, swing)
    paired = jnp.stack([swing, -swing], axis=1).reshape(LEAVES)
    owners = jnp.arange(LEAVES) // LD
    return jnp.where(owners == busiest, 6 + paired, base).astype(jnp.int32)


def choose_rows(key, row_count, pool, count):
    keys = jax.random.split(key, row_count)

    def pick_one(row_key):
        return jax.random.permutation(row_key, pool)[:count]
    return jax.vmap(pick_one)(keys).astype(jnp.int32)


def draw_skel_leaf(key, part):
    return choose_rows(key, LEAVES, P_SIZE, S)


def draw_skel_local(key, part):
    return choose_rows(key, LOCAL, 2 * S, S)


def draw_skel_upper(key, part):
    return choose_rows(key, UPPER, 2 * S, S)


def shard_levels(key, shape, pieces, least, largest):
    factor_of = 1.0
    for dim, shards_of in pieces:
        draws = jax.random.uniform(jax.random.fold_in(jax.random.fold_in(key, 6), dim), (shards_of,), jnp.float32, least / len(pieces), largest / len(pieces))
        factor_of = factor_of * jnp.repeat(jnp.exp(draws), shape[dim] // shards_of).reshape((-1,) + (1,) * (len(shape) - 1 - dim))
    return factor_of


def normal_values(own_key, shape, spread, most, pieces=(), kind=jnp.bfloat16):
    level = shard_levels(own_key, shape, pieces, -0.22, 0.18) if pieces else 1.0
    values = jax.random.normal(own_key, shape, jnp.float32) * spread * level
    return jnp.minimum(jnp.maximum(values, -most), most).astype(kind)


def setup_inputs(seed: int = 0) -> dict:
    splits = jax.random.split(jax.random.key(seed), 8)
    points = draw_points(jax.random.fold_in(splits[7], 71), 0)
    weights = normal_values(splits[1], (C, POINTS), 1.0, 6.0, ((1, 128),))
    near = draw_near(jax.random.fold_in(splits[7], 71), 0)
    counts = draw_counts(jax.random.fold_in(splits[7], 71), 0)
    skel_leaf = draw_skel_leaf(jax.random.fold_in(splits[7], 71), 0)
    skel_local = draw_skel_local(jax.random.fold_in(splits[7], 71), 0)
    skel_upper = draw_skel_upper(jax.random.fold_in(splits[7], 71), 0)
    return dict(points=points, weights=weights, near=near, counts=counts, skel_leaf=skel_leaf, skel_local=skel_local, skel_upper=skel_upper)


def affinity(left, right):
    left_wide = left.astype(jnp.float32)
    right_wide = right.astype(jnp.float32)
    sharpness = math.sqrt(left.shape[-1] / 8.0)
    inner = jnp.einsum('...ad,...bd->...ab', left_wide, right_wide)
    left_norms = lax.optimization_barrier(jnp.sum(left_wide * left_wide, axis=-1))
    right_norms = lax.optimization_barrier(jnp.sum(right_wide * right_wide, axis=-1))
    spacing = left_norms[..., :, None] + right_norms[..., None, :] - 2.0 * inner
    return jnp.exp(sharpness * (2.0 - spacing) - 0.5)

def take_one(block, chosen):
    return block[chosen]

def pick_rows(block, chosen):
    return jax.vmap(take_one)(block, chosen)

def reference(points, weights, near, counts, skel_leaf, skel_local, skel_upper):
    devices = N_GRP * N_SUB
    inverse_leaf = 1.0 / math.sqrt(P_SIZE)
    inverse_rank = 1.0 / S
    inverse_pair = 1.0 / (math.sqrt(2.0) * S)
    leaf_points = points.reshape(LEAVES, P_SIZE, D)
    leaf_weights = weights.reshape(C, LEAVES, P_SIZE).transpose(1, 0, 2)
    slot_ids = jnp.arange(NEAR, dtype=jnp.int32)
    diagonal = jnp.eye(P_SIZE, dtype=bool)

    def near_leaf(payload):
        near_row, live_count, leaf_number = payload
        source_points = leaf_points[near_row]
        source_weights = leaf_weights[near_row]
        target = jnp.broadcast_to(leaf_points[leaf_number][None], source_points.shape)
        kernel_tile = affinity(source_points, target)
        same = (near_row == leaf_number)[:, None, None] & diagonal[None]
        kernel_tile = jnp.where(same, 0.0, kernel_tile).astype(jnp.bfloat16)
        live = (slot_ids < live_count).astype(jnp.bfloat16)
        source_weights = source_weights * live[:, None, None]
        return jnp.einsum('mcp,mpq->cq', source_weights.astype(jnp.float32), kernel_tile.astype(jnp.float32))
    near_part = lax.map(near_leaf, (near, counts, jnp.arange(LEAVES, dtype=jnp.int32)))
    skel_points = pick_rows(leaf_points, skel_leaf)
    upward = affinity(leaf_points, skel_points)
    upward = jnp.where(jnp.arange(P_SIZE)[None, :, None] == skel_leaf[:, None, :], 0.0, upward).astype(jnp.bfloat16)
    summary = (jnp.einsum('lcp,lps->lcs', leaf_weights.astype(jnp.float32), upward.astype(jnp.float32)) * inverse_leaf).astype(jnp.bfloat16)
    local_depth = LD.bit_length() - 1
    total_depth = local_depth + devices.bit_length() - 1
    level_points = [skel_points]
    level_summary = [summary]
    level_kernels = [upward]
    local_rows = skel_local.reshape(devices, LD - 1, S)
    for height in range(1, total_depth):
        node_count = LEAVES >> height
        if height <= local_depth:
            offset = LD - (LD >> height - 1)
            chosen = local_rows[:, offset:offset + (LD >> height)].reshape(node_count, S)
        else:
            upper_height = height - local_depth
            offset = devices - (devices >> upper_height - 1)
            chosen = skel_upper[offset:offset + node_count]
        child_points = skel_points.reshape(node_count, 2 * S, D)
        child_summary = summary.reshape(node_count, 2, C, S).transpose(0, 2, 1, 3).reshape(node_count, C, 2 * S)
        skel_points = pick_rows(child_points, chosen)
        lifted = affinity(child_points, skel_points)
        same = jnp.arange(2 * S)[None, :, None] == chosen[:, None, :]
        lifted = jnp.where(same, 0.0, lifted).astype(jnp.bfloat16)
        summary = (jnp.einsum('ncr,nrs->ncs', child_summary.astype(jnp.float32), lifted.astype(jnp.float32)) * inverse_pair).astype(jnp.bfloat16)
        level_points.append(skel_points)
        level_summary.append(summary)
        level_kernels.append(lifted)
    level_terms = []
    for height in range(total_depth):
        node_points = level_points[height]
        node_summary = level_summary[height]
        sibling = jnp.arange(node_points.shape[0]) ^ 1
        kernel_tile = affinity(node_points[sibling], node_points).astype(jnp.bfloat16)
        level_terms.append(jnp.einsum('ncs,nst->nct', node_summary[sibling].astype(jnp.float32), kernel_tile.astype(jnp.float32)) * inverse_rank)
    value = level_terms[total_depth - 1].astype(jnp.bfloat16)
    for height in range(total_depth - 2, -1, -1):
        lifted = level_kernels[height + 1]
        parents = lifted.shape[0]
        down = jnp.einsum('nct,nrt->ncr', value.astype(jnp.float32), lifted.astype(jnp.float32))
        down = down.reshape(parents, C, 2, S).transpose(0, 2, 1, 3).reshape(2 * parents, C, S)
        value = (level_terms[height] + down * inverse_rank).astype(jnp.bfloat16)
    far_part = jnp.einsum('lcs,lps->lcp', value.astype(jnp.float32), level_kernels[0].astype(jnp.float32)) * inverse_rank
    result = near_part * inverse_leaf + far_part
    return result.transpose(1, 0, 2).reshape(C, POINTS)
```

```python
import functools
import math

import jax
import jax.numpy as jnp
from jax import lax
from jax.experimental import pallas as pl
from jax.experimental.pallas import tpu as pltpu
from jax.sharding import PartitionSpec as P

F32 = jnp.float32
BF16 = jnp.bfloat16
LOG2E = 1.4426950408889634
NT = (((1,), (1,)), ((), ()))
LAST_ROWS = 128


def call(kernel, name, flops, exps, nbytes, vmem=12, **kw):
    return pl.pallas_call(
        kernel,
        name=name,
        cost_estimate=pl.CostEstimate(flops=flops, bytes_accessed=nbytes, transcendentals=exps),
        compiler_params=pltpu.CompilerParams(vmem_limit_bytes=vmem * 2**20),
        **kw,
    )


def dot(a, b):
    return jnp.dot(a, b, preferred_element_type=F32)


def dot_nt(a, b):
    return lax.dot_general(a, b, NT, preferred_element_type=F32)


def half_exponents(block):
    sharpness = math.sqrt(block.shape[-1] / 8.0)
    wide = block.astype(F32)
    norms = jnp.sum(wide * wide, axis=-1, keepdims=True)
    return LOG2E * (sharpness * (1.0 - norms) - 0.25)


def as_row(column):
    rows = column.shape[0]
    return jnp.transpose(jnp.broadcast_to(column, (rows, 128)))[0:1, :]


def kappa(left, right, left_half, right_half_row):
    scale = LOG2E * 2.0 * math.sqrt(left.shape[-1] / 8.0)
    return jnp.exp2(dot_nt(left, right) * scale + left_half + right_half_row)


def one_hot(chosen_row, pool):
    rank = chosen_row.shape[1]
    spread = jnp.transpose(jnp.broadcast_to(chosen_row, (128, rank)).astype(F32)).astype(jnp.int32)
    lanes = lax.broadcasted_iota(jnp.int32, (rank, 128), 1)
    pieces = [
        jnp.where(spread == lanes + 128 * j, 1.0, 0.0).astype(BF16) for j in range(pool // 128)
    ]
    return jnp.concatenate(pieces, axis=1)


def pack_kernel(
    leaf_size, first, rows, with_weights, chosen, points_ref, weights_ref, out_ref, sems
):
    classes = weights_ref.shape[0]
    half = leaf_size // 2

    def copies(j):
        leaf = chosen[j]
        start = pl.multiple_of(leaf * leaf_size + first, 128)
        made = [
            pltpu.make_async_copy(
                points_ref.at[pl.ds(start, rows), :],
                out_ref.at[j, pl.ds(0, rows), :],
                sems.at[j, 0],
            )
        ]
        if with_weights:
            for piece in range(2):
                column = pl.multiple_of(leaf * leaf_size + piece * half, 128)
                made.append(
                    pltpu.make_async_copy(
                        weights_ref.at[:, pl.ds(column, half)],
                        out_ref.at[j, pl.ds(rows + piece * classes, classes), :],
                        sems.at[j, 1 + piece],
                    )
                )
        return made

    def start(j, carry):
        for copy in copies(j):
            copy.start()
        return carry

    def finish(j, carry):
        for copy in copies(j):
            copy.wait()
        return carry

    lax.fori_loop(0, out_ref.shape[0], start, 0)
    lax.fori_loop(0, out_ref.shape[0], finish, 0)


def pack(chosen, points, weights, leaf_size, first, rows, with_weights):
    total = rows + (2 * weights.shape[0] if with_weights else 0)
    shape = (chosen.shape[0], total, points.shape[1])
    return call(
        functools.partial(pack_kernel, leaf_size, first, rows, with_weights),
        "pack",
        0,
        0,
        2 * math.prod(shape) * 2,
        out_shape=pltpu.HBM(shape, BF16),
        grid_spec=pltpu.PrefetchScalarGridSpec(
            num_scalar_prefetch=1,
            grid=(1,),
            in_specs=[
                pl.BlockSpec(memory_space=pltpu.HBM),
                pl.BlockSpec(memory_space=pltpu.HBM),
            ],
            out_specs=pl.BlockSpec(memory_space=pltpu.HBM),
            scratch_shapes=[pltpu.SemaphoreType.DMA((shape[0], 3))],
        ),
    )(chosen, points, weights)


def leaf_kernel(points_ref, weights_ref, chosen_ref, own_ref, skel_ref, up_ref, summary_ref):
    leaf = pl.program_id(0)
    block = points_ref[...]
    leaf_size = block.shape[0]
    inverse_leaf = 1.0 / math.sqrt(leaf_size)
    half = half_exponents(block)
    tile = kappa(block, block, half, as_row(half))
    rows = lax.broadcasted_iota(jnp.int32, tile.shape, 0)
    columns = lax.broadcasted_iota(jnp.int32, tile.shape, 1)
    tile = jnp.where(rows == columns, 0.0, tile).astype(BF16)
    own = dot(weights_ref[...], tile) * inverse_leaf
    own_ref[...] = own
    selector = one_hot(chosen_ref[pl.ds(leaf, 1), :], leaf_size)
    skel_ref[0] = dot(selector, block).astype(BF16)
    up_ref[0] = dot_nt(tile, selector).astype(BF16)
    summary_ref[0] = dot_nt(own.astype(BF16), selector).astype(BF16)


def leaf_level(points, weights, skel_leaf):
    leaves, rank = skel_leaf.shape
    classes = weights.shape[0]
    width = points.shape[1]
    size = points.shape[0] // leaves
    return call(
        leaf_kernel,
        "leaf",
        leaves * 2 * size * (size * (width + classes + rank) + rank * width + classes * rank),
        leaves * size * size,
        8 * 2**20,
        out_shape=(
            jax.ShapeDtypeStruct(weights.shape, F32),
            jax.ShapeDtypeStruct((leaves, rank, width), BF16),
            jax.ShapeDtypeStruct((leaves, size, rank), BF16),
            jax.ShapeDtypeStruct((leaves, classes, rank), BF16),
        ),
        grid=(leaves,),
        in_specs=[
            pl.BlockSpec((size, width), lambda i: (i, 0)),
            pl.BlockSpec((classes, size), lambda i: (0, i)),
            pl.BlockSpec((leaves, rank), lambda i: (0, 0)),
        ],
        out_specs=(
            pl.BlockSpec((classes, size), lambda i: (0, i)),
            pl.BlockSpec((1, rank, width), lambda i: (i, 0, 0)),
            pl.BlockSpec((1, size, rank), lambda i: (i, 0, 0)),
            pl.BlockSpec((1, classes, rank), lambda i: (i, 0, 0)),
        ),
    )(points, weights, skel_leaf)


def local_kernel(skel_ref, summary_ref, chosen_ref, lifted_ref, terms_ref, state_ref, nodes, sums):
    leaves, rank, width = skel_ref.shape
    classes = summary_ref.shape[1]
    inverse_rank = 1.0 / rank
    inverse_pair = 1.0 / (math.sqrt(2.0) * rank)
    nodes[pl.ds(0, leaves)] = skel_ref[...]
    sums[pl.ds(0, leaves)] = summary_ref[...]

    def step(i, carry):
        even, odd = nodes[2 * i], nodes[2 * i + 1]
        even_sum, odd_sum = sums[2 * i], sums[2 * i + 1]
        child = jnp.concatenate([even, odd], axis=0)
        chosen = chosen_ref[pl.ds(i, 1), :]
        half = half_exponents(child)
        parent = dot(one_hot(chosen, 2 * rank), child).astype(BF16)
        lifted = kappa(child, parent, half, as_row(half_exponents(parent)))
        same = lax.broadcasted_iota(jnp.int32, lifted.shape, 0) == chosen
        lifted = jnp.where(same, 0.0, lifted).astype(BF16)
        lifted_ref[i] = lifted
        summed = dot(even_sum, lifted[:rank]) + dot(odd_sum, lifted[rank:])
        nodes[leaves + i] = parent
        sums[leaves + i] = (summed * inverse_pair).astype(BF16)
        tile = kappa(even, odd, half[:rank], as_row(half[rank:])).astype(BF16)
        terms_ref[2 * i] = dot_nt(odd_sum, tile) * inverse_rank
        terms_ref[2 * i + 1] = dot(even_sum, tile) * inverse_rank
        return carry

    lax.fori_loop(0, leaves - 1, step, 0)
    state_ref[pl.ds(0, rank), :] = nodes[2 * leaves - 2]
    state_ref[pl.ds(rank, classes), :] = sums[2 * leaves - 2]


def local_levels(skel, summary, skel_local):
    leaves, rank, width = skel.shape
    classes = summary.shape[1]
    inner = leaves - 1
    return call(
        local_kernel,
        "local",
        inner * 2 * rank * rank * (5 * width + 4 * classes),
        inner * 3 * rank * rank,
        6 * 2**20,
        out_shape=(
            jax.ShapeDtypeStruct((inner, 2 * rank, rank), BF16),
            jax.ShapeDtypeStruct((2 * inner, classes, rank), F32),
            jax.ShapeDtypeStruct((rank + classes, width), BF16),
        ),
        scratch_shapes=[
            pltpu.VMEM((2 * leaves, rank, width), BF16),
            pltpu.VMEM((2 * leaves, classes, rank), BF16),
        ],
    )(skel, summary, skel_local)


def meet(mine, far, mine_row, far_half, far_sum):
    tile = kappa(far, mine, far_half, mine_row).astype(BF16)
    return dot(far_sum, tile) * (1.0 / far.shape[0])


def rise_kernel(level, numbers, mine_ref, far_ref, chosen_ref, state_ref, lifted_ref, term_ref):
    classes, rank = term_ref.shape
    inverse_pair = 1.0 / (math.sqrt(2.0) * rank)
    mine, far = mine_ref[pl.ds(0, rank), :], far_ref[pl.ds(0, rank), :]
    mine_sum, far_sum = mine_ref[pl.ds(rank, classes), :], far_ref[pl.ds(rank, classes), :]
    side, row = numbers[2 * level], numbers[2 * level + 1]
    chosen = lax.rem(chosen_ref[pl.ds(row, 1), :] + side * rank, 2 * rank)
    child = jnp.concatenate([mine, far], axis=0)
    half = half_exponents(child)
    parent = dot(one_hot(chosen, 2 * rank), child).astype(BF16)
    lifted = kappa(child, parent, half, as_row(half_exponents(parent)))
    same = lax.broadcasted_iota(jnp.int32, lifted.shape, 0) == chosen
    lifted = jnp.where(same, 0.0, lifted).astype(BF16)
    summed = dot(mine_sum, lifted[:rank]) + dot(far_sum, lifted[rank:])
    state_ref[pl.ds(0, rank), :] = parent
    state_ref[pl.ds(rank, classes), :] = (summed * inverse_pair).astype(BF16)
    lifted_ref[...] = lifted[:rank]
    term_ref[...] = meet(mine, far, as_row(half[:rank]), half[rank:], far_sum)


def rise(level, numbers, mine, far, skel_upper):
    rank = skel_upper.shape[1]
    classes = mine.shape[0] - rank
    width = mine.shape[1]
    whole = lambda shape: pl.BlockSpec(shape, lambda i, n: (0, 0))
    return call(
        functools.partial(rise_kernel, level),
        "rise",
        2 * rank * rank * (5 * width + 3 * classes),
        3 * rank * rank,
        2**20,
        out_shape=(
            jax.ShapeDtypeStruct(mine.shape, BF16),
            jax.ShapeDtypeStruct((rank, rank), BF16),
            jax.ShapeDtypeStruct((classes, rank), F32),
        ),
        grid_spec=pltpu.PrefetchScalarGridSpec(
            num_scalar_prefetch=1,
            grid=(1,),
            in_specs=[whole(mine.shape), whole(mine.shape), whole(skel_upper.shape)],
            out_specs=(whole(mine.shape), whole((rank, rank)), whole((classes, rank))),
        ),
    )(numbers, mine, far, skel_upper)


def down_kernel(path, *refs):
    mine_ref, far_ref = refs[:2]
    path_terms = refs[2 : 2 + path]
    path_lifted = refs[2 + path : 2 + 2 * path]
    lifted_ref, terms_ref, up_ref, own_ref, out_ref, values = refs[2 + 2 * path :]
    inner, _, rank = lifted_ref.shape
    leaves, size, _ = up_ref.shape
    classes = own_ref.shape[0]
    inverse_rank = 1.0 / rank
    mine, far = mine_ref[pl.ds(0, rank), :], far_ref[pl.ds(0, rank), :]
    top = meet(
        mine,
        far,
        as_row(half_exponents(mine)),
        half_exponents(far),
        far_ref[pl.ds(rank, classes), :],
    )
    value = top.astype(BF16)
    for level in range(path - 1, -1, -1):
        down = dot_nt(value, path_lifted[level][...])
        value = (path_terms[level][...] + down * inverse_rank).astype(BF16)
    values[2 * leaves - 2] = value

    def lower(step, carry):
        i = inner - 1 - step
        down = dot_nt(values[leaves + i], lifted_ref[i]) * inverse_rank
        values[2 * i] = (terms_ref[2 * i] + down[:, :rank]).astype(BF16)
        values[2 * i + 1] = (terms_ref[2 * i + 1] + down[:, rank:]).astype(BF16)
        return carry

    lax.fori_loop(0, inner, lower, 0)
    for leaf in range(leaves):
        columns = pl.ds(leaf * size, size)
        spread = dot_nt(values[leaf], up_ref[leaf]) * inverse_rank
        out_ref[:, columns] = own_ref[:, columns] + spread


def down(mine, far, path_terms, path_lifted, lifted, terms, up, own):
    path = len(path_terms)
    leaves, size, rank = up.shape
    classes = own.shape[0]
    return call(
        functools.partial(down_kernel, path),
        "down",
        2 * classes * rank * (path * rank + leaves * size * 2),
        rank * rank,
        8 * 2**20,
        out_shape=jax.ShapeDtypeStruct(own.shape, F32),
        scratch_shapes=[pltpu.VMEM((2 * leaves, classes, rank), BF16)],
    )(mine, far, *path_terms, *path_lifted, lifted, terms, up, own)


def near_kernel(first, rows, sources, live, points_ref, start_ref, *refs):
    out_ref, block_buf, weight_buf, total, cursor, sems = refs[-6:]
    block_ref = refs[0]
    weight_ref = refs[len(refs) - 7]
    leaf = pl.program_id(0)
    leaves = pl.num_programs(0)
    slots = sources.shape[0] // live.shape[0]
    classes, size = out_ref.shape
    weight_rows = weight_ref.shape[1] - 2 * classes
    half_size = size // 2
    inverse_leaf = 1.0 / math.sqrt(size)
    count = live[leaf]

    def copies(leaf_number, slot, buffer):
        source = sources[leaf_number * slots + slot]
        return [
            pltpu.make_async_copy(
                block_ref.at[source, pl.ds(0, rows), :], block_buf.at[buffer], sems.at[buffer, 0]
            ),
            pltpu.make_async_copy(
                weight_ref.at[source, pl.ds(weight_rows, 2 * classes), :],
                weight_buf.at[buffer],
                sems.at[buffer, 1],
            ),
        ]

    @pl.when(leaf == 0)
    def _():
        cursor[0] = 0
        for copy in copies(0, 1, 0):
            copy.start()

    target = points_ref[...]
    target_row = as_row(half_exponents(target))
    total[...] = jnp.zeros_like(total)
    base = cursor[0]

    def step(slot, carry):
        buffer = lax.rem(base + slot - 1, 2)
        for copy in copies(leaf, slot, buffer):
            copy.wait()
        more = slot + 1 < count

        @pl.when(jnp.logical_or(more, leaf + 1 < leaves))
        def _():
            next_leaf = jnp.where(more, leaf, leaf + 1)
            next_slot = jnp.where(more, slot + 1, 1)
            for copy in copies(next_leaf, next_slot, 1 - buffer):
                copy.start()

        block = block_buf[buffer]
        tile = kappa(block, target, half_exponents(block), target_row).astype(BF16)
        done = 0
        added = None
        for piece in range(2):
            low, high = max(first, piece * half_size), min(first + rows, (piece + 1) * half_size)
            if low < high:
                weights = weight_buf[
                    buffer,
                    pl.ds(piece * classes, classes),
                    pl.ds(low - piece * half_size, high - low),
                ]
                term = dot(weights, tile[done : done + high - low])
                added = term if added is None else added + term
                done += high - low
        total[...] += added
        return carry

    lax.fori_loop(1, count, step, 0)
    cursor[0] = base + count - 1
    out_ref[...] = start_ref[...] + total[...] * inverse_leaf


def near_part(first, rows, sources, live, points, start, blocks, weight_blocks):
    leaves = live.shape[0]
    size = points.shape[0] // leaves
    width = points.shape[1]
    classes = start.shape[0]
    operands = [blocks] if weight_blocks is blocks else [blocks, weight_blocks]
    tiles = 24
    return call(
        functools.partial(near_kernel, first, rows),
        "near",
        tiles * 2 * rows * size * (width + classes),
        tiles * rows * size,
        tiles * rows * width * 2 + 4 * 2**20,
        out_shape=jax.ShapeDtypeStruct(start.shape, F32),
        grid_spec=pltpu.PrefetchScalarGridSpec(
            num_scalar_prefetch=2,
            grid=(leaves,),
            in_specs=[
                pl.BlockSpec((size, width), lambda i, s, n: (i, 0)),
                pl.BlockSpec((classes, size), lambda i, s, n: (0, i)),
            ]
            + [pl.BlockSpec(memory_space=pltpu.HBM) for _ in operands],
            out_specs=pl.BlockSpec((classes, size), lambda i, s, n: (0, i)),
            scratch_shapes=[
                pltpu.VMEM((2, rows, width), BF16),
                pltpu.VMEM((2, 2 * classes, width), BF16),
                pltpu.VMEM((classes, size), F32),
                pltpu.SMEM((1,), jnp.int32),
                pltpu.SemaphoreType.DMA((2, 2)),
            ],
        ),
    )(sources, live, points, start, *operands)


def swap(value, axis, bit):
    pairs = [(source, source ^ (1 << bit)) for source in range(lax.axis_size(axis))]
    return lax.ppermute(value, axis, pairs)


def per_device(points, weights, near, counts, skel_leaf, skel_local, skel_upper):
    leaves, rank = skel_leaf.shape
    size = points.shape[0] // leaves
    slots = near.shape[1]
    sub_count = lax.axis_size("sub")
    grp_count = lax.axis_size("grp")
    devices = sub_count * grp_count
    sub_index = lax.axis_index("sub")
    grp_index = lax.axis_index("grp")
    device = grp_index * sub_count + sub_index
    sub_bits = sub_count.bit_length() - 1
    grp_bits = grp_count.bit_length() - 1
    path = sub_bits + grp_bits - 1

    group_first = grp_index * sub_count * leaves
    slot_ids = jnp.arange(slots)
    group_rows = lax.dynamic_slice_in_dim(near, group_first, sub_count * leaves, 0)
    group_counts = lax.dynamic_slice_in_dim(counts, group_first, sub_count * leaves, 0)
    owned = (
        (group_rows // leaves == device)
        & (slot_ids[None, :] < group_counts[:, None])
        & (slot_ids[None, :] > 0)
    )
    chosen = jnp.where(owned, group_rows - device * leaves, 0).reshape(sub_count, leaves * slots)
    chosen = jnp.max(chosen, axis=1)

    first_rows = size - LAST_ROWS
    sent = pack(chosen, points, weights, size, 0, first_rows, True)
    arrived = lax.all_to_all(sent, "sub", split_axis=0, concat_axis=0, tiled=True)

    own, skel, up, summary = leaf_level(points, weights, skel_leaf)
    lifted, terms, state = local_levels(skel, summary, skel_local)
    numbers = []
    for level in range(path):
        numbers.append(device >> level & 1)
        numbers.append(devices - (devices >> level) + (device >> level + 1))
    numbers = jnp.stack(numbers).astype(jnp.int32)
    path_terms, path_lifted = [], []
    for level in range(path + 1):
        if level < sub_bits:
            far = swap(state, "sub", level)
        else:
            far = swap(state, "grp", level - sub_bits)
        if level < path:
            state, lifted_mine, term = rise(level, numbers, state, far, skel_upper)
            path_lifted.append(lifted_mine)
            path_terms.append(term)
    total = down(state, far, path_terms, path_lifted, lifted, terms, up, own)

    sent_last = pack(chosen, points, weights, size, first_rows, LAST_ROWS, False)
    sent_last, total = lax.optimization_barrier((sent_last, total))
    arrived_last = lax.all_to_all(sent_last, "sub", split_axis=0, concat_axis=0, tiled=True)

    my_rows = lax.dynamic_slice_in_dim(near, device * leaves, leaves, 0)
    sources = (my_rows // leaves % sub_count).reshape(-1)
    live = lax.dynamic_slice_in_dim(counts, device * leaves, leaves, 0)
    total = near_part(0, first_rows, sources, live, points, total, arrived, arrived)
    return near_part(
        first_rows, LAST_ROWS, sources, live, points, total, arrived_last, arrived
    )


def solution(mesh):
    split = P(("grp", "sub"), None)
    columns = P(None, ("grp", "sub"))
    return jax.shard_map(
        per_device,
        mesh=mesh,
        in_specs=(split, columns, P(), P(), split, split, P()),
        out_specs=columns,
        check_vma=False,
    )
```

```python
import functools
import math

import jax
import jax.numpy as jnp
import numpy as np
from jax import lax
from jax.experimental import pallas as pl
from jax.experimental.pallas import tpu as pltpu
from jax.sharding import PartitionSpec as P

F32 = jnp.float32
BF16 = jnp.bfloat16
LOG2E = 1.4426950408889634
NT = (((1,), (1,)), ((), ()))
LAST_ROWS = 128
NEIGHBOURS = 8


def call(kernel, name, flops, exps, nbytes, vmem=12, **kw):
    return pl.pallas_call(
        kernel,
        name=name,
        cost_estimate=pl.CostEstimate(flops=flops, bytes_accessed=nbytes, transcendentals=exps),
        compiler_params=pltpu.CompilerParams(vmem_limit_bytes=vmem * 2**20),
        **kw,
    )


def dot(a, b):
    return jnp.dot(a, b, preferred_element_type=F32)


def dot_nt(a, b):
    return lax.dot_general(a, b, NT, preferred_element_type=F32)


def half_exponents(block):
    sharpness = math.sqrt(block.shape[-1] / 8.0)
    wide = block.astype(F32)
    norms = jnp.sum(wide * wide, axis=-1, keepdims=True)
    return LOG2E * (sharpness * (1.0 - norms) - 0.25)


def as_row(column):
    rows = column.shape[0]
    return jnp.transpose(jnp.broadcast_to(column, (rows, 128)))[0:1, :]


def kappa(left, right, left_half, right_half_row):
    scale = LOG2E * 2.0 * math.sqrt(left.shape[-1] / 8.0)
    return jnp.exp2(dot_nt(left, right) * scale + left_half + right_half_row)


def one_hot(chosen_row, pool):
    rank = chosen_row.shape[1]
    spread = jnp.transpose(jnp.broadcast_to(chosen_row, (128, rank)).astype(F32)).astype(jnp.int32)
    lanes = lax.broadcasted_iota(jnp.int32, (rank, 128), 1)
    pieces = [
        jnp.where(spread == lanes + 128 * j, 1.0, 0.0).astype(BF16) for j in range(pool // 128)
    ]
    return jnp.concatenate(pieces, axis=1)


def pack_kernel(
    leaf_size, first, rows, with_weights, chosen, points_ref, weights_ref, out_ref, sems
):
    classes = weights_ref.shape[0]
    half = leaf_size // 2

    def copies(j):
        leaf = chosen[j]
        start = pl.multiple_of(leaf * leaf_size + first, 128)
        made = [
            pltpu.make_async_copy(
                points_ref.at[pl.ds(start, rows), :],
                out_ref.at[j, pl.ds(0, rows), :],
                sems.at[j, 0],
            )
        ]
        if with_weights:
            for piece in range(2):
                column = pl.multiple_of(leaf * leaf_size + piece * half, 128)
                made.append(
                    pltpu.make_async_copy(
                        weights_ref.at[:, pl.ds(column, half)],
                        out_ref.at[j, pl.ds(rows + piece * classes, classes), :],
                        sems.at[j, 1 + piece],
                    )
                )
        return made

    def start(j, carry):
        for copy in copies(j):
            copy.start()
        return carry

    def finish(j, carry):
        for copy in copies(j):
            copy.wait()
        return carry

    lax.fori_loop(0, out_ref.shape[0], start, 0)
    lax.fori_loop(0, out_ref.shape[0], finish, 0)


def pack(chosen, points, weights, leaf_size, first, rows, with_weights):
    total = rows + (2 * weights.shape[0] if with_weights else 0)
    shape = (chosen.shape[0], total, points.shape[1])
    return call(
        functools.partial(pack_kernel, leaf_size, first, rows, with_weights),
        "pack",
        0,
        0,
        2 * math.prod(shape) * 2,
        out_shape=pltpu.HBM(shape, BF16),
        grid_spec=pltpu.PrefetchScalarGridSpec(
            num_scalar_prefetch=1,
            grid=(1,),
            in_specs=[
                pl.BlockSpec(memory_space=pltpu.HBM),
                pl.BlockSpec(memory_space=pltpu.HBM),
            ],
            out_specs=pl.BlockSpec(memory_space=pltpu.HBM),
            scratch_shapes=[pltpu.SemaphoreType.DMA((shape[0], 3))],
        ),
    )(chosen, points, weights)


def leaf_kernel(points_ref, weights_ref, chosen_ref, own_ref, skel_ref, up_ref, summary_ref):
    leaf = pl.program_id(0)
    block = points_ref[...]
    leaf_size = block.shape[0]
    inverse_leaf = 1.0 / math.sqrt(leaf_size)
    half = half_exponents(block)
    tile = kappa(block, block, half, as_row(half))
    rows = lax.broadcasted_iota(jnp.int32, tile.shape, 0)
    columns = lax.broadcasted_iota(jnp.int32, tile.shape, 1)
    tile = jnp.where(rows == columns, 0.0, tile).astype(BF16)
    own = dot(weights_ref[...], tile) * inverse_leaf
    own_ref[...] = own
    selector = one_hot(chosen_ref[pl.ds(leaf, 1), :], leaf_size)
    skel_ref[0] = dot(selector, block).astype(BF16)
    up_ref[0] = dot_nt(tile, selector).astype(BF16)
    summary_ref[0] = dot_nt(own.astype(BF16), selector).astype(BF16)


def leaf_level(points, weights, skel_leaf):
    leaves, rank = skel_leaf.shape
    classes = weights.shape[0]
    width = points.shape[1]
    size = points.shape[0] // leaves
    return call(
        leaf_kernel,
        "leaf",
        leaves * 2 * size * (size * (width + classes + rank) + rank * width + classes * rank),
        leaves * size * size,
        8 * 2**20,
        out_shape=(
            jax.ShapeDtypeStruct(weights.shape, F32),
            jax.ShapeDtypeStruct((leaves, rank, width), BF16),
            jax.ShapeDtypeStruct((leaves, size, rank), BF16),
            jax.ShapeDtypeStruct((leaves, classes, rank), BF16),
        ),
        grid=(leaves,),
        in_specs=[
            pl.BlockSpec((size, width), lambda i: (i, 0)),
            pl.BlockSpec((classes, size), lambda i: (0, i)),
            pl.BlockSpec((leaves, rank), lambda i: (0, 0)),
        ],
        out_specs=(
            pl.BlockSpec((classes, size), lambda i: (0, i)),
            pl.BlockSpec((1, rank, width), lambda i: (i, 0, 0)),
            pl.BlockSpec((1, size, rank), lambda i: (i, 0, 0)),
            pl.BlockSpec((1, classes, rank), lambda i: (i, 0, 0)),
        ),
    )(points, weights, skel_leaf)


def subtree_kernel(count, inner, states, rows, *refs):
    chosen_ref = refs[0]
    inputs = refs[1 : len(refs) - 5]
    lifted_ref, terms_ref, state_ref, nodes, sums = refs[len(refs) - 5 :]
    _, rank, width = nodes.shape
    classes = sums.shape[1]
    inverse_rank = 1.0 / rank
    inverse_pair = 1.0 / (math.sqrt(2.0) * rank)
    if states == 0:
        nodes[pl.ds(0, count)] = inputs[0][...]
        sums[pl.ds(0, count)] = inputs[1][...]
    elif states == 1:
        nodes[pl.ds(0, count)] = inputs[0][:, pl.ds(0, rank), :]
        sums[pl.ds(0, count)] = inputs[0][:, pl.ds(rank, classes), :]
    else:
        for mask in range(count):
            place = lax.bitwise_xor(rows[inner], mask)
            nodes[place] = inputs[mask][pl.ds(0, rank), :]
            sums[place] = inputs[mask][pl.ds(rank, classes), :]

    def pair(i, even, odd, even_half, odd_half):
        tile = kappa(even, odd, even_half, as_row(odd_half)).astype(BF16)
        terms_ref[2 * i] = dot_nt(sums[2 * i + 1], tile) * inverse_rank
        terms_ref[2 * i + 1] = dot(sums[2 * i], tile) * inverse_rank

    def step(i, carry):
        even, odd = nodes[2 * i], nodes[2 * i + 1]
        child = jnp.concatenate([even, odd], axis=0)
        chosen = chosen_ref[pl.ds(rows[i], 1), :]
        half = half_exponents(child)
        parent = dot(one_hot(chosen, 2 * rank), child).astype(BF16)
        lifted = kappa(child, parent, half, as_row(half_exponents(parent)))
        same = lax.broadcasted_iota(jnp.int32, lifted.shape, 0) == chosen
        lifted = jnp.where(same, 0.0, lifted).astype(BF16)
        lifted_ref[i] = lifted
        summed = dot(sums[2 * i], lifted[:rank]) + dot(sums[2 * i + 1], lifted[rank:])
        nodes[count + i] = parent
        sums[count + i] = (summed * inverse_pair).astype(BF16)
        pair(i, even, odd, half[:rank], half[rank:])
        return carry

    lax.fori_loop(0, inner, step, 0)
    if inner == count - 1:
        state_ref[pl.ds(0, rank), :] = nodes[count + inner - 1]
        state_ref[pl.ds(rank, classes), :] = sums[count + inner - 1]
    else:
        even, odd = nodes[2 * inner], nodes[2 * inner + 1]
        pair(inner, even, odd, half_exponents(even), half_exponents(odd))
        state_ref[...] = jnp.zeros_like(state_ref)


def subtree(name, count, inner, states, rows, table, inputs, classes):
    rank = table.shape[1]
    width = inputs[0].shape[-1]

    def whole(array):
        zeros = (0,) * array.ndim
        return pl.BlockSpec(array.shape, lambda i, r: zeros)

    shapes = (
        jax.ShapeDtypeStruct((inner, 2 * rank, rank), BF16),
        jax.ShapeDtypeStruct((2 * count - 2, classes, rank), F32),
        jax.ShapeDtypeStruct((rank + classes, width), BF16),
    )
    return call(
        functools.partial(subtree_kernel, count, inner, states),
        name,
        inner * 2 * rank * rank * (5 * width + 4 * classes),
        inner * 3 * rank * rank,
        6 * 2**20,
        vmem=16,
        out_shape=shapes,
        grid_spec=pltpu.PrefetchScalarGridSpec(
            num_scalar_prefetch=1,
            grid=(1,),
            in_specs=[whole(table)] + [whole(array) for array in inputs],
            out_specs=tuple(whole(shape) for shape in shapes),
            scratch_shapes=[
                pltpu.VMEM((2 * count, rank, width), BF16),
                pltpu.VMEM((2 * count, classes, rank), BF16),
            ],
        ),
    )(rows, table, *inputs)


def path_of(place, count):
    numbers = [place]
    while 2 ** len(numbers) < count:
        numbers.append(count + (numbers[-1] >> 1))
    return numbers


def place_table(near_bits, far_bits, grp_bits):
    devices = 1 << near_bits + far_bits + grp_bits

    def upper_rows(device, height, step, wanted):
        rows = []
        for u in range(height + 1, height + step + 1):
            under = 1 << (height + step - u)
            base = devices - (devices >> u - 1) + (device >> height + step) * under
            rows += [base + i for i in range(under)]
        return rows[:wanted]

    table = []
    for device in range(devices):
        near_place = device & (1 << near_bits) - 1
        far_place = device >> near_bits & (1 << far_bits) - 1
        grp_place = device >> near_bits + far_bits
        paths = [
            path_of(grp_place, 1 << grp_bits)[::-1],
            path_of(far_place, 1 << far_bits)[::-1],
            path_of(near_place, 1 << near_bits)[::-1],
        ]
        parts = [
            upper_rows(device, 0, near_bits, (1 << near_bits) - 1),
            upper_rows(device, near_bits, far_bits, (1 << far_bits) - 1) + [far_place],
            upper_rows(device, near_bits + far_bits, grp_bits, (1 << grp_bits) - 2) + [grp_place],
            [node for path in paths for node in path],
        ]
        table.append([number for part in parts for number in part])
    starts = np.cumsum([0] + [len(part) for part in parts]).tolist()
    return np.array(table, np.int32), starts, tuple(len(path) for path in paths)


def down_kernel(path, counts, numbers, *refs):
    stages = len(counts)
    lifted_ref, terms_ref, up_ref, own_ref, out_ref, values = refs[2 * stages :]
    inner, _, rank = lifted_ref.shape
    leaves, size, _ = up_ref.shape
    inverse_rank = 1.0 / rank
    value = None
    at = 0
    for stage, steps in enumerate(path):
        stage_lifted, stage_terms = refs[2 * stage], refs[2 * stage + 1]
        for _ in range(steps):
            node = numbers[at]
            at += 1
            term = stage_terms[node]
            if value is not None:
                half = pl.ds(pl.multiple_of((node & 1) * rank, rank), rank)
                child = stage_lifted[node >> 1, half, :]
                term = term + dot_nt(value, child) * inverse_rank
            value = term.astype(BF16)
    values[2 * leaves - 2] = value

    def lower(step, carry):
        i = inner - 1 - step
        down = dot_nt(values[leaves + i], lifted_ref[i]) * inverse_rank
        values[2 * i] = (terms_ref[2 * i] + down[:, :rank]).astype(BF16)
        values[2 * i + 1] = (terms_ref[2 * i + 1] + down[:, rank:]).astype(BF16)
        return carry

    lax.fori_loop(0, inner, lower, 0)
    for leaf in range(leaves):
        columns = pl.ds(leaf * size, size)
        spread = dot_nt(values[leaf], up_ref[leaf]) * inverse_rank
        out_ref[:, columns] = own_ref[:, columns] + spread


def down(numbers, path, stages, lifted, terms, up, own):
    leaves, size, rank = up.shape
    classes = own.shape[0]
    inputs = [array for stage in stages for array in stage] + [lifted, terms, up, own]

    def whole(array):
        zeros = (0,) * array.ndim
        return pl.BlockSpec(array.shape, lambda i, n: zeros)

    return call(
        functools.partial(down_kernel, path, tuple(len(stage) for stage in stages)),
        "down",
        2 * classes * rank * (sum(path) * rank + leaves * size * 2),
        rank * rank,
        8 * 2**20,
        vmem=24,
        out_shape=jax.ShapeDtypeStruct(own.shape, F32),
        grid_spec=pltpu.PrefetchScalarGridSpec(
            num_scalar_prefetch=1,
            grid=(1,),
            in_specs=[whole(array) for array in inputs],
            out_specs=whole(own),
            scratch_shapes=[pltpu.VMEM((2 * leaves, classes, rank), BF16)],
        ),
    )(numbers, *inputs)


def near_kernel(first, rows, depth, sources, live, points_ref, start_ref, *refs):
    out_ref, block_buf, weight_buf, total, order, cursor, sems = refs[-7:]
    block_ref = refs[0]
    weight_ref = refs[len(refs) - 8]
    leaf = pl.program_id(0)
    leaves = live.shape[0]
    classes, size = out_ref.shape
    weight_rows = weight_ref.shape[1] - 2 * classes
    half_size = size // 2
    inverse_leaf = 1.0 / math.sqrt(size)
    count = live[leaf]

    def copies(number):
        source = order[number]
        buffer = lax.rem(number, depth)
        return [
            pltpu.make_async_copy(
                block_ref.at[source, pl.ds(0, rows), :], block_buf.at[buffer], sems.at[buffer, 0]
            ),
            pltpu.make_async_copy(
                weight_ref.at[source, pl.ds(weight_rows, 2 * classes), :],
                weight_buf.at[buffer],
                sems.at[buffer, 1],
            ),
        ]

    @pl.when(leaf == 0)
    def _():
        def list_leaf(number, filled):
            def list_slot(slot, carry):
                order[filled + slot - 1] = lax.rem(sources[number, slot] // leaves, block_ref.shape[0])
                return carry

            lax.fori_loop(1, live[number], list_slot, 0)
            return filled + live[number] - 1

        cursor[0] = 0
        cursor[1] = lax.fori_loop(0, leaves, list_leaf, 0)
        for number in range(depth):

            @pl.when(number < cursor[1])
            def _():
                for copy in copies(number):
                    copy.start()

    target = points_ref[...]
    target_row = as_row(half_exponents(target))
    total[...] = jnp.zeros_like(total)
    base = cursor[0]
    last = cursor[1]

    def step(slot, carry):
        number = base + slot - 1
        buffer = lax.rem(number, depth)
        for copy in copies(number):
            copy.wait()
        block = block_buf[buffer]
        tile = kappa(block, target, half_exponents(block), target_row).astype(BF16)
        done = 0
        added = None
        for piece in range(2):
            low, high = max(first, piece * half_size), min(first + rows, (piece + 1) * half_size)
            if low < high:
                weights = weight_buf[
                    buffer,
                    pl.ds(piece * classes, classes),
                    pl.ds(low - piece * half_size, high - low),
                ]
                term = dot(weights, tile[done : done + high - low])
                added = term if added is None else added + term
                done += high - low
        total[...] += added

        @pl.when(number + depth < last)
        def _():
            for copy in copies(number + depth):
                copy.start()

        return carry

    lax.fori_loop(1, count, step, 0)
    cursor[0] = base + count - 1
    out_ref[...] = start_ref[...] + total[...] * inverse_leaf


def near_part(first, rows, depth, sources, live, points, start, blocks, weight_blocks):
    leaves = live.shape[0]
    size = points.shape[0] // leaves
    width = points.shape[1]
    classes = start.shape[0]
    operands = [blocks] if weight_blocks is blocks else [blocks, weight_blocks]
    tiles = 24
    return call(
        functools.partial(near_kernel, first, rows, depth),
        "near",
        tiles * 2 * rows * size * (width + classes),
        tiles * rows * size,
        tiles * rows * width * 2 + 4 * 2**20,
        out_shape=jax.ShapeDtypeStruct(start.shape, F32),
        grid_spec=pltpu.PrefetchScalarGridSpec(
            num_scalar_prefetch=2,
            grid=(leaves,),
            in_specs=[
                pl.BlockSpec((size, width), lambda i, s, n: (i, 0)),
                pl.BlockSpec((classes, size), lambda i, s, n: (0, i)),
            ]
            + [pl.BlockSpec(memory_space=pltpu.HBM) for _ in operands],
            out_specs=pl.BlockSpec((classes, size), lambda i, s, n: (0, i)),
            scratch_shapes=[
                pltpu.VMEM((depth, rows, width), BF16),
                pltpu.VMEM((depth, 2 * classes, width), BF16),
                pltpu.VMEM((classes, size), F32),
                pltpu.SMEM((sources.size,), jnp.int32),
                pltpu.SMEM((2,), jnp.int32),
                pltpu.SemaphoreType.DMA((depth, 2)),
            ],
        ),
    )(sources, live, points, start, *operands)


def swap(value, axis, mask):
    pairs = [(source, source ^ mask) for source in range(lax.axis_size(axis))]
    return lax.ppermute(value, axis, pairs)


def per_device(points, weights, near, counts, skel_leaf, skel_local, skel_upper):
    leaves, rank = skel_leaf.shape
    size = points.shape[0] // leaves
    classes = weights.shape[0]
    slots = near.shape[1]
    sub_count = lax.axis_size("sub")
    grp_count = lax.axis_size("grp")
    devices = sub_count * grp_count
    sub_index = lax.axis_index("sub")
    grp_index = lax.axis_index("grp")
    device = grp_index * sub_count + sub_index
    near_count = NEIGHBOURS
    far_count = sub_count // near_count

    group_first = grp_index * sub_count * leaves
    slot_ids = jnp.arange(slots)
    group_rows = lax.dynamic_slice_in_dim(near, group_first, sub_count * leaves, 0)
    group_counts = lax.dynamic_slice_in_dim(counts, group_first, sub_count * leaves, 0)
    owned = (
        (group_rows // leaves == device)
        & (slot_ids[None, :] < group_counts[:, None])
        & (slot_ids[None, :] > 0)
    )
    chosen = jnp.where(owned, group_rows - device * leaves, 0).reshape(sub_count, leaves * slots)
    chosen = jnp.max(chosen, axis=1)

    first_rows = size - LAST_ROWS
    sent = pack(chosen, points, weights, size, 0, first_rows, True)
    arrived = lax.all_to_all(sent, "sub", split_axis=0, concat_axis=0, tiled=True)

    near_bits = near_count.bit_length() - 1
    far_bits = far_count.bit_length() - 1
    table, starts, path_lengths = place_table(near_bits, far_bits, grp_count.bit_length() - 1)
    mine = lax.dynamic_slice_in_dim(jnp.asarray(table), device, 1, 0)[0]
    near_rows, far_rows, top_rows, path_nodes = (
        mine[low:high] for low, high in zip(starts[:-1], starts[1:])
    )

    own, skel, up, summary = leaf_level(points, weights, skel_leaf)
    lifted, terms, state = subtree(
        "local",
        leaves,
        leaves - 1,
        0,
        jnp.arange(leaves, dtype=jnp.int32),
        skel_local,
        (skel, summary),
        classes,
    )
    blocks = [[i * near_count + j for j in range(near_count)] for i in range(far_count)]
    gathered = lax.all_gather(state, "sub", axis_index_groups=blocks, tiled=False)
    near_lifted, near_terms, state = subtree(
        "near_nodes", near_count, near_count - 1, 1, near_rows, skel_upper, (gathered,), classes
    )
    far_states = [state] + [
        swap(state, "sub", mask * near_count) for mask in range(1, far_count)
    ]
    sent_last = pack(chosen, points, weights, size, first_rows, LAST_ROWS, False)
    sent_last, far_states = lax.optimization_barrier((sent_last, far_states))
    arrived_last = lax.all_to_all(sent_last, "sub", split_axis=0, concat_axis=0, tiled=True)

    far_lifted, far_terms, state = subtree(
        "far_nodes", far_count, far_count - 1, 2, far_rows, skel_upper, far_states, classes
    )
    top_states = [state] + [swap(state, "grp", mask) for mask in range(1, grp_count)]

    sources = lax.dynamic_slice_in_dim(near, device * leaves, leaves, 0)
    live = lax.dynamic_slice_in_dim(counts, device * leaves, leaves, 0)
    sources, live, state = lax.optimization_barrier((sources, live, state))
    total = near_part(0, first_rows, 4, sources, live, points, own, arrived, arrived)

    top_rows, total = lax.optimization_barrier((top_rows, total))
    top_lifted, top_terms, _ = subtree(
        "top_nodes", grp_count, grp_count - 2, 2, top_rows, skel_upper, top_states, classes
    )
    stages = [(top_lifted, top_terms), (far_lifted, far_terms), (near_lifted, near_terms)]
    total = down(
        path_nodes, path_lengths, stages, lifted, terms, up, total
    )
    return near_part(
        first_rows, LAST_ROWS, 8, sources, live, points, total, arrived_last, arrived
    )


def solution(mesh):
    split = P(("grp", "sub"), None)
    columns = P(None, ("grp", "sub"))
    return jax.shard_map(
        per_device,
        mesh=mesh,
        in_specs=(split, columns, P(), P(), split, split, P()),
        out_specs=columns,
        check_vma=False,
    )
```

```python
import functools
import math

import jax
import jax.numpy as jnp
import numpy as np
from jax import lax
from jax.experimental import pallas as pl
from jax.experimental.pallas import tpu as pltpu
from jax.sharding import PartitionSpec as P

F32 = jnp.float32
BF16 = jnp.bfloat16
LOG2E = 1.4426950408889634
NT = (((1,), (1,)), ((), ()))
LAST_ROWS = 128
NEIGHBOURS = 8
GROUP = 2


def call(kernel, name, flops, exps, nbytes, vmem=12, **kw):
    return pl.pallas_call(
        kernel,
        name=name,
        cost_estimate=pl.CostEstimate(flops=flops, bytes_accessed=nbytes, transcendentals=exps),
        compiler_params=pltpu.CompilerParams(vmem_limit_bytes=vmem * 2**20),
        **kw,
    )


def in_hbm(array):
    return pltpu.with_memory_space_constraint(array, pltpu.HBM)


def dot(a, b):
    return jnp.dot(a, b, preferred_element_type=F32)


def dot_nt(a, b):
    return lax.dot_general(a, b, NT, preferred_element_type=F32)


def half_exponents(block):
    sharpness = math.sqrt(block.shape[-1] / 8.0)
    wide = block.astype(F32)
    norms = jnp.sum(wide * wide, axis=-1, keepdims=True)
    return LOG2E * (sharpness * (1.0 - norms) - 0.25)


def as_row(column):
    rows = column.shape[0]
    return jnp.transpose(jnp.broadcast_to(column, (rows, 128)))[0:1, :]


def kappa_of(inner, width, left_half, right_half_row):
    scale = LOG2E * 2.0 * math.sqrt(width / 8.0)
    return jnp.exp2(inner * scale + left_half + right_half_row)


def kappa(left, right, left_half, right_half_row):
    return kappa_of(dot_nt(left, right), left.shape[-1], left_half, right_half_row)


def one_hot(chosen_row, pool):
    rank = chosen_row.shape[1]
    spread = jnp.transpose(jnp.broadcast_to(chosen_row, (128, rank)).astype(F32)).astype(jnp.int32)
    lanes = lax.broadcasted_iota(jnp.int32, (rank, 128), 1)
    pieces = [
        jnp.where(spread == lanes + 128 * j, 1.0, 0.0).astype(BF16) for j in range(pool // 128)
    ]
    return jnp.concatenate(pieces, axis=1)


def score_pieces(rows, classes, width):
    pieces = []
    for column in range(0, rows, width):
        row = rows + column * classes // width
        if rows - column >= width:
            pieces.append((column, width, 0, classes, row, 0))
        else:
            half = classes // 2
            pieces.append((column, width // 2, 0, half, row, 0))
            pieces.append((column, width // 2, half, half, row, width // 2))
    return pieces


def pack_kernel(leaf_size, first, rows, chosen, points_ref, weights_ref, out_ref, sems):
    classes = weights_ref.shape[0]
    pieces = score_pieces(rows, classes, points_ref.shape[1])

    def copies(j):
        start = pl.multiple_of(chosen[j] * leaf_size + first, 128)
        made = [
            pltpu.make_async_copy(
                points_ref.at[pl.ds(start, rows), :],
                out_ref.at[j, pl.ds(0, rows), :],
                sems.at[j, 0],
            )
        ]
        for number, (column, columns, from_class, count, row, lane) in enumerate(pieces):
            made.append(
                pltpu.make_async_copy(
                    weights_ref.at[
                        pl.ds(from_class, count),
                        pl.ds(pl.multiple_of(start + column, 128), columns),
                    ],
                    out_ref.at[j, pl.ds(row, count), pl.ds(lane, columns)],
                    sems.at[j, 1 + number],
                )
            )
        return made

    def start(j, carry):
        for copy in copies(j):
            copy.start()
        return carry

    def finish(j, carry):
        for copy in copies(j):
            copy.wait()
        return carry

    lax.fori_loop(0, out_ref.shape[0], start, 0)
    lax.fori_loop(0, out_ref.shape[0], finish, 0)


def pack(chosen, points, weights, leaf_size, first, rows):
    classes, width = weights.shape[0], points.shape[1]
    shape = (chosen.shape[0], rows + rows * classes // width, width)
    return call(
        functools.partial(pack_kernel, leaf_size, first, rows),
        "pack",
        0,
        0,
        2 * math.prod(shape) * 2,
        out_shape=pltpu.HBM(shape, BF16),
        grid_spec=pltpu.PrefetchScalarGridSpec(
            num_scalar_prefetch=1,
            grid=(1,),
            in_specs=[
                pl.BlockSpec(memory_space=pltpu.HBM),
                pl.BlockSpec(memory_space=pltpu.HBM),
            ],
            out_specs=pl.BlockSpec(memory_space=pltpu.HBM),
            scratch_shapes=[
                pltpu.SemaphoreType.DMA((shape[0], 1 + len(score_pieces(rows, classes, width))))
            ],
        ),
    )(chosen, in_hbm(points), in_hbm(weights))


def leaf_kernel(
    points_ref,
    weights_ref,
    chosen_ref,
    own_ref,
    skel_ref,
    up_ref,
    summary_ref,
    target_ref,
    half_ref,
):
    leaf = pl.program_id(0)
    block = points_ref[...]
    turned = jnp.transpose(block)
    target_ref[0] = turned
    leaf_size = block.shape[0]
    inverse_leaf = 1.0 / math.sqrt(leaf_size)
    half = half_exponents(block)
    half_row = as_row(half)
    half_ref[0] = half_row
    tile = kappa_of(dot(block, turned), block.shape[1], half, half_row)
    rows = lax.broadcasted_iota(jnp.int32, tile.shape, 0)
    columns = lax.broadcasted_iota(jnp.int32, tile.shape, 1)
    tile = jnp.where(rows == columns, 0.0, tile).astype(BF16)
    own = dot(weights_ref[...], tile) * inverse_leaf
    own_ref[...] = own
    chosen = chosen_ref[pl.ds(leaf, 1), :]
    rank = chosen.shape[1]
    skel_ref[0] = dot(one_hot(chosen, leaf_size), block).astype(BF16)
    places = lax.broadcasted_iota(jnp.int32, (leaf_size, rank), 0)
    columns_of = jnp.where(places == chosen, 1.0, 0.0).astype(BF16)
    up_ref[0] = dot(tile, columns_of).astype(BF16)
    summary_ref[0] = dot(own.astype(BF16), columns_of).astype(BF16)


def leaf_level(points, weights, skel_leaf):
    leaves, rank = skel_leaf.shape
    classes = weights.shape[0]
    width = points.shape[1]
    size = points.shape[0] // leaves
    return call(
        leaf_kernel,
        "leaf",
        leaves * 2 * size * (size * (width + classes + rank) + rank * width + classes * rank),
        leaves * size * size,
        8 * 2**20,
        out_shape=(
            pltpu.HBM(weights.shape, F32),
            jax.ShapeDtypeStruct((leaves, rank, width), BF16),
            pltpu.HBM((leaves, size, rank), BF16),
            jax.ShapeDtypeStruct((leaves, classes, rank), BF16),
            pltpu.HBM((leaves, width, size), BF16),
            pltpu.HBM((leaves, 1, size), F32),
        ),
        grid=(leaves,),
        in_specs=[
            pl.BlockSpec((size, width), lambda i: (i, 0)),
            pl.BlockSpec((classes, size), lambda i: (0, i)),
            pl.BlockSpec((leaves, rank), lambda i: (0, 0)),
        ],
        out_specs=(
            pl.BlockSpec((classes, size), lambda i: (0, i)),
            pl.BlockSpec((1, rank, width), lambda i: (i, 0, 0)),
            pl.BlockSpec((1, size, rank), lambda i: (i, 0, 0)),
            pl.BlockSpec((1, classes, rank), lambda i: (i, 0, 0)),
            pl.BlockSpec((1, width, size), lambda i: (i, 0, 0)),
            pl.BlockSpec((1, 1, size), lambda i: (i, 0, 0)),
        ),
    )(points, weights, skel_leaf)


def subtree_kernel(count, inner, states, rows, *refs):
    chosen_ref = refs[0]
    inputs = refs[1 : len(refs) - 5]
    lifted_ref, terms_ref, state_ref, nodes, sums = refs[len(refs) - 5 :]
    _, rank, width = nodes.shape
    classes = sums.shape[1]
    inverse_rank = 1.0 / rank
    inverse_pair = 1.0 / (math.sqrt(2.0) * rank)
    if states == 0:
        nodes[pl.ds(0, count)] = inputs[0][...]
        sums[pl.ds(0, count)] = inputs[1][...]
    elif states == 1:
        nodes[pl.ds(0, count)] = inputs[0][:, pl.ds(0, rank), :]
        sums[pl.ds(0, count)] = inputs[0][:, pl.ds(rank, classes), :]
    else:
        for mask in range(count):
            place = lax.bitwise_xor(rows[inner], mask)
            nodes[place] = inputs[mask][pl.ds(0, rank), :]
            sums[place] = inputs[mask][pl.ds(rank, classes), :]

    def pair(i, even, odd, even_half, odd_half):
        tile = kappa(even, odd, even_half, as_row(odd_half)).astype(BF16)
        terms_ref[2 * i] = dot_nt(sums[2 * i + 1], tile) * inverse_rank
        terms_ref[2 * i + 1] = dot(sums[2 * i], tile) * inverse_rank

    def step(i, carry):
        even, odd = nodes[2 * i], nodes[2 * i + 1]
        child = jnp.concatenate([even, odd], axis=0)
        chosen = chosen_ref[pl.ds(rows[i], 1), :]
        half = half_exponents(child)
        parent = dot(one_hot(chosen, 2 * rank), child).astype(BF16)
        lifted = kappa(child, parent, half, as_row(half_exponents(parent)))
        same = lax.broadcasted_iota(jnp.int32, lifted.shape, 0) == chosen
        lifted = jnp.where(same, 0.0, lifted).astype(BF16)
        lifted_ref[i] = lifted
        summed = dot(sums[2 * i], lifted[:rank]) + dot(sums[2 * i + 1], lifted[rank:])
        nodes[count + i] = parent
        sums[count + i] = (summed * inverse_pair).astype(BF16)
        pair(i, even, odd, half[:rank], half[rank:])
        return carry

    lax.fori_loop(0, inner, step, 0)
    if inner == count - 1:
        state_ref[pl.ds(0, rank), :] = nodes[count + inner - 1]
        state_ref[pl.ds(rank, classes), :] = sums[count + inner - 1]
    else:
        even, odd = nodes[2 * inner], nodes[2 * inner + 1]
        pair(inner, even, odd, half_exponents(even), half_exponents(odd))
        state_ref[...] = jnp.zeros_like(state_ref)


def subtree(name, count, inner, states, rows, table, inputs, classes):
    rank = table.shape[1]
    width = inputs[0].shape[-1]

    def whole(array):
        zeros = (0,) * len(array.shape)
        return pl.BlockSpec(array.shape, lambda i, r: zeros)

    shapes = (
        pltpu.HBM((inner, 2 * rank, rank), BF16),
        pltpu.HBM((2 * count - 2, classes, rank), F32),
        jax.ShapeDtypeStruct((rank + classes, width), BF16),
    )
    return call(
        functools.partial(subtree_kernel, count, inner, states),
        name,
        inner * 2 * rank * rank * (5 * width + 4 * classes),
        inner * 3 * rank * rank,
        6 * 2**20,
        vmem=16,
        out_shape=shapes,
        grid_spec=pltpu.PrefetchScalarGridSpec(
            num_scalar_prefetch=1,
            grid=(1,),
            in_specs=[whole(table)] + [whole(array) for array in inputs],
            out_specs=tuple(whole(shape) for shape in shapes),
            scratch_shapes=[
                pltpu.VMEM((2 * count, rank, width), BF16),
                pltpu.VMEM((2 * count, classes, rank), BF16),
            ],
        ),
    )(in_hbm(rows), in_hbm(table), *inputs)


def path_of(place, count):
    numbers = [place]
    while 2 ** len(numbers) < count:
        numbers.append(count + (numbers[-1] >> 1))
    return numbers


def place_table(near_bits, far_bits, grp_bits):
    devices = 1 << near_bits + far_bits + grp_bits

    def upper_rows(device, height, step, wanted):
        rows = []
        for u in range(height + 1, height + step + 1):
            under = 1 << (height + step - u)
            base = devices - (devices >> u - 1) + (device >> height + step) * under
            rows += [base + i for i in range(under)]
        return rows[:wanted]

    table = []
    for device in range(devices):
        near_place = device & (1 << near_bits) - 1
        far_place = device >> near_bits & (1 << far_bits) - 1
        grp_place = device >> near_bits + far_bits
        paths = [
            path_of(grp_place, 1 << grp_bits)[::-1],
            path_of(far_place, 1 << far_bits)[::-1],
            path_of(near_place, 1 << near_bits)[::-1],
        ]
        parts = [
            upper_rows(device, 0, near_bits, (1 << near_bits) - 1),
            upper_rows(device, near_bits, far_bits, (1 << far_bits) - 1) + [far_place],
            upper_rows(device, near_bits + far_bits, grp_bits, (1 << grp_bits) - 2) + [grp_place],
            [node for path in paths for node in path],
        ]
        table.append([number for part in parts for number in part])
    starts = np.cumsum([0] + [len(part) for part in parts]).tolist()
    return np.array(table, np.int32), starts, tuple(len(path) for path in paths)


def down_kernel(path, counts, numbers, *refs):
    stages = len(counts)
    lifted_ref, terms_ref, up_ref, own_ref, out_ref, values = refs[2 * stages :]
    inner, _, rank = lifted_ref.shape
    leaves, size, _ = up_ref.shape
    inverse_rank = 1.0 / rank
    value = None
    at = 0
    for stage, steps in enumerate(path):
        stage_lifted, stage_terms = refs[2 * stage], refs[2 * stage + 1]
        for _ in range(steps):
            node = numbers[at]
            at += 1
            term = stage_terms[node]
            if value is not None:
                half = pl.ds(pl.multiple_of((node & 1) * rank, rank), rank)
                child = stage_lifted[node >> 1, half, :]
                term = term + dot_nt(value, child) * inverse_rank
            value = term.astype(BF16)
    values[2 * leaves - 2] = value

    def lower(step, carry):
        i = inner - 1 - step
        down = dot_nt(values[leaves + i], lifted_ref[i]) * inverse_rank
        values[2 * i] = (terms_ref[2 * i] + down[:, :rank]).astype(BF16)
        values[2 * i + 1] = (terms_ref[2 * i + 1] + down[:, rank:]).astype(BF16)
        return carry

    lax.fori_loop(0, inner, lower, 0)
    for leaf in range(leaves):
        columns = pl.ds(leaf * size, size)
        spread = dot_nt(values[leaf], up_ref[leaf]) * inverse_rank
        out_ref[:, columns] = own_ref[:, columns] + spread


def down(numbers, path, stages, lifted, terms, up, own):
    leaves, size, rank = up.shape
    classes = own.shape[0]
    inputs = [array for stage in stages for array in stage] + [lifted, terms, up, own]

    def whole(array):
        zeros = (0,) * array.ndim
        return pl.BlockSpec(array.shape, lambda i, n: zeros)

    return call(
        functools.partial(down_kernel, path, tuple(len(stage) for stage in stages)),
        "down",
        2 * classes * rank * (sum(path) * rank + leaves * size * 2),
        rank * rank,
        8 * 2**20,
        vmem=24,
        out_shape=pltpu.HBM(own.shape, F32),
        grid_spec=pltpu.PrefetchScalarGridSpec(
            num_scalar_prefetch=1,
            grid=(1,),
            in_specs=[whole(array) for array in inputs],
            out_specs=whole(own),
            scratch_shapes=[pltpu.VMEM((2 * leaves, classes, rank), BF16)],
        ),
    )(in_hbm(numbers), *(in_hbm(array) for array in inputs))


def near_kernel(rows, group, slots, targets_ref, halves_ref, start_ref, block_ref, *refs):
    out_ref, order = refs
    leaves, width, size = targets_ref.shape
    classes = out_ref.shape[0]
    inverse_leaf = 1.0 / math.sqrt(size)

    def list_leaf(number, filled):
        def list_slot(slot, carry):
            order[filled + slot - 1, 0] = number
            order[filled + slot - 1, 1] = lax.rem(slots[number, slot] // leaves, block_ref.shape[0])
            return carry

        live = slots[number, slots.shape[1] - 1]
        lax.fori_loop(1, live, list_slot, 0)
        return filled + live - 1

    def repeat_last(number, carry):
        order[number, 0] = order[count - 1, 0]
        order[number, 1] = order[count - 1, 1]
        return carry

    count = lax.fori_loop(0, leaves, list_leaf, 0)
    steps = (count + group - 1) // group
    lax.fori_loop(count, steps * group, repeat_last, 0)
    out_ref[...] = start_ref[...]

    def contribution(number):
        leaf, source = order[number, 0], order[number, 1]
        block = block_ref[source, pl.ds(0, rows), :]
        inner = dot(block, targets_ref[leaf])
        tile = kappa_of(inner, width, half_exponents(block), halves_ref[leaf]).astype(BF16)
        added = None
        for column in range(0, rows, width):
            columns = min(width, rows - column)
            place = pl.ds(rows + column * classes // width, classes * columns // width)
            weights = block_ref[source, place, :]
            if columns < width:
                weights = jnp.concatenate(
                    [weights[:, : width // 2], weights[:, width // 2 :]], axis=0
                )
            term = dot(weights, tile[column : column + columns])
            added = term if added is None else added + term
        return added * jnp.where(number < count, inverse_leaf, 0.0)

    def step(first, carry):
        numbers = [first * group + k for k in range(group)]
        added = [contribution(number) for number in numbers]
        for number, term in zip(numbers, added):
            columns = pl.ds(pl.multiple_of(order[number, 0] * size, size), size)
            out_ref[:, columns] += term
        return carry

    lax.fori_loop(0, steps, step, 0)


def near_part(rows, group, slots, targets, halves, start, blocks, out_type):
    classes, columns = start.shape
    size, width = targets.shape[2], targets.shape[1]
    tiles = 24
    scalars = pl.BlockSpec(memory_space=pltpu.SMEM)
    whole = pl.BlockSpec(memory_space=pltpu.VMEM)
    return call(
        functools.partial(near_kernel, rows, group),
        "near",
        tiles * 2 * rows * size * (width + classes),
        tiles * rows * size,
        tiles * rows * width * 2 + 4 * 2**20,
        vmem=24,
        out_shape=out_type(start.shape, F32),
        in_specs=[scalars, whole, whole, whole, whole],
        out_specs=whole,
        scratch_shapes=[pltpu.SMEM((slots.size + group, 2), jnp.int32)],
    )(in_hbm(slots), in_hbm(targets), in_hbm(halves), in_hbm(start), blocks)


def swap(value, axis, mask):
    pairs = [(source, source ^ mask) for source in range(lax.axis_size(axis))]
    return lax.ppermute(value, axis, pairs)


def per_device(points, weights, near, counts, skel_leaf, skel_local, skel_upper):
    leaves, rank = skel_leaf.shape
    size = points.shape[0] // leaves
    classes = weights.shape[0]
    slots = near.shape[1]
    sub_count = lax.axis_size("sub")
    grp_count = lax.axis_size("grp")
    devices = sub_count * grp_count
    sub_index = lax.axis_index("sub")
    grp_index = lax.axis_index("grp")
    device = grp_index * sub_count + sub_index
    near_count = NEIGHBOURS
    far_count = sub_count // near_count

    group_first = grp_index * sub_count * leaves
    slot_ids = jnp.arange(slots)
    group_rows = lax.dynamic_slice_in_dim(near, group_first, sub_count * leaves, 0)
    group_counts = lax.dynamic_slice_in_dim(counts, group_first, sub_count * leaves, 0)
    owned = (
        (group_rows // leaves == device)
        & (slot_ids[None, :] < group_counts[:, None])
        & (slot_ids[None, :] > 0)
    )
    chosen = jnp.where(owned, group_rows - device * leaves, 0).reshape(sub_count, leaves * slots)
    chosen = jnp.max(chosen, axis=1)

    first_rows = size - LAST_ROWS
    sent = pack(chosen, points, weights, size, 0, first_rows)
    arrived = lax.all_to_all(sent, "sub", split_axis=0, concat_axis=0, tiled=True)

    near_bits = near_count.bit_length() - 1
    far_bits = far_count.bit_length() - 1
    table, starts, path_lengths = place_table(near_bits, far_bits, grp_count.bit_length() - 1)
    mine = lax.dynamic_slice_in_dim(jnp.asarray(table), device, 1, 0)[0]
    near_slots = jnp.concatenate(
        [
            lax.dynamic_slice_in_dim(near, device * leaves, leaves, 0),
            lax.dynamic_slice_in_dim(counts, device * leaves, leaves, 0)[:, None],
        ],
        axis=1,
    )
    near_rows, far_rows, top_rows, path_nodes = (
        mine[low:high] for low, high in zip(starts[:-1], starts[1:])
    )

    own, skel, up, summary, targets, halves = leaf_level(points, weights, skel_leaf)
    lifted, terms, state = subtree(
        "local",
        leaves,
        leaves - 1,
        0,
        jnp.arange(leaves, dtype=jnp.int32),
        skel_local,
        (skel, summary),
        classes,
    )
    blocks = [[i * near_count + j for j in range(near_count)] for i in range(far_count)]
    state, near_slots, far_rows, top_rows, path_nodes = lax.optimization_barrier(
        (state, near_slots, far_rows, top_rows, path_nodes)
    )
    gathered = lax.all_gather(state, "sub", axis_index_groups=blocks, tiled=False)
    near_lifted, near_terms, state = subtree(
        "near_nodes", near_count, near_count - 1, 1, near_rows, skel_upper, (gathered,), classes
    )
    far_states = [state] + [
        swap(state, "sub", mask * near_count) for mask in range(1, far_count)
    ]
    sent_last = pack(chosen, points, weights, size, first_rows, LAST_ROWS)
    sent_last, far_states = lax.optimization_barrier((sent_last, far_states))
    arrived_last = lax.all_to_all(sent_last, "sub", split_axis=0, concat_axis=0, tiled=True)

    far_lifted, far_terms, state = subtree(
        "far_nodes", far_count, far_count - 1, 2, far_rows, skel_upper, far_states, classes
    )
    top_states = [state] + [swap(state, "grp", mask) for mask in range(1, grp_count)]

    near_slots, state = lax.optimization_barrier((near_slots, state))
    total = near_part(first_rows, GROUP, near_slots, targets, halves, own, arrived, pltpu.HBM)

    top_rows, total = lax.optimization_barrier((top_rows, total))
    top_lifted, top_terms, _ = subtree(
        "top_nodes", grp_count, grp_count - 2, 2, top_rows, skel_upper, top_states, classes
    )
    stages = [(top_lifted, top_terms), (far_lifted, far_terms), (near_lifted, near_terms)]
    total = down(
        path_nodes, path_lengths, stages, lifted, terms, up, total
    )
    return near_part(
        LAST_ROWS, GROUP, near_slots, targets, halves, total, arrived_last, jax.ShapeDtypeStruct
    )


def solution(mesh):
    split = P(("grp", "sub"), None)
    columns = P(None, ("grp", "sub"))
    return jax.shard_map(
        per_device,
        mesh=mesh,
        in_specs=(split, columns, P(), P(), split, split, P()),
        out_specs=columns,
        check_vma=False,
    )
```

```python
import functools
import math

import jax
import jax.numpy as jnp
import numpy as np
from jax import lax
from jax.experimental import pallas as pl
from jax.experimental.pallas import tpu as pltpu
from jax.sharding import PartitionSpec as P

F32 = jnp.float32
BF16 = jnp.bfloat16
LOG2E = 1.4426950408889634
NT = (((1,), (1,)), ((), ()))
LAST_ROWS = 128
NEIGHBOURS = 8
GROUP = 2


def call(kernel, name, flops, exps, nbytes, vmem=12, **kw):
    return pl.pallas_call(
        kernel,
        name=name,
        cost_estimate=pl.CostEstimate(flops=flops, bytes_accessed=nbytes, transcendentals=exps),
        compiler_params=pltpu.CompilerParams(vmem_limit_bytes=vmem * 2**20),
        **kw,
    )


def in_hbm(array):
    return pltpu.with_memory_space_constraint(array, pltpu.HBM)


def dot(a, b):
    return jnp.dot(a, b, preferred_element_type=F32)


def dot_nt(a, b):
    return lax.dot_general(a, b, NT, preferred_element_type=F32)


def half_exponents(block):
    sharpness = math.sqrt(block.shape[-1] / 8.0)
    wide = block.astype(F32)
    norms = jnp.sum(wide * wide, axis=-1, keepdims=True)
    return LOG2E * (sharpness * (1.0 - norms) - 0.25)


def as_row(column):
    rows = column.shape[0]
    return jnp.transpose(jnp.broadcast_to(column, (rows, 128)))[0:1, :]


def kappa_of(inner, width, left_half, right_half_row):
    scale = LOG2E * 2.0 * math.sqrt(width / 8.0)
    return jnp.exp2(inner * scale + left_half + right_half_row)


def kappa(left, right, left_half, right_half_row):
    return kappa_of(dot_nt(left, right), left.shape[-1], left_half, right_half_row)


def one_hot(chosen_row, pool):
    rank = chosen_row.shape[1]
    spread = jnp.transpose(jnp.broadcast_to(chosen_row, (128, rank)).astype(F32)).astype(jnp.int32)
    lanes = lax.broadcasted_iota(jnp.int32, (rank, 128), 1)
    pieces = [
        jnp.where(spread == lanes + 128 * j, 1.0, 0.0).astype(BF16) for j in range(pool // 128)
    ]
    return jnp.concatenate(pieces, axis=1)


def score_pieces(rows, classes, width):
    pieces = []
    for column in range(0, rows, width):
        row = rows + column * classes // width
        if rows - column >= width:
            pieces.append((column, width, 0, classes, row, 0))
        else:
            half = classes // 2
            pieces.append((column, width // 2, 0, half, row, 0))
            pieces.append((column, width // 2, half, half, row, width // 2))
    return pieces


def pack_kernel(leaf_size, first, rows, chosen, points_ref, weights_ref, out_ref, sems):
    classes = weights_ref.shape[0]
    pieces = score_pieces(rows, classes, points_ref.shape[1])

    def copies(j):
        start = pl.multiple_of(chosen[j] * leaf_size + first, 128)
        made = [
            pltpu.make_async_copy(
                points_ref.at[pl.ds(start, rows), :],
                out_ref.at[j, pl.ds(0, rows), :],
                sems.at[j, 0],
            )
        ]
        for number, (column, columns, from_class, count, row, lane) in enumerate(pieces):
            made.append(
                pltpu.make_async_copy(
                    weights_ref.at[
                        pl.ds(from_class, count),
                        pl.ds(pl.multiple_of(start + column, 128), columns),
                    ],
                    out_ref.at[j, pl.ds(row, count), pl.ds(lane, columns)],
                    sems.at[j, 1 + number],
                )
            )
        return made

    def start(j, carry):
        @pl.when(chosen[j] >= 0)
        def _():
            for copy in copies(j):
                copy.start()

        return carry

    def finish(j, carry):
        @pl.when(chosen[j] >= 0)
        def _():
            for copy in copies(j):
                copy.wait()

        return carry

    lax.fori_loop(0, out_ref.shape[0], start, 0)
    lax.fori_loop(0, out_ref.shape[0], finish, 0)


def pack(chosen, points, weights, leaf_size, first, rows):
    classes, width = weights.shape[0], points.shape[1]
    shape = (chosen.shape[0], rows + rows * classes // width, width)
    return call(
        functools.partial(pack_kernel, leaf_size, first, rows),
        "pack",
        0,
        0,
        2 * math.prod(shape) * 2,
        out_shape=pltpu.HBM(shape, BF16),
        grid_spec=pltpu.PrefetchScalarGridSpec(
            num_scalar_prefetch=1,
            grid=(1,),
            in_specs=[
                pl.BlockSpec(points.shape, lambda i, c: (0, 0)),
                pl.BlockSpec(weights.shape, lambda i, c: (0, 0)),
            ],
            out_specs=pl.BlockSpec(memory_space=pltpu.HBM),
            scratch_shapes=[
                pltpu.SemaphoreType.DMA((shape[0], 1 + len(score_pieces(rows, classes, width))))
            ],
        ),
    )(chosen, in_hbm(points), in_hbm(weights))


def leaf_kernel(
    points_ref,
    weights_ref,
    chosen_ref,
    own_ref,
    skel_ref,
    up_ref,
    summary_ref,
    target_ref,
    half_ref,
):
    leaf = pl.program_id(0)
    block = points_ref[...]
    turned = jnp.transpose(block)
    target_ref[0] = turned
    leaf_size = block.shape[0]
    inverse_leaf = 1.0 / math.sqrt(leaf_size)
    half = half_exponents(block)
    half_row = as_row(half)
    half_ref[0] = half_row
    tile = kappa_of(dot(block, turned), block.shape[1], half, half_row)
    rows = lax.broadcasted_iota(jnp.int32, tile.shape, 0)
    columns = lax.broadcasted_iota(jnp.int32, tile.shape, 1)
    tile = jnp.where(rows == columns, 0.0, tile).astype(BF16)
    own = dot(weights_ref[...], tile) * inverse_leaf
    own_ref[...] = own
    chosen = chosen_ref[pl.ds(leaf, 1), :]
    rank = chosen.shape[1]
    skel_ref[0] = dot(one_hot(chosen, leaf_size), block).astype(BF16)
    places = lax.broadcasted_iota(jnp.int32, (leaf_size, rank), 0)
    columns_of = jnp.where(places == chosen, 1.0, 0.0).astype(BF16)
    up_ref[0] = dot(tile, columns_of).astype(BF16)
    summary_ref[0] = dot(own.astype(BF16), columns_of).astype(BF16)


def leaf_level(points, weights, skel_leaf):
    leaves, rank = skel_leaf.shape
    classes = weights.shape[0]
    width = points.shape[1]
    size = points.shape[0] // leaves
    return call(
        leaf_kernel,
        "leaf",
        leaves * 2 * size * (size * (width + classes + rank) + rank * width + classes * rank),
        leaves * size * size,
        8 * 2**20,
        out_shape=(
            pltpu.HBM(weights.shape, F32),
            jax.ShapeDtypeStruct((leaves, rank, width), BF16),
            pltpu.HBM((leaves, size, rank), BF16),
            jax.ShapeDtypeStruct((leaves, classes, rank), BF16),
            pltpu.HBM((leaves, width, size), BF16),
            pltpu.HBM((leaves, 1, size), F32),
        ),
        grid=(leaves,),
        in_specs=[
            pl.BlockSpec((size, width), lambda i: (i, 0)),
            pl.BlockSpec((classes, size), lambda i: (0, i)),
            pl.BlockSpec((leaves, rank), lambda i: (0, 0)),
        ],
        out_specs=(
            pl.BlockSpec((classes, size), lambda i: (0, i)),
            pl.BlockSpec((1, rank, width), lambda i: (i, 0, 0)),
            pl.BlockSpec((1, size, rank), lambda i: (i, 0, 0)),
            pl.BlockSpec((1, classes, rank), lambda i: (i, 0, 0)),
            pl.BlockSpec((1, width, size), lambda i: (i, 0, 0)),
            pl.BlockSpec((1, 1, size), lambda i: (i, 0, 0)),
        ),
    )(points, weights, skel_leaf)


def subtree_kernel(count, inner, states, rows, *refs):
    chosen_ref = refs[0]
    inputs = refs[1 : len(refs) - 5]
    lifted_ref, terms_ref, state_ref, nodes, sums = refs[len(refs) - 5 :]
    _, rank, width = nodes.shape
    classes = sums.shape[1]
    inverse_rank = 1.0 / rank
    inverse_pair = 1.0 / (math.sqrt(2.0) * rank)
    if states == 0:
        nodes[pl.ds(0, count)] = inputs[0][...]
        sums[pl.ds(0, count)] = inputs[1][...]
    elif states == 1:
        nodes[pl.ds(0, count)] = inputs[0][:, pl.ds(0, rank), :]
        sums[pl.ds(0, count)] = inputs[0][:, pl.ds(rank, classes), :]
    else:
        for mask in range(count):
            place = lax.bitwise_xor(rows[inner], mask)
            nodes[place] = inputs[mask][pl.ds(0, rank), :]
            sums[place] = inputs[mask][pl.ds(rank, classes), :]

    def pair(i, even, odd, even_half, odd_half):
        tile = kappa(even, odd, even_half, as_row(odd_half)).astype(BF16)
        terms_ref[2 * i] = dot_nt(sums[2 * i + 1], tile) * inverse_rank
        terms_ref[2 * i + 1] = dot(sums[2 * i], tile) * inverse_rank

    def step(i, carry):
        even, odd = nodes[2 * i], nodes[2 * i + 1]
        child = jnp.concatenate([even, odd], axis=0)
        chosen = chosen_ref[pl.ds(rows[i], 1), :]
        half = half_exponents(child)
        parent = dot(one_hot(chosen, 2 * rank), child).astype(BF16)
        lifted = kappa(child, parent, half, as_row(half_exponents(parent)))
        same = lax.broadcasted_iota(jnp.int32, lifted.shape, 0) == chosen
        lifted = jnp.where(same, 0.0, lifted).astype(BF16)
        lifted_ref[i] = lifted
        summed = dot(sums[2 * i], lifted[:rank]) + dot(sums[2 * i + 1], lifted[rank:])
        nodes[count + i] = parent
        sums[count + i] = (summed * inverse_pair).astype(BF16)
        pair(i, even, odd, half[:rank], half[rank:])
        return carry

    lax.fori_loop(0, inner, step, 0)
    if inner == count - 1:
        state_ref[pl.ds(0, rank), :] = nodes[count + inner - 1]
        state_ref[pl.ds(rank, classes), :] = sums[count + inner - 1]
    else:
        even, odd = nodes[2 * inner], nodes[2 * inner + 1]
        pair(inner, even, odd, half_exponents(even), half_exponents(odd))
        state_ref[...] = jnp.zeros_like(state_ref)


def subtree(name, count, inner, states, rows, table, inputs, classes):
    rank = table.shape[1]
    width = inputs[0].shape[-1]

    def whole(array):
        zeros = (0,) * len(array.shape)
        return pl.BlockSpec(array.shape, lambda i, r: zeros)

    shapes = (
        pltpu.HBM((inner, 2 * rank, rank), BF16),
        pltpu.HBM((2 * count - 2, classes, rank), F32),
        jax.ShapeDtypeStruct((rank + classes, width), BF16),
    )
    return call(
        functools.partial(subtree_kernel, count, inner, states),
        name,
        inner * 2 * rank * rank * (5 * width + 4 * classes),
        inner * 3 * rank * rank,
        6 * 2**20,
        vmem=16,
        out_shape=shapes,
        grid_spec=pltpu.PrefetchScalarGridSpec(
            num_scalar_prefetch=1,
            grid=(1,),
            in_specs=[whole(table)] + [whole(array) for array in inputs],
            out_specs=tuple(whole(shape) for shape in shapes),
            scratch_shapes=[
                pltpu.VMEM((2 * count, rank, width), BF16),
                pltpu.VMEM((2 * count, classes, rank), BF16),
            ],
        ),
    )(in_hbm(rows), in_hbm(table), *inputs)


def path_of(place, count):
    numbers = [place]
    while 2 ** len(numbers) < count:
        numbers.append(count + (numbers[-1] >> 1))
    return numbers


def place_table(near_bits, far_bits, grp_bits):
    devices = 1 << near_bits + far_bits + grp_bits

    def upper_rows(device, height, step, wanted):
        rows = []
        for u in range(height + 1, height + step + 1):
            under = 1 << (height + step - u)
            base = devices - (devices >> u - 1) + (device >> height + step) * under
            rows += [base + i for i in range(under)]
        return rows[:wanted]

    table = []
    for device in range(devices):
        near_place = device & (1 << near_bits) - 1
        far_place = device >> near_bits & (1 << far_bits) - 1
        grp_place = device >> near_bits + far_bits
        paths = [
            path_of(grp_place, 1 << grp_bits)[::-1],
            path_of(far_place, 1 << far_bits)[::-1],
            path_of(near_place, 1 << near_bits)[::-1],
        ]
        parts = [
            upper_rows(device, 0, near_bits, (1 << near_bits) - 1),
            upper_rows(device, near_bits, far_bits, (1 << far_bits) - 1) + [far_place],
            upper_rows(device, near_bits + far_bits, grp_bits, (1 << grp_bits) - 2) + [grp_place],
            [node for path in paths for node in path],
        ]
        table.append([number for part in parts for number in part])
    starts = np.cumsum([0] + [len(part) for part in parts]).tolist()
    return np.array(table, np.int32), starts, tuple(len(path) for path in paths)


def down_kernel(path, stages, numbers, *refs):
    lifted_hbm, terms_hbm, up_hbm, own_hbm, out_ref = refs[2 * stages : 2 * stages + 5]
    lifted_ref, terms_ref, up_ref, path_lifted, path_terms, values = refs[2 * stages + 5 : -3]
    path_sems, up_sems, sems = refs[-3:]
    inner, _, rank = lifted_ref.shape
    leaves, size, _ = up_ref.shape
    inverse_rank = 1.0 / rank

    path_copies = []
    for stage, steps in enumerate(path):
        for _ in range(steps):
            at = len(path_copies)
            node = numbers[at]
            copies = [
                pltpu.make_async_copy(
                    refs[2 * stage + 1].at[node], path_terms.at[at], path_sems.at[at, 0]
                )
            ]
            if at > 0:
                half = pl.ds(pl.multiple_of((node & 1) * rank, rank), rank)
                copies.append(
                    pltpu.make_async_copy(
                        refs[2 * stage].at[node >> 1, half, :],
                        path_lifted.at[at],
                        path_sems.at[at, 1],
                    )
                )
            path_copies.append(copies)
    local_copies = [
        pltpu.make_async_copy(terms_hbm, terms_ref, sems.at[0]),
        pltpu.make_async_copy(lifted_hbm, lifted_ref, sems.at[1]),
    ]
    own_copy = pltpu.make_async_copy(own_hbm, out_ref, sems.at[2])
    up_copies = [
        pltpu.make_async_copy(up_hbm.at[leaf], up_ref.at[leaf], up_sems.at[leaf])
        for leaf in range(leaves)
    ]
    for copies in path_copies:
        for copy in copies:
            copy.start()
    for copy in local_copies + [own_copy] + up_copies:
        copy.start()

    value = None
    for at, copies in enumerate(path_copies):
        for copy in copies:
            copy.wait()
        term = path_terms[at]
        if at > 0:
            term = term + dot_nt(value, path_lifted[at]) * inverse_rank
        value = term.astype(BF16)
    values[2 * leaves - 2] = value
    for copy in local_copies:
        copy.wait()

    def lower(step, carry):
        i = inner - 1 - step
        down = dot_nt(values[leaves + i], lifted_ref[i]) * inverse_rank
        values[2 * i] = (terms_ref[2 * i] + down[:, :rank]).astype(BF16)
        values[2 * i + 1] = (terms_ref[2 * i + 1] + down[:, rank:]).astype(BF16)
        return carry

    lax.fori_loop(0, inner, lower, 0)
    own_copy.wait()
    for leaf in range(leaves):
        up_copies[leaf].wait()
        columns = pl.ds(leaf * size, size)
        out_ref[:, columns] += dot_nt(values[leaf], up_ref[leaf]) * inverse_rank


def down(numbers, path, stages, lifted, terms, up, own):
    leaves, size, rank = up.shape
    classes = own.shape[0]
    inputs = [array for stage in stages for array in stage] + [lifted, terms, up, own]
    hbm = pl.BlockSpec(memory_space=pltpu.HBM)
    return call(
        functools.partial(down_kernel, path, len(stages)),
        "down",
        2 * classes * rank * (sum(path) * rank + leaves * size * 2),
        rank * rank,
        8 * 2**20,
        vmem=24,
        out_shape=pltpu.HBM(own.shape, F32),
        in_specs=[pl.BlockSpec(memory_space=pltpu.SMEM)] + [hbm] * len(inputs),
        out_specs=pl.BlockSpec(memory_space=pltpu.VMEM),
        scratch_shapes=[
            pltpu.VMEM(lifted.shape, BF16),
            pltpu.VMEM(terms.shape, F32),
            pltpu.VMEM(up.shape, BF16),
            pltpu.VMEM((sum(path), rank, rank), BF16),
            pltpu.VMEM((sum(path), classes, rank), F32),
            pltpu.VMEM((2 * leaves, classes, rank), BF16),
            pltpu.SemaphoreType.DMA((sum(path), 2)),
            pltpu.SemaphoreType.DMA((leaves,)),
            pltpu.SemaphoreType.DMA((3,)),
        ],
    )(in_hbm(numbers), *(in_hbm(array) for array in inputs))


def near_kernel(
    rows, group, resident, slots, halves_ref, targets_hbm, start_hbm, block_hbm, out_ref, *refs
):
    order, leaf_state, block_state, targets_ref, start_ref = refs[:5]
    leaf_sems, block_sems, start_sem = refs[-3:]
    block_ref = block_hbm if resident else refs[5]
    leaves, width, size = targets_ref.shape
    sources = block_hbm.shape[0]
    classes = out_ref.shape[0]
    inverse_leaf = 1.0 / math.sqrt(size)

    def target_copy(leaf):
        return pltpu.make_async_copy(
            targets_hbm.at[leaf], targets_ref.at[leaf], leaf_sems.at[leaf]
        )

    def block_copy(source):
        return pltpu.make_async_copy(
            block_hbm.at[source], block_ref.at[source], block_sems.at[source]
        )

    def clear(source, carry):
        block_state[source] = 0
        return carry

    def list_leaf(number, filled):
        target_copy(number).start()
        leaf_state[number] = 1

        def list_slot(slot, carry):
            source = lax.rem(slots[number, slot] // leaves, sources)
            order[filled + slot - 1, 0] = number
            order[filled + slot - 1, 1] = source
            if not resident:

                @pl.when(block_state[source] == 0)
                def _():
                    block_state[source] = 1
                    block_copy(source).start()

            return carry

        live = slots[number, slots.shape[1] - 1]
        lax.fori_loop(1, live, list_slot, 0)
        return filled + live - 1

    def repeat_last(number, carry):
        order[number, 0] = order[count - 1, 0]
        order[number, 1] = order[count - 1, 1]
        return carry

    if not resident:
        lax.fori_loop(0, sources, clear, 0)
    count = lax.fori_loop(0, leaves, list_leaf, 0)
    start_copy = pltpu.make_async_copy(start_hbm, start_ref, start_sem)
    start_copy.start()
    steps = (count + group - 1) // group
    lax.fori_loop(count, steps * group, repeat_last, 0)
    out_ref[...] = jnp.zeros_like(out_ref)

    def arrive(number):
        leaf, source = order[number, 0], order[number, 1]

        @pl.when(leaf_state[leaf] == 1)
        def _():
            leaf_state[leaf] = 2
            target_copy(leaf).wait()

        if not resident:

            @pl.when(block_state[source] == 1)
            def _():
                block_state[source] = 2
                block_copy(source).wait()

    def contribution(number):
        leaf, source = order[number, 0], order[number, 1]
        block = block_ref[source, pl.ds(0, rows), :]
        inner = dot(block, targets_ref[leaf])
        tile = kappa_of(inner, width, half_exponents(block), halves_ref[leaf]).astype(BF16)
        added = None
        for column in range(0, rows, width):
            columns = min(width, rows - column)
            place = pl.ds(rows + column * classes // width, classes * columns // width)
            weights = block_ref[source, place, :]
            if columns < width:
                weights = jnp.concatenate(
                    [weights[:, : width // 2], weights[:, width // 2 :]], axis=0
                )
            term = dot(weights, tile[column : column + columns])
            added = term if added is None else added + term
        return added * jnp.where(number < count, inverse_leaf, 0.0)

    def step(first, carry):
        numbers = [first * group + k for k in range(group)]
        for number in numbers:
            arrive(number)
        added = [contribution(number) for number in numbers]
        for number, term in zip(numbers, added):
            columns = pl.ds(pl.multiple_of(order[number, 0] * size, size), size)
            out_ref[:, columns] += term
        return carry

    lax.fori_loop(0, steps, step, 0)
    start_copy.wait()
    out_ref[...] += start_ref[...]


def near_part(rows, group, slots, targets, halves, start, blocks, resident, out_type):
    classes, columns = start.shape
    leaves, width, size = targets.shape
    tiles = 24
    whole = pl.BlockSpec(memory_space=pltpu.VMEM)
    hbm = pl.BlockSpec(memory_space=pltpu.HBM)
    scratch = [
        pltpu.SMEM((slots.size + group, 2), jnp.int32),
        pltpu.SMEM((leaves,), jnp.int32),
        pltpu.SMEM((blocks.shape[0],), jnp.int32),
        pltpu.VMEM(targets.shape, BF16),
        pltpu.VMEM(start.shape, F32),
    ]
    if not resident:
        scratch.append(pltpu.VMEM(blocks.shape, BF16))
    scratch += [
        pltpu.SemaphoreType.DMA((leaves,)),
        pltpu.SemaphoreType.DMA((blocks.shape[0],)),
        pltpu.SemaphoreType.DMA,
    ]
    return call(
        functools.partial(near_kernel, rows, group, resident),
        "near",
        tiles * 2 * rows * size * (width + classes),
        tiles * rows * size,
        tiles * rows * width * 2 + 4 * 2**20,
        vmem=24,
        out_shape=out_type(start.shape, F32),
        in_specs=[
            pl.BlockSpec(memory_space=pltpu.SMEM),
            whole,
            hbm,
            hbm,
            whole if resident else hbm,
        ],
        out_specs=whole,
        scratch_shapes=scratch,
    )(
        in_hbm(slots),
        in_hbm(halves),
        in_hbm(targets),
        in_hbm(start),
        blocks if resident else in_hbm(blocks),
    )


def swap(value, axis, mask):
    pairs = [(source, source ^ mask) for source in range(lax.axis_size(axis))]
    return lax.ppermute(value, axis, pairs)


def per_device(points, weights, near, counts, skel_leaf, skel_local, skel_upper):
    leaves, rank = skel_leaf.shape
    size = points.shape[0] // leaves
    classes = weights.shape[0]
    slots = near.shape[1]
    sub_count = lax.axis_size("sub")
    grp_count = lax.axis_size("grp")
    devices = sub_count * grp_count
    sub_index = lax.axis_index("sub")
    grp_index = lax.axis_index("grp")
    device = grp_index * sub_count + sub_index
    near_count = NEIGHBOURS
    far_count = sub_count // near_count

    group_first = grp_index * sub_count * leaves
    slot_ids = jnp.arange(slots)
    group_rows = lax.dynamic_slice_in_dim(near, group_first, sub_count * leaves, 0)
    group_counts = lax.dynamic_slice_in_dim(counts, group_first, sub_count * leaves, 0)
    owned = (
        (group_rows // leaves == device)
        & (slot_ids[None, :] < group_counts[:, None])
        & (slot_ids[None, :] > 0)
    )
    chosen = jnp.where(owned, group_rows - device * leaves, -1).reshape(sub_count, leaves * slots)
    chosen = jnp.max(chosen, axis=1)

    first_rows = size - LAST_ROWS
    sent = pack(chosen, points, weights, size, 0, first_rows)
    arrived = lax.all_to_all(sent, "sub", split_axis=0, concat_axis=0, tiled=True)

    near_bits = near_count.bit_length() - 1
    far_bits = far_count.bit_length() - 1
    table, starts, path_lengths = place_table(near_bits, far_bits, grp_count.bit_length() - 1)
    mine = lax.dynamic_slice_in_dim(jnp.asarray(table), device, 1, 0)[0]
    near_slots = jnp.concatenate(
        [
            lax.dynamic_slice_in_dim(near, device * leaves, leaves, 0),
            lax.dynamic_slice_in_dim(counts, device * leaves, leaves, 0)[:, None],
        ],
        axis=1,
    )
    near_rows, far_rows, top_rows, path_nodes = (
        mine[low:high] for low, high in zip(starts[:-1], starts[1:])
    )

    own, skel, up, summary, targets, halves = leaf_level(points, weights, skel_leaf)
    lifted, terms, state = subtree(
        "local",
        leaves,
        leaves - 1,
        0,
        jnp.arange(leaves, dtype=jnp.int32),
        skel_local,
        (skel, summary),
        classes,
    )
    blocks = [[i * near_count + j for j in range(near_count)] for i in range(far_count)]
    state, near_slots, far_rows, top_rows, path_nodes = lax.optimization_barrier(
        (state, near_slots, far_rows, top_rows, path_nodes)
    )
    gathered = lax.all_gather(state, "sub", axis_index_groups=blocks, tiled=False)
    near_lifted, near_terms, state = subtree(
        "near_nodes", near_count, near_count - 1, 1, near_rows, skel_upper, (gathered,), classes
    )
    far_states = [state] + [
        swap(state, "sub", mask * near_count) for mask in range(1, far_count)
    ]
    sent_last = pack(chosen, points, weights, size, first_rows, LAST_ROWS)
    sent_last, far_states = lax.optimization_barrier((sent_last, far_states))
    arrived_last = lax.all_to_all(sent_last, "sub", split_axis=0, concat_axis=0, tiled=True)

    far_lifted, far_terms, state = subtree(
        "far_nodes", far_count, far_count - 1, 2, far_rows, skel_upper, far_states, classes
    )
    top_states = [state] + [swap(state, "grp", mask) for mask in range(1, grp_count)]

    near_slots, state = lax.optimization_barrier((near_slots, state))
    total = near_part(first_rows, GROUP, near_slots, targets, halves, own, arrived, False, pltpu.HBM)

    top_rows, total = lax.optimization_barrier((top_rows, total))
    top_lifted, top_terms, _ = subtree(
        "top_nodes", grp_count, grp_count - 2, 2, top_rows, skel_upper, top_states, classes
    )
    stages = [(top_lifted, top_terms), (far_lifted, far_terms), (near_lifted, near_terms)]
    total = down(
        path_nodes, path_lengths, stages, lifted, terms, up, total
    )
    return near_part(
        LAST_ROWS,
        GROUP,
        near_slots,
        targets,
        halves,
        total,
        arrived_last,
        True,
        jax.ShapeDtypeStruct,
    )


def solution(mesh):
    split = P(("grp", "sub"), None)
    columns = P(None, ("grp", "sub"))
    return jax.shard_map(
        per_device,
        mesh=mesh,
        in_specs=(split, columns, P(), P(), split, split, P()),
        out_specs=columns,
        check_vma=False,
    )
```

```python
import functools
import math

import jax
import jax.numpy as jnp
import numpy as np
from jax import lax
from jax.experimental import pallas as pl
from jax.experimental.pallas import tpu as pltpu
from jax.sharding import PartitionSpec as P

F32 = jnp.float32
BF16 = jnp.bfloat16
LOG2E = 1.4426950408889634
NT = (((1,), (1,)), ((), ()))
LAST_ROWS = 256
GROUP = 1


def call(kernel, name, flops, exps, nbytes, vmem=12, **kw):
    return pl.pallas_call(
        kernel,
        name=name,
        cost_estimate=pl.CostEstimate(flops=flops, bytes_accessed=nbytes, transcendentals=exps),
        compiler_params=pltpu.CompilerParams(vmem_limit_bytes=vmem * 2**20),
        **kw,
    )


def in_hbm(array):
    return pltpu.with_memory_space_constraint(array, pltpu.HBM)


def dot(a, b):
    return jnp.dot(a, b, preferred_element_type=F32)


def dot_nt(a, b):
    return lax.dot_general(a, b, NT, preferred_element_type=F32)


def half_exponents(block):
    sharpness = math.sqrt(block.shape[-1] / 8.0)
    wide = block.astype(F32)
    norms = jnp.sum(wide * wide, axis=-1, keepdims=True)
    return LOG2E * (sharpness * (1.0 - norms) - 0.25)


def as_row(column):
    rows = column.shape[0]
    return jnp.transpose(jnp.broadcast_to(column, (rows, 128)))[0:1, :]


def kappa_of(inner, width, left_half, right_half_row):
    scale = LOG2E * 2.0 * math.sqrt(width / 8.0)
    return jnp.exp2(inner * scale + left_half + right_half_row)


def kappa(left, right, left_half, right_half_row):
    return kappa_of(dot_nt(left, right), left.shape[-1], left_half, right_half_row)


def one_hot(chosen_row, pool):
    rank = chosen_row.shape[1]
    spread = jnp.transpose(jnp.broadcast_to(chosen_row, (128, rank)).astype(F32)).astype(jnp.int32)
    lanes = lax.broadcasted_iota(jnp.int32, (rank, 128), 1)
    pieces = [
        jnp.where(spread == lanes + 128 * j, 1.0, 0.0).astype(BF16) for j in range(pool // 128)
    ]
    return jnp.concatenate(pieces, axis=1)


def score_pieces(rows, classes, width):
    pieces = []
    for column in range(0, rows, width):
        row = rows + column * classes // width
        if rows - column >= width:
            pieces.append((column, width, 0, classes, row, 0))
        else:
            half = classes // 2
            pieces.append((column, width // 2, 0, half, row, 0))
            pieces.append((column, width // 2, half, half, row, width // 2))
    return pieces


def pack_kernel(leaf_size, first, rows, chosen, points_ref, weights_ref, out_ref, sems):
    classes = weights_ref.shape[0]
    pieces = score_pieces(rows, classes, points_ref.shape[1])

    def copies(j):
        start = pl.multiple_of(chosen[j] * leaf_size + first, 128)
        made = [
            pltpu.make_async_copy(
                points_ref.at[pl.ds(start, rows), :],
                out_ref.at[j, pl.ds(0, rows), :],
                sems.at[j, 0],
            )
        ]
        for number, (column, columns, from_class, count, row, lane) in enumerate(pieces):
            made.append(
                pltpu.make_async_copy(
                    weights_ref.at[
                        pl.ds(from_class, count),
                        pl.ds(pl.multiple_of(start + column, 128), columns),
                    ],
                    out_ref.at[j, pl.ds(row, count), pl.ds(lane, columns)],
                    sems.at[j, 1 + number],
                )
            )
        return made

    def start(j, carry):
        @pl.when(chosen[j] >= 0)
        def _():
            for copy in copies(j):
                copy.start()

        return carry

    def finish(j, carry):
        @pl.when(chosen[j] >= 0)
        def _():
            for copy in copies(j):
                copy.wait()

        return carry

    lax.fori_loop(0, out_ref.shape[0], start, 0)
    lax.fori_loop(0, out_ref.shape[0], finish, 0)


def pack(chosen, points, weights, leaf_size, first, rows):
    classes, width = weights.shape[0], points.shape[1]
    shape = (chosen.shape[0], rows + rows * classes // width, width)
    return call(
        functools.partial(pack_kernel, leaf_size, first, rows),
        "pack",
        0,
        0,
        2 * math.prod(shape) * 2,
        out_shape=pltpu.HBM(shape, BF16),
        grid_spec=pltpu.PrefetchScalarGridSpec(
            num_scalar_prefetch=1,
            grid=(1,),
            in_specs=[
                pl.BlockSpec(points.shape, lambda i, c: (0, 0)),
                pl.BlockSpec(weights.shape, lambda i, c: (0, 0)),
            ],
            out_specs=pl.BlockSpec(memory_space=pltpu.HBM),
            scratch_shapes=[
                pltpu.SemaphoreType.DMA((shape[0], 1 + len(score_pieces(rows, classes, width))))
            ],
        ),
    )(chosen, in_hbm(points), in_hbm(weights))


def leaf_kernel(
    points_ref,
    weights_ref,
    chosen_ref,
    own_ref,
    skel_ref,
    up_ref,
    summary_ref,
    target_ref,
    half_ref,
):
    leaf = pl.program_id(0)
    block = points_ref[...]
    turned = jnp.transpose(block)
    target_ref[0] = turned
    leaf_size = block.shape[0]
    inverse_leaf = 1.0 / math.sqrt(leaf_size)
    half = half_exponents(block)
    half_row = as_row(half)
    half_ref[0] = half_row
    tile = kappa_of(dot(block, turned), block.shape[1], half, half_row)
    rows = lax.broadcasted_iota(jnp.int32, tile.shape, 0)
    columns = lax.broadcasted_iota(jnp.int32, tile.shape, 1)
    tile = jnp.where(rows == columns, 0.0, tile).astype(BF16)
    own = dot(weights_ref[...], tile) * inverse_leaf
    own_ref[...] = own
    chosen = chosen_ref[pl.ds(leaf, 1), :]
    rank = chosen.shape[1]
    skel_ref[0] = dot(one_hot(chosen, leaf_size), block).astype(BF16)
    places = lax.broadcasted_iota(jnp.int32, (leaf_size, rank), 0)
    columns_of = jnp.where(places == chosen, 1.0, 0.0).astype(BF16)
    up_ref[0] = dot(tile, columns_of).astype(BF16)
    summary_ref[0] = dot(own.astype(BF16), columns_of).astype(BF16)


def leaf_level(points, weights, skel_leaf):
    leaves, rank = skel_leaf.shape
    classes = weights.shape[0]
    width = points.shape[1]
    size = points.shape[0] // leaves
    return call(
        leaf_kernel,
        "leaf",
        leaves * 2 * size * (size * (width + classes + rank) + rank * width + classes * rank),
        leaves * size * size,
        8 * 2**20,
        out_shape=(
            pltpu.HBM(weights.shape, F32),
            jax.ShapeDtypeStruct((leaves, rank, width), BF16),
            pltpu.HBM((leaves, size, rank), BF16),
            jax.ShapeDtypeStruct((leaves, classes, rank), BF16),
            pltpu.HBM((leaves, width, size), BF16),
            pltpu.HBM((leaves, 1, size), F32),
        ),
        grid=(leaves,),
        in_specs=[
            pl.BlockSpec((size, width), lambda i: (i, 0)),
            pl.BlockSpec((classes, size), lambda i: (0, i)),
            pl.BlockSpec((leaves, rank), lambda i: (0, 0)),
        ],
        out_specs=(
            pl.BlockSpec((classes, size), lambda i: (0, i)),
            pl.BlockSpec((1, rank, width), lambda i: (i, 0, 0)),
            pl.BlockSpec((1, size, rank), lambda i: (i, 0, 0)),
            pl.BlockSpec((1, classes, rank), lambda i: (i, 0, 0)),
            pl.BlockSpec((1, width, size), lambda i: (i, 0, 0)),
            pl.BlockSpec((1, 1, size), lambda i: (i, 0, 0)),
        ),
    )(points, weights, skel_leaf)


def subtree_kernel(count, inner, states, rows, *refs):
    chosen_ref = refs[0]
    inputs = refs[1 : len(refs) - 5]
    lifted_ref, terms_ref, state_ref, nodes, sums = refs[len(refs) - 5 :]
    _, rank, width = nodes.shape
    classes = sums.shape[1]
    inverse_rank = 1.0 / rank
    inverse_pair = 1.0 / (math.sqrt(2.0) * rank)
    if states == 0:
        nodes[pl.ds(0, count)] = inputs[0][...]
        sums[pl.ds(0, count)] = inputs[1][...]
    else:
        for mask in range(count):
            place = lax.bitwise_xor(rows[inner], mask)
            nodes[place] = inputs[mask][pl.ds(0, rank), :]
            sums[place] = inputs[mask][pl.ds(rank, classes), :]

    def pair(i, even, odd, even_half, odd_half):
        tile = kappa(even, odd, even_half, as_row(odd_half)).astype(BF16)
        terms_ref[2 * i] = dot_nt(sums[2 * i + 1], tile) * inverse_rank
        terms_ref[2 * i + 1] = dot(sums[2 * i], tile) * inverse_rank

    def step(i, carry):
        even, odd = nodes[2 * i], nodes[2 * i + 1]
        child = jnp.concatenate([even, odd], axis=0)
        chosen = chosen_ref[pl.ds(rows[i], 1), :]
        half = half_exponents(child)
        parent = dot(one_hot(chosen, 2 * rank), child).astype(BF16)
        lifted = kappa(child, parent, half, as_row(half_exponents(parent)))
        same = lax.broadcasted_iota(jnp.int32, lifted.shape, 0) == chosen
        lifted = jnp.where(same, 0.0, lifted).astype(BF16)
        lifted_ref[i] = lifted
        summed = dot(sums[2 * i], lifted[:rank]) + dot(sums[2 * i + 1], lifted[rank:])
        nodes[count + i] = parent
        sums[count + i] = (summed * inverse_pair).astype(BF16)
        pair(i, even, odd, half[:rank], half[rank:])
        return carry

    lax.fori_loop(0, inner, step, 0)
    if inner == count - 1:
        state_ref[pl.ds(0, rank), :] = nodes[count + inner - 1]
        state_ref[pl.ds(rank, classes), :] = sums[count + inner - 1]
    else:
        even, odd = nodes[2 * inner], nodes[2 * inner + 1]
        pair(inner, even, odd, half_exponents(even), half_exponents(odd))
        state_ref[...] = jnp.zeros_like(state_ref)


def subtree(name, count, inner, states, rows, table, inputs, classes):
    rank = table.shape[1]
    width = inputs[0].shape[-1]

    def whole(array):
        zeros = (0,) * len(array.shape)
        return pl.BlockSpec(array.shape, lambda i, r: zeros)

    shapes = (
        pltpu.HBM((inner, 2 * rank, rank), BF16),
        pltpu.HBM((2 * count - 2, classes, rank), F32),
        jax.ShapeDtypeStruct((rank + classes, width), BF16),
    )
    return call(
        functools.partial(subtree_kernel, count, inner, states),
        name,
        inner * 2 * rank * rank * (5 * width + 4 * classes),
        inner * 3 * rank * rank,
        6 * 2**20,
        vmem=16,
        out_shape=shapes,
        grid_spec=pltpu.PrefetchScalarGridSpec(
            num_scalar_prefetch=1,
            grid=(1,),
            in_specs=[whole(table)] + [whole(array) for array in inputs],
            out_specs=tuple(whole(shape) for shape in shapes),
            scratch_shapes=[
                pltpu.VMEM((2 * count, rank, width), BF16),
                pltpu.VMEM((2 * count, classes, rank), BF16),
            ],
        ),
    )(in_hbm(rows), in_hbm(table), *inputs)


def path_of(place, count):
    numbers = [place]
    while 2 ** len(numbers) < count:
        numbers.append(count + (numbers[-1] >> 1))
    return numbers


def place_table(steps):
    devices = 1 << sum(steps)
    table = []
    for device in range(devices):
        parts, paths, height = [], [], 0
        for number, step in enumerate(steps):
            rows = []
            for u in range(height + 1, height + step + 1):
                under = 1 << (height + step - u)
                base = devices - (devices >> u - 1) + (device >> height + step) * under
                rows += [base + i for i in range(under)]
            if number + 1 == len(steps):
                rows = rows[:-1]
            place = device >> height & (1 << step) - 1
            parts.append(rows + [place])
            paths.insert(0, path_of(place, 1 << step)[::-1])
            height += step
        parts.append([node for path in paths for node in path])
        table.append([number for part in parts for number in part])
    starts = np.cumsum([0] + [len(part) for part in parts]).tolist()
    return np.array(table, np.int32), starts, tuple(len(path) for path in paths)


def down_kernel(path, stages, numbers, *refs):
    lifted_hbm, terms_hbm, up_hbm, own_hbm, out_ref = refs[2 * stages : 2 * stages + 5]
    lifted_ref, terms_ref, up_ref, path_lifted, path_terms, values = refs[2 * stages + 5 : -3]
    path_sems, up_sems, sems = refs[-3:]
    inner, _, rank = lifted_ref.shape
    leaves, size, _ = up_ref.shape
    inverse_rank = 1.0 / rank

    path_copies = []
    for stage, steps in enumerate(path):
        for _ in range(steps):
            at = len(path_copies)
            node = numbers[at]
            copies = [
                pltpu.make_async_copy(
                    refs[2 * stage + 1].at[node], path_terms.at[at], path_sems.at[at, 0]
                )
            ]
            if at > 0:
                half = pl.ds(pl.multiple_of((node & 1) * rank, rank), rank)
                copies.append(
                    pltpu.make_async_copy(
                        refs[2 * stage].at[node >> 1, half, :],
                        path_lifted.at[at],
                        path_sems.at[at, 1],
                    )
                )
            path_copies.append(copies)
    local_copies = [
        pltpu.make_async_copy(terms_hbm, terms_ref, sems.at[0]),
        pltpu.make_async_copy(lifted_hbm, lifted_ref, sems.at[1]),
    ]
    own_copy = pltpu.make_async_copy(own_hbm, out_ref, sems.at[2])
    up_copies = [
        pltpu.make_async_copy(up_hbm.at[leaf], up_ref.at[leaf], up_sems.at[leaf])
        for leaf in range(leaves)
    ]
    for copies in path_copies:
        for copy in copies:
            copy.start()
    for copy in local_copies + [own_copy] + up_copies:
        copy.start()

    value = None
    for at, copies in enumerate(path_copies):
        for copy in copies:
            copy.wait()
        term = path_terms[at]
        if at > 0:
            term = term + dot_nt(value, path_lifted[at]) * inverse_rank
        value = term.astype(BF16)
    values[2 * leaves - 2] = value
    for copy in local_copies:
        copy.wait()

    def lower(step, carry):
        i = inner - 1 - step
        down = dot_nt(values[leaves + i], lifted_ref[i]) * inverse_rank
        values[2 * i] = (terms_ref[2 * i] + down[:, :rank]).astype(BF16)
        values[2 * i + 1] = (terms_ref[2 * i + 1] + down[:, rank:]).astype(BF16)
        return carry

    lax.fori_loop(0, inner, lower, 0)
    own_copy.wait()
    for leaf in range(leaves):
        up_copies[leaf].wait()
        columns = pl.ds(leaf * size, size)
        out_ref[:, columns] += dot_nt(values[leaf], up_ref[leaf]) * inverse_rank


def down(numbers, path, stages, lifted, terms, up, own):
    leaves, size, rank = up.shape
    classes = own.shape[0]
    inputs = [array for stage in stages for array in stage] + [lifted, terms, up, own]
    hbm = pl.BlockSpec(memory_space=pltpu.HBM)
    return call(
        functools.partial(down_kernel, path, len(stages)),
        "down",
        2 * classes * rank * (sum(path) * rank + leaves * size * 2),
        rank * rank,
        8 * 2**20,
        vmem=24,
        out_shape=pltpu.HBM(own.shape, F32),
        in_specs=[pl.BlockSpec(memory_space=pltpu.SMEM)] + [hbm] * len(inputs),
        out_specs=pl.BlockSpec(memory_space=pltpu.VMEM),
        scratch_shapes=[
            pltpu.VMEM(lifted.shape, BF16),
            pltpu.VMEM(terms.shape, F32),
            pltpu.VMEM(up.shape, BF16),
            pltpu.VMEM((sum(path), rank, rank), BF16),
            pltpu.VMEM((sum(path), classes, rank), F32),
            pltpu.VMEM((2 * leaves, classes, rank), BF16),
            pltpu.SemaphoreType.DMA((sum(path), 2)),
            pltpu.SemaphoreType.DMA((leaves,)),
            pltpu.SemaphoreType.DMA((3,)),
        ],
    )(in_hbm(numbers), *(in_hbm(array) for array in inputs))


def near_kernel(
    rows, group, resident, slots, halves_ref, targets_hbm, start_hbm, block_hbm, out_ref, *refs
):
    order, leaf_state, block_state, targets_ref, start_ref = refs[:5]
    leaf_sems, block_sems, start_sem = refs[-3:]
    block_ref = block_hbm if resident else refs[5]
    leaves, width, size = targets_ref.shape
    sources = block_hbm.shape[0]
    classes = out_ref.shape[0]
    inverse_leaf = 1.0 / math.sqrt(size)

    def target_copy(leaf):
        return pltpu.make_async_copy(
            targets_hbm.at[leaf], targets_ref.at[leaf], leaf_sems.at[leaf]
        )

    def block_copy(source):
        return pltpu.make_async_copy(
            block_hbm.at[source], block_ref.at[source], block_sems.at[source]
        )

    def clear(source, carry):
        block_state[source] = 0
        return carry

    def list_leaf(number, filled):
        target_copy(number).start()
        leaf_state[number] = 1

        def list_slot(slot, carry):
            source = lax.rem(slots[number, slot] // leaves, sources)
            place = filled + (slot - 1) // 2

            @pl.when(lax.rem(slot, 2) == 1)
            def _():
                order[place, 0] = number
                order[place, 1] = source
                order[place, 2] = source
                order[place, 3] = 0

            @pl.when(lax.rem(slot, 2) == 0)
            def _():
                order[place, 2] = source
                order[place, 3] = 1

            if not resident:

                @pl.when(block_state[source] == 0)
                def _():
                    block_state[source] = 1
                    block_copy(source).start()

            return carry

        live = slots[number, slots.shape[1] - 1]
        lax.fori_loop(1, live, list_slot, 0)
        return filled + live // 2

    def repeat_last(number, carry):
        for field in range(4):
            order[number, field] = order[count - 1, field]
        return carry

    if not resident:
        lax.fori_loop(0, sources, clear, 0)
    count = lax.fori_loop(0, leaves, list_leaf, 0)
    start_copy = pltpu.make_async_copy(start_hbm, start_ref, start_sem)
    start_copy.start()
    steps = (count + group - 1) // group
    lax.fori_loop(count, steps * group, repeat_last, 0)
    out_ref[...] = jnp.zeros_like(out_ref)

    def arrive(number):
        leaf = order[number, 0]

        @pl.when(leaf_state[leaf] == 1)
        def _():
            leaf_state[leaf] = 2
            target_copy(leaf).wait()

        for field in (1, 2) if not resident else ():
            source = order[number, field]

            @pl.when(block_state[source] == 1)
            def _():
                block_state[source] = 2
                block_copy(source).wait()

    def scores_of(source):
        found = []
        for column in range(0, rows, width):
            columns = min(width, rows - column)
            place = pl.ds(rows + column * classes // width, classes * columns // width)
            weights = block_ref[source, place, :]
            if columns < width:
                weights = jnp.concatenate(
                    [weights[:, : width // 2], weights[:, width // 2 :]], axis=0
                )
            found.append(weights)
        return found

    def contribution(number):
        leaf, one, two = order[number, 0], order[number, 1], order[number, 2]
        block = jnp.concatenate(
            [block_ref[one, pl.ds(0, rows), :], block_ref[two, pl.ds(0, rows), :]], axis=0
        )
        inner = dot(block, targets_ref[leaf])
        tile = kappa_of(inner, width, half_exponents(block), halves_ref[leaf]).astype(BF16)
        second = order[number, 3].astype(F32)
        scores = scores_of(one)
        scores += [(part.astype(F32) * second).astype(BF16) for part in scores_of(two)]
        added = dot(jnp.concatenate(scores, axis=1), tile)
        return added * jnp.where(number < count, inverse_leaf, 0.0)

    def step(first, carry):
        numbers = [first * group + k for k in range(group)]
        for number in numbers:
            arrive(number)
        added = [contribution(number) for number in numbers]
        for number, term in zip(numbers, added):
            columns = pl.ds(pl.multiple_of(order[number, 0] * size, size), size)
            out_ref[:, columns] += term
        return carry

    lax.fori_loop(0, steps, step, 0)
    start_copy.wait()
    out_ref[...] += start_ref[...]


def near_part(rows, group, slots, targets, halves, start, blocks, resident, out_type):
    classes, columns = start.shape
    leaves, width, size = targets.shape
    tiles = 24
    whole = pl.BlockSpec(memory_space=pltpu.VMEM)
    hbm = pl.BlockSpec(memory_space=pltpu.HBM)
    scratch = [
        pltpu.SMEM((slots.size // 2 + group, 4), jnp.int32),
        pltpu.SMEM((leaves,), jnp.int32),
        pltpu.SMEM((blocks.shape[0],), jnp.int32),
        pltpu.VMEM(targets.shape, BF16),
        pltpu.VMEM(start.shape, F32),
    ]
    if not resident:
        scratch.append(pltpu.VMEM(blocks.shape, BF16))
    scratch += [
        pltpu.SemaphoreType.DMA((leaves,)),
        pltpu.SemaphoreType.DMA((blocks.shape[0],)),
        pltpu.SemaphoreType.DMA,
    ]
    return call(
        functools.partial(near_kernel, rows, group, resident),
        "near",
        tiles * 2 * rows * size * (width + classes),
        tiles * rows * size,
        tiles * rows * width * 2 + 4 * 2**20,
        vmem=24,
        out_shape=out_type(start.shape, F32),
        in_specs=[
            pl.BlockSpec(memory_space=pltpu.SMEM),
            whole,
            hbm,
            hbm,
            whole if resident else hbm,
        ],
        out_specs=whole,
        scratch_shapes=scratch,
    )(
        in_hbm(slots),
        in_hbm(halves),
        in_hbm(targets),
        in_hbm(start),
        blocks if resident else in_hbm(blocks),
    )


def swap(value, axis, mask):
    pairs = [(source, source ^ mask) for source in range(lax.axis_size(axis))]
    return lax.ppermute(value, axis, pairs)


def per_device(points, weights, near, counts, skel_leaf, skel_local, skel_upper):
    leaves, rank = skel_leaf.shape
    size = points.shape[0] // leaves
    classes = weights.shape[0]
    slots = near.shape[1]
    sub_count = lax.axis_size("sub")
    grp_count = lax.axis_size("grp")
    sub_index = lax.axis_index("sub")
    grp_index = lax.axis_index("grp")
    device = grp_index * sub_count + sub_index

    group_first = grp_index * sub_count * leaves
    slot_ids = jnp.arange(slots)
    group_rows = lax.dynamic_slice_in_dim(near, group_first, sub_count * leaves, 0)
    group_counts = lax.dynamic_slice_in_dim(counts, group_first, sub_count * leaves, 0)
    owned = (
        (group_rows // leaves == device)
        & (slot_ids[None, :] < group_counts[:, None])
        & (slot_ids[None, :] > 0)
    )
    chosen = jnp.where(owned, group_rows - device * leaves, -1).reshape(sub_count, leaves * slots)
    chosen = jnp.max(chosen, axis=1)

    first_rows = size - LAST_ROWS
    sent = pack(chosen, points, weights, size, 0, first_rows)
    arrived = lax.all_to_all(sent, "sub", split_axis=0, concat_axis=0, tiled=True)

    sub_bits = sub_count.bit_length() - 1
    far_bits = (sub_bits - 1) // 2
    steps = [1, sub_bits - 1 - far_bits, far_bits, grp_count.bit_length() - 1]
    table, starts, path_lengths = place_table(steps)
    mine = lax.dynamic_slice_in_dim(jnp.asarray(table), device, 1, 0)[0]
    *stage_rows, path_nodes = (mine[low:high] for low, high in zip(starts[:-1], starts[1:]))
    near_slots = jnp.concatenate(
        [
            lax.dynamic_slice_in_dim(near, device * leaves, leaves, 0),
            lax.dynamic_slice_in_dim(counts, device * leaves, leaves, 0)[:, None],
        ],
        axis=1,
    )

    own, skel, up, summary, targets, halves = leaf_level(points, weights, skel_leaf)
    lifted, terms, state = subtree(
        "local",
        leaves,
        leaves - 1,
        0,
        jnp.arange(leaves, dtype=jnp.int32),
        skel_local,
        (skel, summary),
        classes,
    )
    state, near_slots, stage_rows, path_nodes = lax.optimization_barrier(
        (state, near_slots, stage_rows, path_nodes)
    )

    def exchange(state, stage):
        axis = "grp" if stage + 1 == len(steps) else "sub"
        low = 0 if axis == "grp" else sum(steps[:stage])
        return [state] + [swap(state, axis, mask << low) for mask in range(1, 1 << steps[stage])]

    def climb(name, states, stage, rows):
        count = 1 << steps[stage]
        inner = count - 2 if stage + 1 == len(steps) else count - 1
        *done, state = subtree(name, count, inner, 2, rows, skel_upper, states, classes)
        return done, state

    core_stage, state = climb("core_nodes", exchange(state, 0), 0, stage_rows[0])
    x_states = exchange(state, 1)
    sent_last = pack(chosen, points, weights, size, first_rows, LAST_ROWS)
    sent_last, x_rows = lax.optimization_barrier((sent_last, stage_rows[1]))
    x_stage, state = climb("x_nodes", x_states, 1, x_rows)
    y_states = exchange(state, 2)
    sent_last, _ = lax.optimization_barrier((sent_last, y_states))
    arrived_last = lax.all_to_all(sent_last, "sub", split_axis=0, concat_axis=0, tiled=True)

    y_stage, state = climb("y_nodes", y_states, 2, stage_rows[2])
    z_states = exchange(state, 3)
    near_slots, _ = lax.optimization_barrier((near_slots, state))
    total = near_part(
        first_rows, GROUP, near_slots, targets, halves, own, arrived, False, pltpu.HBM
    )
    z_rows, total = lax.optimization_barrier((stage_rows[3], total))
    z_stage, _ = climb("z_nodes", z_states, 3, z_rows)
    stages = [z_stage, y_stage, x_stage, core_stage]
    total = down(path_nodes, path_lengths, stages, lifted, terms, up, total)
    return near_part(
        LAST_ROWS,
        GROUP,
        near_slots,
        targets,
        halves,
        total,
        arrived_last,
        False,
        jax.ShapeDtypeStruct,
    )


def solution(mesh):
    split = P(("grp", "sub"), None)
    columns = P(None, ("grp", "sub"))
    return jax.shard_map(
        per_device,
        mesh=mesh,
        in_specs=(split, columns, P(), P(), split, split, P()),
        out_specs=columns,
        check_vma=False,
    )
```

```python
import functools
import math

import jax
import jax.numpy as jnp
import numpy as np
from jax import lax
from jax.experimental import pallas as pl
from jax.experimental.pallas import tpu as pltpu
from jax.sharding import PartitionSpec as P

F32 = jnp.float32
BF16 = jnp.bfloat16
LOG2E = 1.4426950408889634
NT = (((1,), (1,)), ((), ()))
PARTS = (256, 128, 128)
GROUP = 1


def call(kernel, name, flops, exps, nbytes, vmem=12, **kw):
    return pl.pallas_call(
        kernel,
        name=name,
        cost_estimate=pl.CostEstimate(flops=flops, bytes_accessed=nbytes, transcendentals=exps),
        compiler_params=pltpu.CompilerParams(vmem_limit_bytes=vmem * 2**20),
        **kw,
    )


def in_hbm(array):
    return pltpu.with_memory_space_constraint(array, pltpu.HBM)


def dot(a, b):
    return jnp.dot(a, b, preferred_element_type=F32)


def dot_nt(a, b):
    return lax.dot_general(a, b, NT, preferred_element_type=F32)


def half_exponents(block):
    sharpness = math.sqrt(block.shape[-1] / 8.0)
    wide = block.astype(F32)
    norms = jnp.sum(wide * wide, axis=-1, keepdims=True)
    return LOG2E * (sharpness * (1.0 - norms) - 0.25)


def as_row(column):
    rows = column.shape[0]
    return jnp.transpose(jnp.broadcast_to(column, (rows, 128)))[0:1, :]


def kappa_of(inner, width, left_half, right_half_row):
    scale = LOG2E * 2.0 * math.sqrt(width / 8.0)
    return jnp.exp2(inner * scale + left_half + right_half_row)


def kappa(left, right, left_half, right_half_row):
    return kappa_of(dot_nt(left, right), left.shape[-1], left_half, right_half_row)


def one_hot(chosen_row, pool):
    rank = chosen_row.shape[1]
    spread = jnp.transpose(jnp.broadcast_to(chosen_row, (128, rank)).astype(F32)).astype(jnp.int32)
    lanes = lax.broadcasted_iota(jnp.int32, (rank, 128), 1)
    pieces = [
        jnp.where(spread == lanes + 128 * j, 1.0, 0.0).astype(BF16) for j in range(pool // 128)
    ]
    return jnp.concatenate(pieces, axis=1)


def score_pieces(rows, classes, width):
    pieces = []
    for column in range(0, rows, width):
        row = rows + column * classes // width
        if rows - column >= width:
            pieces.append((column, width, 0, classes, row, 0))
        else:
            half = classes // 2
            pieces.append((column, width // 2, 0, half, row, 0))
            pieces.append((column, width // 2, half, half, row, width // 2))
    return pieces


def pack_kernel(leaf_size, first, rows, chosen, points_ref, weights_ref, out_ref, sems):
    classes = weights_ref.shape[0]
    pieces = score_pieces(rows, classes, points_ref.shape[1])

    def copies(j):
        start = pl.multiple_of(chosen[j] * leaf_size + first, 128)
        made = [
            pltpu.make_async_copy(
                points_ref.at[pl.ds(start, rows), :],
                out_ref.at[j, pl.ds(0, rows), :],
                sems.at[j, 0],
            )
        ]
        for number, (column, columns, from_class, count, row, lane) in enumerate(pieces):
            made.append(
                pltpu.make_async_copy(
                    weights_ref.at[
                        pl.ds(from_class, count),
                        pl.ds(pl.multiple_of(start + column, 128), columns),
                    ],
                    out_ref.at[j, pl.ds(row, count), pl.ds(lane, columns)],
                    sems.at[j, 1 + number],
                )
            )
        return made

    def start(j, carry):
        @pl.when(chosen[j] >= 0)
        def _():
            for copy in copies(j):
                copy.start()

        return carry

    def finish(j, carry):
        @pl.when(chosen[j] >= 0)
        def _():
            for copy in copies(j):
                copy.wait()

        return carry

    lax.fori_loop(0, out_ref.shape[0], start, 0)
    lax.fori_loop(0, out_ref.shape[0], finish, 0)


def pack(chosen, points, weights, leaf_size, first, rows):
    classes, width = weights.shape[0], points.shape[1]
    shape = (chosen.shape[0], rows + rows * classes // width, width)
    return call(
        functools.partial(pack_kernel, leaf_size, first, rows),
        "pack",
        0,
        0,
        2 * math.prod(shape) * 2,
        out_shape=pltpu.HBM(shape, BF16),
        grid_spec=pltpu.PrefetchScalarGridSpec(
            num_scalar_prefetch=1,
            grid=(1,),
            in_specs=[
                pl.BlockSpec(points.shape, lambda i, c: (0, 0)),
                pl.BlockSpec(weights.shape, lambda i, c: (0, 0)),
            ],
            out_specs=pl.BlockSpec(memory_space=pltpu.HBM),
            scratch_shapes=[
                pltpu.SemaphoreType.DMA((shape[0], 1 + len(score_pieces(rows, classes, width))))
            ],
        ),
    )(chosen, in_hbm(points), in_hbm(weights))


def leaf_kernel(
    points_ref,
    weights_ref,
    chosen_ref,
    own_ref,
    skel_ref,
    up_ref,
    summary_ref,
    target_ref,
    half_ref,
):
    leaf = pl.program_id(0)
    block = points_ref[...]
    turned = jnp.transpose(block)
    target_ref[0] = turned
    leaf_size = block.shape[0]
    inverse_leaf = 1.0 / math.sqrt(leaf_size)
    half = half_exponents(block)
    half_row = as_row(half)
    half_ref[0] = half_row
    tile = kappa_of(dot(block, turned), block.shape[1], half, half_row)
    rows = lax.broadcasted_iota(jnp.int32, tile.shape, 0)
    columns = lax.broadcasted_iota(jnp.int32, tile.shape, 1)
    tile = jnp.where(rows == columns, 0.0, tile).astype(BF16)
    own = dot(weights_ref[...], tile) * inverse_leaf
    own_ref[...] = own
    chosen = chosen_ref[pl.ds(leaf, 1), :]
    rank = chosen.shape[1]
    skel_ref[0] = dot(one_hot(chosen, leaf_size), block).astype(BF16)
    places = lax.broadcasted_iota(jnp.int32, (leaf_size, rank), 0)
    columns_of = jnp.where(places == chosen, 1.0, 0.0).astype(BF16)
    up_ref[0] = dot(tile, columns_of).astype(BF16)
    summary_ref[0] = dot(own.astype(BF16), columns_of).astype(BF16)


def leaf_level(points, weights, skel_leaf):
    leaves, rank = skel_leaf.shape
    classes = weights.shape[0]
    width = points.shape[1]
    size = points.shape[0] // leaves
    return call(
        leaf_kernel,
        "leaf",
        leaves * 2 * size * (size * (width + classes + rank) + rank * width + classes * rank),
        leaves * size * size,
        8 * 2**20,
        out_shape=(
            pltpu.HBM(weights.shape, F32),
            jax.ShapeDtypeStruct((leaves, rank, width), BF16),
            pltpu.HBM((leaves, size, rank), BF16),
            jax.ShapeDtypeStruct((leaves, classes, rank), BF16),
            pltpu.HBM((leaves, width, size), BF16),
            pltpu.HBM((leaves, 1, size), F32),
        ),
        grid=(leaves,),
        in_specs=[
            pl.BlockSpec((size, width), lambda i: (i, 0)),
            pl.BlockSpec((classes, size), lambda i: (0, i)),
            pl.BlockSpec((leaves, rank), lambda i: (0, 0)),
        ],
        out_specs=(
            pl.BlockSpec((classes, size), lambda i: (0, i)),
            pl.BlockSpec((1, rank, width), lambda i: (i, 0, 0)),
            pl.BlockSpec((1, size, rank), lambda i: (i, 0, 0)),
            pl.BlockSpec((1, classes, rank), lambda i: (i, 0, 0)),
            pl.BlockSpec((1, width, size), lambda i: (i, 0, 0)),
            pl.BlockSpec((1, 1, size), lambda i: (i, 0, 0)),
        ),
    )(points, weights, skel_leaf)


def subtree_kernel(count, inner, states, rows, *refs):
    chosen_ref = refs[0]
    inputs = refs[1 : len(refs) - 5]
    lifted_ref, terms_ref, state_ref, nodes, sums = refs[len(refs) - 5 :]
    _, rank, width = nodes.shape
    classes = sums.shape[1]
    inverse_rank = 1.0 / rank
    inverse_pair = 1.0 / (math.sqrt(2.0) * rank)
    if states == 0:
        nodes[pl.ds(0, count)] = inputs[0][...]
        sums[pl.ds(0, count)] = inputs[1][...]
    else:
        for mask in range(count):
            place = lax.bitwise_xor(rows[inner], mask)
            nodes[place] = inputs[mask][pl.ds(0, rank), :]
            sums[place] = inputs[mask][pl.ds(rank, classes), :]

    def pair(i, even, odd, even_half, odd_half):
        tile = kappa(even, odd, even_half, as_row(odd_half)).astype(BF16)
        terms_ref[2 * i] = dot_nt(sums[2 * i + 1], tile) * inverse_rank
        terms_ref[2 * i + 1] = dot(sums[2 * i], tile) * inverse_rank

    def step(i, carry):
        even, odd = nodes[2 * i], nodes[2 * i + 1]
        child = jnp.concatenate([even, odd], axis=0)
        chosen = chosen_ref[pl.ds(rows[i], 1), :]
        half = half_exponents(child)
        parent = dot(one_hot(chosen, 2 * rank), child).astype(BF16)
        lifted = kappa(child, parent, half, as_row(half_exponents(parent)))
        same = lax.broadcasted_iota(jnp.int32, lifted.shape, 0) == chosen
        lifted = jnp.where(same, 0.0, lifted).astype(BF16)
        lifted_ref[i] = lifted
        summed = dot(sums[2 * i], lifted[:rank]) + dot(sums[2 * i + 1], lifted[rank:])
        nodes[count + i] = parent
        sums[count + i] = (summed * inverse_pair).astype(BF16)
        pair(i, even, odd, half[:rank], half[rank:])
        return carry

    if count > 4:
        lax.fori_loop(0, inner, step, 0)
    else:
        for i in range(inner):
            step(i, 0)
    if inner == count - 1:
        state_ref[pl.ds(0, rank), :] = nodes[count + inner - 1]
        state_ref[pl.ds(rank, classes), :] = sums[count + inner - 1]
    else:
        even, odd = nodes[2 * inner], nodes[2 * inner + 1]
        pair(inner, even, odd, half_exponents(even), half_exponents(odd))
        state_ref[...] = jnp.zeros_like(state_ref)


def subtree(name, count, inner, states, rows, table, inputs, classes):
    rank = table.shape[1]
    width = inputs[0].shape[-1]

    def whole(array):
        zeros = (0,) * len(array.shape)
        return pl.BlockSpec(array.shape, lambda i, r: zeros)

    shapes = (
        pltpu.HBM((inner, 2 * rank, rank), BF16),
        pltpu.HBM((2 * count - 2, classes, rank), F32),
        jax.ShapeDtypeStruct((rank + classes, width), BF16),
    )
    return call(
        functools.partial(subtree_kernel, count, inner, states),
        name,
        inner * 2 * rank * rank * (5 * width + 4 * classes),
        inner * 3 * rank * rank,
        6 * 2**20,
        vmem=16,
        out_shape=shapes,
        grid_spec=pltpu.PrefetchScalarGridSpec(
            num_scalar_prefetch=1,
            grid=(1,),
            in_specs=[whole(table)] + [whole(array) for array in inputs],
            out_specs=tuple(whole(shape) for shape in shapes),
            scratch_shapes=[
                pltpu.VMEM((2 * count, rank, width), BF16),
                pltpu.VMEM((2 * count, classes, rank), BF16),
            ],
        ),
    )(in_hbm(rows), in_hbm(table), *inputs)


def path_of(place, count):
    numbers = [place]
    while 2 ** len(numbers) < count:
        numbers.append(count + (numbers[-1] >> 1))
    return numbers


def place_table(steps):
    devices = 1 << sum(steps)
    table = []
    for device in range(devices):
        parts, paths, height = [], [], 0
        for number, step in enumerate(steps):
            rows = []
            for u in range(height + 1, height + step + 1):
                under = 1 << (height + step - u)
                base = devices - (devices >> u - 1) + (device >> height + step) * under
                rows += [base + i for i in range(under)]
            if number + 1 == len(steps):
                rows = rows[:-1]
            place = device >> height & (1 << step) - 1
            parts.append(rows + [place])
            paths.insert(0, path_of(place, 1 << step)[::-1])
            height += step
        parts.append([node for path in paths for node in path])
        table.append([number for part in parts for number in part])
    starts = np.cumsum([0] + [len(part) for part in parts]).tolist()
    return np.array(table, np.int32), starts, tuple(len(path) for path in paths)


def down_kernel(path, stages, numbers, *refs):
    lifted_hbm, terms_hbm, up_hbm, own_hbm, out_ref = refs[2 * stages : 2 * stages + 5]
    lifted_ref, terms_ref, up_ref, path_lifted, path_terms, values = refs[2 * stages + 5 : -3]
    path_sems, up_sems, sems = refs[-3:]
    inner, _, rank = lifted_ref.shape
    leaves, size, _ = up_ref.shape
    inverse_rank = 1.0 / rank

    path_copies = []
    for stage, steps in enumerate(path):
        for _ in range(steps):
            at = len(path_copies)
            node = numbers[at]
            copies = [
                pltpu.make_async_copy(
                    refs[2 * stage + 1].at[node], path_terms.at[at], path_sems.at[at, 0]
                )
            ]
            if at > 0:
                half = pl.ds(pl.multiple_of((node & 1) * rank, rank), rank)
                copies.append(
                    pltpu.make_async_copy(
                        refs[2 * stage].at[node >> 1, half, :],
                        path_lifted.at[at],
                        path_sems.at[at, 1],
                    )
                )
            path_copies.append(copies)
    local_copies = [
        pltpu.make_async_copy(terms_hbm, terms_ref, sems.at[0]),
        pltpu.make_async_copy(lifted_hbm, lifted_ref, sems.at[1]),
    ]
    own_copy = pltpu.make_async_copy(own_hbm, out_ref, sems.at[2])
    up_copies = [
        pltpu.make_async_copy(up_hbm.at[leaf], up_ref.at[leaf], up_sems.at[leaf])
        for leaf in range(leaves)
    ]
    for copies in path_copies:
        for copy in copies:
            copy.start()
    for copy in local_copies + [own_copy] + up_copies:
        copy.start()

    value = None
    for at, copies in enumerate(path_copies):
        for copy in copies:
            copy.wait()
        term = path_terms[at]
        if at > 0:
            term = term + dot_nt(value, path_lifted[at]) * inverse_rank
        value = term.astype(BF16)
    values[2 * leaves - 2] = value
    for copy in local_copies:
        copy.wait()

    for i in range(inner - 1, -1, -1):
        below = dot_nt(values[leaves + i], lifted_ref[i]) * inverse_rank
        values[2 * i] = (terms_ref[2 * i] + below[:, :rank]).astype(BF16)
        values[2 * i + 1] = (terms_ref[2 * i + 1] + below[:, rank:]).astype(BF16)
    own_copy.wait()
    for leaf in range(leaves):
        up_copies[leaf].wait()
        columns = pl.ds(leaf * size, size)
        out_ref[:, columns] += dot_nt(values[leaf], up_ref[leaf]) * inverse_rank


def down(numbers, path, stages, lifted, terms, up, own):
    leaves, size, rank = up.shape
    classes = own.shape[0]
    inputs = [array for stage in stages for array in stage] + [lifted, terms, up, own]
    hbm = pl.BlockSpec(memory_space=pltpu.HBM)
    return call(
        functools.partial(down_kernel, path, len(stages)),
        "down",
        2 * classes * rank * (sum(path) * rank + leaves * size * 2),
        rank * rank,
        8 * 2**20,
        vmem=24,
        out_shape=pltpu.HBM(own.shape, F32),
        in_specs=[pl.BlockSpec(memory_space=pltpu.SMEM)] + [hbm] * len(inputs),
        out_specs=pl.BlockSpec(memory_space=pltpu.VMEM),
        scratch_shapes=[
            pltpu.VMEM(lifted.shape, BF16),
            pltpu.VMEM(terms.shape, F32),
            pltpu.VMEM(up.shape, BF16),
            pltpu.VMEM((sum(path), rank, rank), BF16),
            pltpu.VMEM((sum(path), classes, rank), F32),
            pltpu.VMEM((2 * leaves, classes, rank), BF16),
            pltpu.SemaphoreType.DMA((sum(path), 2)),
            pltpu.SemaphoreType.DMA((leaves,)),
            pltpu.SemaphoreType.DMA((3,)),
        ],
    )(in_hbm(numbers), *(in_hbm(array) for array in inputs))


def near_kernel(
    rows, group, resident, slots, halves_ref, targets_hbm, start_hbm, block_hbm, out_ref, *refs
):
    order, leaf_state, block_state, targets_ref, start_ref = refs[:5]
    leaf_sems, block_sems, start_sem = refs[-3:]
    block_ref = block_hbm if resident else refs[5]
    leaves, width, size = targets_ref.shape
    sources = block_hbm.shape[0]
    classes = out_ref.shape[0]
    inverse_leaf = 1.0 / math.sqrt(size)

    def target_copy(leaf):
        return pltpu.make_async_copy(
            targets_hbm.at[leaf], targets_ref.at[leaf], leaf_sems.at[leaf]
        )

    def block_copy(source):
        return pltpu.make_async_copy(
            block_hbm.at[source], block_ref.at[source], block_sems.at[source]
        )

    def clear(source, carry):
        block_state[source] = 0
        return carry

    def list_leaf(number, filled):
        target_copy(number).start()
        leaf_state[number] = 1

        def list_slot(slot, carry):
            source = lax.rem(slots[number, slot] // leaves, sources)
            place = filled + (slot - 1) // 2

            @pl.when(lax.rem(slot, 2) == 1)
            def _():
                order[place, 0] = number
                order[place, 1] = source
                order[place, 2] = source
                order[place, 3] = 0

            @pl.when(lax.rem(slot, 2) == 0)
            def _():
                order[place, 2] = source
                order[place, 3] = 1

            if not resident:

                @pl.when(block_state[source] == 0)
                def _():
                    block_state[source] = 1
                    block_copy(source).start()

            return carry

        live = slots[number, slots.shape[1] - 1]
        lax.fori_loop(1, live, list_slot, 0)
        return filled + live // 2

    def repeat_last(number, carry):
        for field in range(4):
            order[number, field] = order[count - 1, field]
        return carry

    if not resident:
        lax.fori_loop(0, sources, clear, 0)
    count = lax.fori_loop(0, leaves, list_leaf, 0)
    start_copy = pltpu.make_async_copy(start_hbm, start_ref, start_sem)
    start_copy.start()
    steps = (count + group - 1) // group
    lax.fori_loop(count, steps * group, repeat_last, 0)
    out_ref[...] = jnp.zeros_like(out_ref)

    def arrive(number):
        leaf = order[number, 0]

        @pl.when(leaf_state[leaf] == 1)
        def _():
            leaf_state[leaf] = 2
            target_copy(leaf).wait()

        for field in (1, 2) if not resident else ():
            source = order[number, field]

            @pl.when(block_state[source] == 1)
            def _():
                block_state[source] = 2
                block_copy(source).wait()

    def scores_of(source):
        found = []
        for column in range(0, rows, width):
            columns = min(width, rows - column)
            place = pl.ds(rows + column * classes // width, classes * columns // width)
            weights = block_ref[source, place, :]
            if columns < width:
                weights = jnp.concatenate(
                    [weights[:, : width // 2], weights[:, width // 2 :]], axis=0
                )
            found.append(weights)
        return found

    def contribution(number):
        leaf, one, two = order[number, 0], order[number, 1], order[number, 2]
        block = jnp.concatenate(
            [block_ref[one, pl.ds(0, rows), :], block_ref[two, pl.ds(0, rows), :]], axis=0
        )
        inner = dot(block, targets_ref[leaf])
        tile = kappa_of(inner, width, half_exponents(block), halves_ref[leaf]).astype(BF16)
        second = order[number, 3].astype(F32)
        scores = scores_of(one)
        scores += [(part.astype(F32) * second).astype(BF16) for part in scores_of(two)]
        added = dot(jnp.concatenate(scores, axis=1), tile)
        return added * jnp.where(number < count, inverse_leaf, 0.0)

    def step(first, carry):
        numbers = [first * group + k for k in range(group)]
        for number in numbers:
            arrive(number)
        added = [contribution(number) for number in numbers]
        for number, term in zip(numbers, added):
            columns = pl.ds(pl.multiple_of(order[number, 0] * size, size), size)
            out_ref[:, columns] += term
        return carry

    lax.fori_loop(0, steps, step, 0)
    start_copy.wait()
    out_ref[...] += start_ref[...]


def near_part(rows, group, slots, targets, halves, start, blocks, resident, out_type):
    classes, columns = start.shape
    leaves, width, size = targets.shape
    tiles = 24
    whole = pl.BlockSpec(memory_space=pltpu.VMEM)
    hbm = pl.BlockSpec(memory_space=pltpu.HBM)
    scratch = [
        pltpu.SMEM((slots.size // 2 + group, 4), jnp.int32),
        pltpu.SMEM((leaves,), jnp.int32),
        pltpu.SMEM((blocks.shape[0],), jnp.int32),
        pltpu.VMEM(targets.shape, BF16),
        pltpu.VMEM(start.shape, F32),
    ]
    if not resident:
        scratch.append(pltpu.VMEM(blocks.shape, BF16))
    scratch += [
        pltpu.SemaphoreType.DMA((leaves,)),
        pltpu.SemaphoreType.DMA((blocks.shape[0],)),
        pltpu.SemaphoreType.DMA,
    ]
    return call(
        functools.partial(near_kernel, rows, group, resident),
        "near",
        tiles * 2 * rows * size * (width + classes),
        tiles * rows * size,
        tiles * rows * width * 2 + 4 * 2**20,
        vmem=24,
        out_shape=out_type(start.shape, F32),
        in_specs=[
            pl.BlockSpec(memory_space=pltpu.SMEM),
            whole,
            hbm,
            hbm,
            whole if resident else hbm,
        ],
        out_specs=whole,
        scratch_shapes=scratch,
    )(
        in_hbm(slots),
        in_hbm(halves),
        in_hbm(targets),
        in_hbm(start),
        blocks if resident else in_hbm(blocks),
    )


def swap(value, axis, mask):
    pairs = [(source, source ^ mask) for source in range(lax.axis_size(axis))]
    return lax.ppermute(value, axis, pairs)


def per_device(points, weights, near, counts, skel_leaf, skel_local, skel_upper):
    leaves, rank = skel_leaf.shape
    size = points.shape[0] // leaves
    classes = weights.shape[0]
    slots = near.shape[1]
    sub_count = lax.axis_size("sub")
    grp_count = lax.axis_size("grp")
    sub_index = lax.axis_index("sub")
    grp_index = lax.axis_index("grp")
    device = grp_index * sub_count + sub_index

    group_first = grp_index * sub_count * leaves
    slot_ids = jnp.arange(slots)
    group_rows = lax.dynamic_slice_in_dim(near, group_first, sub_count * leaves, 0)
    group_counts = lax.dynamic_slice_in_dim(counts, group_first, sub_count * leaves, 0)
    owned = (
        (group_rows // leaves == device)
        & (slot_ids[None, :] < group_counts[:, None])
        & (slot_ids[None, :] > 0)
    )
    chosen = jnp.where(owned, group_rows - device * leaves, -1).reshape(sub_count, leaves * slots)
    chosen = jnp.max(chosen, axis=1)

    def send(block):
        return lax.all_to_all(block, "sub", split_axis=0, concat_axis=0, tiled=True)

    arrived = [send(pack(chosen, points, weights, size, 0, PARTS[0]))]

    sub_bits = sub_count.bit_length() - 1
    far_bits = (sub_bits - 1) // 2
    steps = [1, sub_bits - 1 - far_bits, far_bits, grp_count.bit_length() - 1]
    table, starts, path_lengths = place_table(steps)
    mine = lax.dynamic_slice_in_dim(jnp.asarray(table), device, 1, 0)[0]
    *stage_rows, path_nodes = (mine[low:high] for low, high in zip(starts[:-1], starts[1:]))
    near_slots = jnp.concatenate(
        [
            lax.dynamic_slice_in_dim(near, device * leaves, leaves, 0),
            lax.dynamic_slice_in_dim(counts, device * leaves, leaves, 0)[:, None],
        ],
        axis=1,
    )

    own, skel, up, summary, targets, halves = leaf_level(points, weights, skel_leaf)
    lifted, terms, state = subtree(
        "local",
        leaves,
        leaves - 1,
        0,
        jnp.arange(leaves, dtype=jnp.int32),
        skel_local,
        (skel, summary),
        classes,
    )
    state, near_slots, stage_rows, path_nodes = lax.optimization_barrier(
        (state, near_slots, stage_rows, path_nodes)
    )

    def exchange(state, stage):
        axis = "grp" if stage + 1 == len(steps) else "sub"
        low = 0 if axis == "grp" else sum(steps[:stage])
        return [state] + [swap(state, axis, mask << low) for mask in range(1, 1 << steps[stage])]

    def climb(name, states, stage, rows):
        count = 1 << steps[stage]
        inner = count - 2 if stage + 1 == len(steps) else count - 1
        *done, state = subtree(name, count, inner, 2, rows, skel_upper, states, classes)
        return done, state

    core_stage, state = climb("core_nodes", exchange(state, 0), 0, stage_rows[0])
    x_states = exchange(state, 1)
    sent = [
        pack(chosen, points, weights, size, sum(PARTS[:part]), PARTS[part]) for part in (1, 2)
    ]
    sent, x_rows, x_states = lax.optimization_barrier((sent, stage_rows[1], x_states))
    arrived.append(send(sent[0]))
    x_stage, state = climb("x_nodes", x_states, 1, x_rows)
    y_states = exchange(state, 2)

    def near_sum(part, slots, start, out_type=pltpu.HBM):
        return near_part(
            PARTS[part], GROUP, slots, targets, halves, start, arrived[part], part == 2, out_type
        )

    near_slots, _ = lax.optimization_barrier((near_slots, state))
    total = near_sum(0, near_slots, own)
    sent_last, _, _ = lax.optimization_barrier((sent[1], y_states, total))
    arrived.append(send(sent_last))
    y_stage, state = climb("y_nodes", y_states, 2, stage_rows[2])
    z_states = exchange(state, 3)
    near_slots, _ = lax.optimization_barrier((near_slots, state))
    total = near_sum(1, near_slots, total)
    z_rows, total = lax.optimization_barrier((stage_rows[3], total))
    z_stage, _ = climb("z_nodes", z_states, 3, z_rows)
    stages = [z_stage, y_stage, x_stage, core_stage]
    total = down(path_nodes, path_lengths, stages, lifted, terms, up, total)
    return near_sum(2, near_slots, total, jax.ShapeDtypeStruct)


def solution(mesh):
    split = P(("grp", "sub"), None)
    columns = P(None, ("grp", "sub"))
    return jax.shard_map(
        per_device,
        mesh=mesh,
        in_specs=(split, columns, P(), P(), split, split, P()),
        out_specs=columns,
        check_vma=False,
    )
```

```python
import functools
import math

import jax
import jax.numpy as jnp
import numpy as np
from jax import lax
from jax.experimental import pallas as pl
from jax.experimental.pallas import tpu as pltpu
from jax.sharding import PartitionSpec as P

F32 = jnp.float32
BF16 = jnp.bfloat16
LOG2E = 1.4426950408889634
NT = (((1,), (1,)), ((), ()))
PARTS = (256, 128, 128)
GROUP = 2


def call(kernel, name, flops, exps, nbytes, vmem=12, **kw):
    return pl.pallas_call(
        kernel,
        name=name,
        cost_estimate=pl.CostEstimate(flops=flops, bytes_accessed=nbytes, transcendentals=exps),
        compiler_params=pltpu.CompilerParams(vmem_limit_bytes=vmem * 2**20),
        **kw,
    )


def in_hbm(array):
    return pltpu.with_memory_space_constraint(array, pltpu.HBM)


def dot(a, b):
    return jnp.dot(a, b, preferred_element_type=F32)


def dot_nt(a, b):
    return lax.dot_general(a, b, NT, preferred_element_type=F32)


def half_exponents(block):
    sharpness = math.sqrt(block.shape[-1] / 8.0)
    wide = block.astype(F32)
    norms = jnp.sum(wide * wide, axis=-1, keepdims=True)
    return LOG2E * (sharpness * (1.0 - norms) - 0.25)


def as_row(column):
    rows = column.shape[0]
    return jnp.transpose(jnp.broadcast_to(column, (rows, 128)))[0:1, :]


def kappa_of(inner, width, left_half, right_half_row):
    scale = LOG2E * 2.0 * math.sqrt(width / 8.0)
    return jnp.exp2(inner * scale + left_half + right_half_row)


def kappa(left, right, left_half, right_half_row):
    return kappa_of(dot_nt(left, right), left.shape[-1], left_half, right_half_row)


def one_hot(chosen_row, pool):
    rank = chosen_row.shape[1]
    spread = jnp.transpose(jnp.broadcast_to(chosen_row, (128, rank)).astype(F32)).astype(jnp.int32)
    lanes = lax.broadcasted_iota(jnp.int32, (rank, 128), 1)
    pieces = [
        jnp.where(spread == lanes + 128 * j, 1.0, 0.0).astype(BF16) for j in range(pool // 128)
    ]
    return jnp.concatenate(pieces, axis=1)


def score_pieces(rows, classes, width):
    pieces = []
    for column in range(0, rows, width):
        row = rows + column * classes // width
        if rows - column >= width:
            pieces.append((column, width, 0, classes, row, 0))
        else:
            half = classes // 2
            pieces.append((column, width // 2, 0, half, row, 0))
            pieces.append((column, width // 2, half, half, row, width // 2))
    return pieces


def pack_kernel(leaf_size, first, rows, chosen, points_ref, weights_ref, out_ref, sems):
    classes = weights_ref.shape[0]
    pieces = score_pieces(rows, classes, points_ref.shape[1])
    group = lax.axis_index("grp") * out_ref.shape[0]

    def copies(j):
        start = pl.multiple_of(chosen[group + j] * leaf_size + first, 128)
        made = [
            pltpu.make_async_copy(
                points_ref.at[pl.ds(start, rows), :],
                out_ref.at[j, pl.ds(0, rows), :],
                sems.at[j, 0],
            )
        ]
        for number, (column, columns, from_class, count, row, lane) in enumerate(pieces):
            made.append(
                pltpu.make_async_copy(
                    weights_ref.at[
                        pl.ds(from_class, count),
                        pl.ds(pl.multiple_of(start + column, 128), columns),
                    ],
                    out_ref.at[j, pl.ds(row, count), pl.ds(lane, columns)],
                    sems.at[j, 1 + number],
                )
            )
        return made

    def start(j, carry):
        @pl.when(chosen[group + j] >= 0)
        def _():
            for copy in copies(j):
                copy.start()

        return carry

    def finish(j, carry):
        @pl.when(chosen[group + j] >= 0)
        def _():
            for copy in copies(j):
                copy.wait()

        return carry

    lax.fori_loop(0, out_ref.shape[0], start, 0)
    lax.fori_loop(0, out_ref.shape[0], finish, 0)


def pack(chosen, points, weights, leaf_size, first, rows):
    classes, width = weights.shape[0], points.shape[1]
    shape = (lax.axis_size("sub"), rows + rows * classes // width, width)
    return call(
        functools.partial(pack_kernel, leaf_size, first, rows),
        "pack",
        0,
        0,
        2 * math.prod(shape) * 2,
        out_shape=pltpu.HBM(shape, BF16),
        grid_spec=pltpu.PrefetchScalarGridSpec(
            num_scalar_prefetch=1,
            grid=(1,),
            in_specs=[
                pl.BlockSpec(points.shape, lambda i, c: (0, 0)),
                pl.BlockSpec(weights.shape, lambda i, c: (0, 0)),
            ],
            out_specs=pl.BlockSpec(memory_space=pltpu.HBM),
            scratch_shapes=[
                pltpu.SemaphoreType.DMA((shape[0], 1 + len(score_pieces(rows, classes, width))))
            ],
        ),
    )(chosen, in_hbm(points), in_hbm(weights))


def leaf_kernel(
    points_ref,
    weights_ref,
    chosen_ref,
    own_ref,
    skel_ref,
    up_ref,
    summary_ref,
    target_ref,
    half_ref,
):
    leaf = pl.program_id(0)
    block = points_ref[...]
    turned = jnp.transpose(block)
    target_ref[0] = turned
    leaf_size = block.shape[0]
    inverse_leaf = 1.0 / math.sqrt(leaf_size)
    half = half_exponents(block)
    half_row = as_row(half)
    half_ref[0] = half_row
    tile = kappa_of(dot(block, turned), block.shape[1], half, half_row)
    rows = lax.broadcasted_iota(jnp.int32, tile.shape, 0)
    columns = lax.broadcasted_iota(jnp.int32, tile.shape, 1)
    tile = jnp.where(rows == columns, 0.0, tile).astype(BF16)
    own = dot(weights_ref[...], tile) * inverse_leaf
    own_ref[...] = own
    chosen = chosen_ref[pl.ds(leaf, 1), :]
    rank = chosen.shape[1]
    skel_ref[0] = dot(one_hot(chosen, leaf_size), block).astype(BF16)
    places = lax.broadcasted_iota(jnp.int32, (leaf_size, rank), 0)
    columns_of = jnp.where(places == chosen, 1.0, 0.0).astype(BF16)
    up_ref[0] = dot(tile, columns_of).astype(BF16)
    summary_ref[0] = dot(own.astype(BF16), columns_of).astype(BF16)


def leaf_level(points, weights, skel_leaf):
    leaves, rank = skel_leaf.shape
    classes = weights.shape[0]
    width = points.shape[1]
    size = points.shape[0] // leaves
    return call(
        leaf_kernel,
        "leaf",
        leaves * 2 * size * (size * (width + classes + rank) + rank * width + classes * rank),
        leaves * size * size,
        8 * 2**20,
        out_shape=(
            pltpu.HBM(weights.shape, F32),
            jax.ShapeDtypeStruct((leaves, rank, width), BF16),
            pltpu.HBM((leaves, size, rank), BF16),
            jax.ShapeDtypeStruct((leaves, classes, rank), BF16),
            pltpu.HBM((leaves, width, size), BF16),
            pltpu.HBM((leaves, 1, size), F32),
        ),
        grid=(leaves,),
        in_specs=[
            pl.BlockSpec((size, width), lambda i: (i, 0)),
            pl.BlockSpec((classes, size), lambda i: (0, i)),
            pl.BlockSpec((leaves, rank), lambda i: (0, 0)),
        ],
        out_specs=(
            pl.BlockSpec((classes, size), lambda i: (0, i)),
            pl.BlockSpec((1, rank, width), lambda i: (i, 0, 0)),
            pl.BlockSpec((1, size, rank), lambda i: (i, 0, 0)),
            pl.BlockSpec((1, classes, rank), lambda i: (i, 0, 0)),
            pl.BlockSpec((1, width, size), lambda i: (i, 0, 0)),
            pl.BlockSpec((1, 1, size), lambda i: (i, 0, 0)),
        ),
    )(points, weights, skel_leaf)


def subtree_kernel(count, inner, states, rows, *refs):
    chosen_ref = refs[0]
    inputs = refs[1 : len(refs) - 5]
    lifted_ref, terms_ref, state_ref, nodes, sums = refs[len(refs) - 5 :]
    _, rank, width = nodes.shape
    classes = sums.shape[1]
    inverse_rank = 1.0 / rank
    inverse_pair = 1.0 / (math.sqrt(2.0) * rank)
    if states == 0:
        nodes[pl.ds(0, count)] = inputs[0][...]
        sums[pl.ds(0, count)] = inputs[1][...]
    else:
        for mask in range(count):
            place = lax.bitwise_xor(rows[inner], mask)
            nodes[place] = inputs[mask][pl.ds(0, rank), :]
            sums[place] = inputs[mask][pl.ds(rank, classes), :]

    def pair(i, even, odd, even_half, odd_half):
        tile = kappa(even, odd, even_half, as_row(odd_half)).astype(BF16)
        terms_ref[2 * i] = dot_nt(sums[2 * i + 1], tile) * inverse_rank
        terms_ref[2 * i + 1] = dot(sums[2 * i], tile) * inverse_rank

    def step(i, carry):
        even, odd = nodes[2 * i], nodes[2 * i + 1]
        child = jnp.concatenate([even, odd], axis=0)
        chosen = chosen_ref[pl.ds(rows[i], 1), :]
        half = half_exponents(child)
        parent = dot(one_hot(chosen, 2 * rank), child).astype(BF16)
        lifted = kappa(child, parent, half, as_row(half_exponents(parent)))
        same = lax.broadcasted_iota(jnp.int32, lifted.shape, 0) == chosen
        lifted = jnp.where(same, 0.0, lifted).astype(BF16)
        lifted_ref[i] = lifted
        summed = dot(sums[2 * i], lifted[:rank]) + dot(sums[2 * i + 1], lifted[rank:])
        nodes[count + i] = parent
        sums[count + i] = (summed * inverse_pair).astype(BF16)
        pair(i, even, odd, half[:rank], half[rank:])
        return carry

    if count > 4:
        lax.fori_loop(0, inner, step, 0)
    else:
        for i in range(inner):
            step(i, 0)
    if inner == count - 1:
        state_ref[pl.ds(0, rank), :] = nodes[count + inner - 1]
        state_ref[pl.ds(rank, classes), :] = sums[count + inner - 1]
    else:
        even, odd = nodes[2 * inner], nodes[2 * inner + 1]
        pair(inner, even, odd, half_exponents(even), half_exponents(odd))
        state_ref[...] = jnp.zeros_like(state_ref)


def subtree(name, count, inner, states, rows, table, inputs, classes):
    rank = table.shape[1]
    width = inputs[0].shape[-1]

    def whole(array):
        zeros = (0,) * len(array.shape)
        return pl.BlockSpec(array.shape, lambda i, r: zeros)

    shapes = (
        pltpu.HBM((inner, 2 * rank, rank), BF16),
        pltpu.HBM((2 * count - 2, classes, rank), F32),
        jax.ShapeDtypeStruct((rank + classes, width), BF16),
    )
    return call(
        functools.partial(subtree_kernel, count, inner, states),
        name,
        inner * 2 * rank * rank * (5 * width + 4 * classes),
        inner * 3 * rank * rank,
        6 * 2**20,
        vmem=16,
        out_shape=shapes,
        grid_spec=pltpu.PrefetchScalarGridSpec(
            num_scalar_prefetch=1,
            grid=(1,),
            in_specs=[whole(table)] + [whole(array) for array in inputs],
            out_specs=tuple(whole(shape) for shape in shapes),
            scratch_shapes=[
                pltpu.VMEM((2 * count, rank, width), BF16),
                pltpu.VMEM((2 * count, classes, rank), BF16),
            ],
        ),
    )(in_hbm(rows), in_hbm(table), *inputs)


def path_of(place, count):
    numbers = [place]
    while 2 ** len(numbers) < count:
        numbers.append(count + (numbers[-1] >> 1))
    return numbers


def place_table(steps):
    devices = 1 << sum(steps)
    table = []
    for device in range(devices):
        parts, paths, height = [], [], 0
        for number, step in enumerate(steps):
            rows = []
            for u in range(height + 1, height + step + 1):
                under = 1 << (height + step - u)
                base = devices - (devices >> u - 1) + (device >> height + step) * under
                rows += [base + i for i in range(under)]
            if number + 1 == len(steps):
                rows = rows[:-1]
            place = device >> height & (1 << step) - 1
            parts.append(rows + [place])
            paths.insert(0, path_of(place, 1 << step)[::-1])
            height += step
        parts.append([node for path in paths for node in path])
        table.append([number for part in parts for number in part])
    starts = np.cumsum([0] + [len(part) for part in parts]).tolist()
    return np.array(table, np.int32), starts, tuple(len(path) for path in paths)


def down_kernel(path, stages, numbers, *refs):
    lifted_hbm, terms_hbm, up_hbm, own_hbm, out_ref = refs[2 * stages : 2 * stages + 5]
    lifted_ref, terms_ref, up_ref, path_lifted, path_terms, values = refs[2 * stages + 5 : -3]
    path_sems, up_sems, sems = refs[-3:]
    inner, _, rank = lifted_ref.shape
    leaves, size, _ = up_ref.shape
    inverse_rank = 1.0 / rank

    path_copies = []
    for stage, steps in enumerate(path):
        for _ in range(steps):
            at = len(path_copies)
            node = numbers[at]
            copies = [
                pltpu.make_async_copy(
                    refs[2 * stage + 1].at[node], path_terms.at[at], path_sems.at[at, 0]
                )
            ]
            if at > 0:
                half = pl.ds(pl.multiple_of((node & 1) * rank, rank), rank)
                copies.append(
                    pltpu.make_async_copy(
                        refs[2 * stage].at[node >> 1, half, :],
                        path_lifted.at[at],
                        path_sems.at[at, 1],
                    )
                )
            path_copies.append(copies)
    local_copies = [
        pltpu.make_async_copy(terms_hbm, terms_ref, sems.at[0]),
        pltpu.make_async_copy(lifted_hbm, lifted_ref, sems.at[1]),
    ]
    own_copy = pltpu.make_async_copy(own_hbm, out_ref, sems.at[2])
    up_copies = [
        pltpu.make_async_copy(up_hbm.at[leaf], up_ref.at[leaf], up_sems.at[leaf])
        for leaf in range(leaves)
    ]
    for copies in path_copies:
        for copy in copies:
            copy.start()
    for copy in local_copies + [own_copy] + up_copies:
        copy.start()

    value = None
    for at, copies in enumerate(path_copies):
        for copy in copies:
            copy.wait()
        term = path_terms[at]
        if at > 0:
            term = term + dot_nt(value, path_lifted[at]) * inverse_rank
        value = term.astype(BF16)
    values[2 * leaves - 2] = value
    for copy in local_copies:
        copy.wait()

    for i in range(inner - 1, -1, -1):
        below = dot_nt(values[leaves + i], lifted_ref[i]) * inverse_rank
        values[2 * i] = (terms_ref[2 * i] + below[:, :rank]).astype(BF16)
        values[2 * i + 1] = (terms_ref[2 * i + 1] + below[:, rank:]).astype(BF16)
    own_copy.wait()
    for leaf in range(leaves):
        up_copies[leaf].wait()
        columns = pl.ds(leaf * size, size)
        out_ref[:, columns] += dot_nt(values[leaf], up_ref[leaf]) * inverse_rank


def down(numbers, path, stages, lifted, terms, up, own):
    leaves, size, rank = up.shape
    classes = own.shape[0]
    inputs = [array for stage in stages for array in stage] + [lifted, terms, up, own]
    hbm = pl.BlockSpec(memory_space=pltpu.HBM)
    return call(
        functools.partial(down_kernel, path, len(stages)),
        "down",
        2 * classes * rank * (sum(path) * rank + leaves * size * 2),
        rank * rank,
        8 * 2**20,
        vmem=24,
        out_shape=pltpu.HBM(own.shape, F32),
        in_specs=[pl.BlockSpec(memory_space=pltpu.SMEM)] + [hbm] * len(inputs),
        out_specs=pl.BlockSpec(memory_space=pltpu.VMEM),
        scratch_shapes=[
            pltpu.VMEM(lifted.shape, BF16),
            pltpu.VMEM(terms.shape, F32),
            pltpu.VMEM(up.shape, BF16),
            pltpu.VMEM((sum(path), rank, rank), BF16),
            pltpu.VMEM((sum(path), classes, rank), F32),
            pltpu.VMEM((2 * leaves, classes, rank), BF16),
            pltpu.SemaphoreType.DMA((sum(path), 2)),
            pltpu.SemaphoreType.DMA((leaves,)),
            pltpu.SemaphoreType.DMA((3,)),
        ],
    )(in_hbm(numbers), *(in_hbm(array) for array in inputs))


def near_kernel(
    rows, group, resident, slots, halves_ref, targets_hbm, start_hbm, block_hbm, out_ref, *refs
):
    order, leaf_state, block_state, targets_ref = refs[:4]
    leaf_sems, block_sems, start_sem = refs[-3:]
    block_ref = block_hbm if resident else refs[4]
    leaves, width, size = targets_ref.shape
    sources = block_hbm.shape[0]
    classes = out_ref.shape[0]
    inverse_leaf = 1.0 / math.sqrt(size)

    def target_copy(leaf):
        return pltpu.make_async_copy(
            targets_hbm.at[leaf], targets_ref.at[leaf], leaf_sems.at[leaf]
        )

    def block_copy(source):
        return pltpu.make_async_copy(
            block_hbm.at[source], block_ref.at[source], block_sems.at[source]
        )

    def clear(source, carry):
        block_state[source] = 0
        return carry

    def list_leaf(number, filled):
        target_copy(number).start()
        leaf_state[number] = 1

        def list_slot(slot, carry):
            source = lax.rem(slots[number, slot] // leaves, sources)
            place = filled + (slot - 1) // 2

            @pl.when(lax.rem(slot, 2) == 1)
            def _():
                order[place, 0] = number
                order[place, 1] = source
                order[place, 2] = source
                order[place, 3] = 0

            @pl.when(lax.rem(slot, 2) == 0)
            def _():
                order[place, 2] = source
                order[place, 3] = 1

            if not resident:

                @pl.when(block_state[source] == 0)
                def _():
                    block_state[source] = 1
                    block_copy(source).start()

            return carry

        live = slots[number, slots.shape[1] - 1]
        lax.fori_loop(1, live, list_slot, 0)
        return filled + live // 2

    def repeat_last(number, carry):
        for field in range(4):
            order[number, field] = order[count - 1, field]
        return carry

    if not resident:
        lax.fori_loop(0, sources, clear, 0)
    start_copy = pltpu.make_async_copy(start_hbm, out_ref, start_sem)
    start_copy.start()
    count = lax.fori_loop(0, leaves, list_leaf, 0)
    steps = (count + group - 1) // group
    lax.fori_loop(count, steps * group, repeat_last, 0)
    start_copy.wait()

    def arrive(number):
        leaf = order[number, 0]

        @pl.when(leaf_state[leaf] == 1)
        def _():
            leaf_state[leaf] = 2
            target_copy(leaf).wait()

        for field in (1, 2) if not resident else ():
            source = order[number, field]

            @pl.when(block_state[source] == 1)
            def _():
                block_state[source] = 2
                block_copy(source).wait()

    def scores_of(source):
        found = []
        for column in range(0, rows, width):
            columns = min(width, rows - column)
            place = pl.ds(rows + column * classes // width, classes * columns // width)
            weights = block_ref[source, place, :]
            if columns < width:
                weights = jnp.concatenate(
                    [weights[:, : width // 2], weights[:, width // 2 :]], axis=0
                )
            found.append(weights)
        return found

    def contribution(number):
        leaf, one, two = order[number, 0], order[number, 1], order[number, 2]
        block = jnp.concatenate(
            [block_ref[one, pl.ds(0, rows), :], block_ref[two, pl.ds(0, rows), :]], axis=0
        )
        inner = dot(block, targets_ref[leaf])
        tile = kappa_of(inner, width, half_exponents(block), halves_ref[leaf]).astype(BF16)
        second = order[number, 3].astype(F32)
        scores = scores_of(one)
        scores += [(part.astype(F32) * second).astype(BF16) for part in scores_of(two)]
        added = dot(jnp.concatenate(scores, axis=1), tile)
        return added * jnp.where(number < count, inverse_leaf, 0.0)

    def step(first, carry):
        numbers = [first * group + k for k in range(group)]
        for number in numbers:
            arrive(number)
        added = [contribution(number) for number in numbers]
        for number, term in zip(numbers, added):
            columns = pl.ds(pl.multiple_of(order[number, 0] * size, size), size)
            out_ref[:, columns] += term
        return carry

    lax.fori_loop(0, steps, step, 0)


def near_part(rows, group, slots, targets, halves, start, blocks, resident, out_type):
    classes, columns = start.shape
    leaves, width, size = targets.shape
    tiles = 24
    whole = pl.BlockSpec(memory_space=pltpu.VMEM)
    hbm = pl.BlockSpec(memory_space=pltpu.HBM)
    scratch = [
        pltpu.SMEM((slots.size // 2 + group, 4), jnp.int32),
        pltpu.SMEM((leaves,), jnp.int32),
        pltpu.SMEM((blocks.shape[0],), jnp.int32),
        pltpu.VMEM(targets.shape, BF16),
    ]
    if not resident:
        scratch.append(pltpu.VMEM(blocks.shape, BF16))
    scratch += [
        pltpu.SemaphoreType.DMA((leaves,)),
        pltpu.SemaphoreType.DMA((blocks.shape[0],)),
        pltpu.SemaphoreType.DMA,
    ]
    return call(
        functools.partial(near_kernel, rows, group, resident),
        "near",
        tiles * 2 * rows * size * (width + classes),
        tiles * rows * size,
        tiles * rows * width * 2 + 4 * 2**20,
        vmem=24,
        out_shape=out_type(start.shape, F32),
        in_specs=[
            pl.BlockSpec(memory_space=pltpu.SMEM),
            whole,
            hbm,
            hbm,
            whole if resident else hbm,
        ],
        out_specs=whole,
        scratch_shapes=scratch,
    )(
        in_hbm(slots),
        in_hbm(halves),
        in_hbm(targets),
        in_hbm(start),
        blocks if resident else in_hbm(blocks),
    )


def swap(value, axis, mask):
    pairs = [(source, source ^ mask) for source in range(lax.axis_size(axis))]
    return lax.ppermute(value, axis, pairs)


def per_device(points, weights, near, counts, skel_leaf, skel_local, skel_upper):
    leaves, rank = skel_leaf.shape
    size = points.shape[0] // leaves
    classes = weights.shape[0]
    slots = near.shape[1]
    sub_count = lax.axis_size("sub")
    grp_count = lax.axis_size("grp")
    sub_index = lax.axis_index("sub")
    grp_index = lax.axis_index("grp")
    device = grp_index * sub_count + sub_index

    slot_ids = jnp.arange(slots)
    owned = (
        (near // leaves == device)
        & (slot_ids[None, :] < counts[:, None])
        & (slot_ids[None, :] > 0)
    )
    chosen = jnp.where(owned, near - device * leaves, -1)
    chosen = jnp.max(chosen.reshape(sub_count * grp_count, leaves * slots), axis=1)

    def send(block):
        return lax.all_to_all(block, "sub", split_axis=0, concat_axis=0, tiled=True)

    arrived = [send(pack(chosen, points, weights, size, 0, PARTS[0]))]

    sub_bits = sub_count.bit_length() - 1
    far_bits = (sub_bits - 1) // 2
    steps = [1, sub_bits - 1 - far_bits, far_bits, grp_count.bit_length() - 1]
    table, starts, path_lengths = place_table(steps)
    mine = lax.dynamic_slice_in_dim(jnp.asarray(table), device, 1, 0)[0]
    *stage_rows, path_nodes = (mine[low:high] for low, high in zip(starts[:-1], starts[1:]))
    near_slots = jnp.concatenate(
        [
            lax.dynamic_slice_in_dim(near, device * leaves, leaves, 0),
            lax.dynamic_slice_in_dim(counts, device * leaves, leaves, 0)[:, None],
        ],
        axis=1,
    )

    own, skel, up, summary, targets, halves = leaf_level(points, weights, skel_leaf)
    lifted, terms, state = subtree(
        "local",
        leaves,
        leaves - 1,
        0,
        jnp.arange(leaves, dtype=jnp.int32),
        skel_local,
        (skel, summary),
        classes,
    )
    state, near_slots, stage_rows, path_nodes = lax.optimization_barrier(
        (state, near_slots, stage_rows, path_nodes)
    )

    def exchange(state, stage):
        axis = "grp" if stage + 1 == len(steps) else "sub"
        low = 0 if axis == "grp" else sum(steps[:stage])
        return [state] + [swap(state, axis, mask << low) for mask in range(1, 1 << steps[stage])]

    def climb(name, states, stage, rows):
        count = 1 << steps[stage]
        inner = count - 2 if stage + 1 == len(steps) else count - 1
        *done, state = subtree(name, count, inner, 2, rows, skel_upper, states, classes)
        return done, state

    core_stage, state = climb("core_nodes", exchange(state, 0), 0, stage_rows[0])
    x_states = exchange(state, 1)
    sent = [
        pack(chosen, points, weights, size, sum(PARTS[:part]), PARTS[part]) for part in (1, 2)
    ]
    sent, x_rows, x_states = lax.optimization_barrier((sent, stage_rows[1], x_states))
    arrived.append(send(sent[0]))
    x_stage, state = climb("x_nodes", x_states, 1, x_rows)
    y_states = exchange(state, 2)

    def near_sum(part, slots, start, out_type=pltpu.HBM):
        return near_part(
            PARTS[part], GROUP, slots, targets, halves, start, arrived[part], part == 2, out_type
        )

    near_slots, _ = lax.optimization_barrier((near_slots, state))
    total = near_sum(0, near_slots, own)
    sent_last, _, _ = lax.optimization_barrier((sent[1], y_states, total))
    arrived.append(send(sent_last))
    y_stage, state = climb("y_nodes", y_states, 2, stage_rows[2])
    z_states = exchange(state, 3)
    near_slots, _ = lax.optimization_barrier((near_slots, state))
    total = near_sum(1, near_slots, total)
    z_rows, total = lax.optimization_barrier((stage_rows[3], total))
    z_stage, _ = climb("z_nodes", z_states, 3, z_rows)
    stages = [z_stage, y_stage, x_stage, core_stage]
    total = down(path_nodes, path_lengths, stages, lifted, terms, up, total)
    return near_sum(2, near_slots, total, jax.ShapeDtypeStruct)


def solution(mesh):
    split = P(("grp", "sub"), None)
    columns = P(None, ("grp", "sub"))
    return jax.shard_map(
        per_device,
        mesh=mesh,
        in_specs=(split, columns, P(), P(), split, split, P()),
        out_specs=columns,
        check_vma=False,
    )
```

```python
import functools
import math

import jax
import jax.numpy as jnp
import numpy as np
from jax import lax
from jax.experimental import pallas as pl
from jax.experimental.pallas import tpu as pltpu
from jax.sharding import PartitionSpec as P

F32 = jnp.float32
BF16 = jnp.bfloat16
LOG2E = 1.4426950408889634
NT = (((1,), (1,)), ((), ()))
PARTS = (256, 128, 128)
GROUP = 2


def call(kernel, name, flops, exps, nbytes, vmem=12, **kw):
    return pl.pallas_call(
        kernel,
        name=name,
        cost_estimate=pl.CostEstimate(flops=flops, bytes_accessed=nbytes, transcendentals=exps),
        compiler_params=pltpu.CompilerParams(vmem_limit_bytes=vmem * 2**20),
        **kw,
    )


def in_hbm(array):
    return pltpu.with_memory_space_constraint(array, pltpu.HBM)


def dot(a, b):
    return jnp.dot(a, b, preferred_element_type=F32)


def dot_nt(a, b):
    return lax.dot_general(a, b, NT, preferred_element_type=F32)


def half_exponents(block):
    sharpness = math.sqrt(block.shape[-1] / 8.0)
    wide = block.astype(F32)
    norms = jnp.sum(wide * wide, axis=-1, keepdims=True)
    return LOG2E * (sharpness * (1.0 - norms) - 0.25)


def as_row(column):
    rows = column.shape[0]
    return jnp.transpose(jnp.broadcast_to(column, (rows, 128)))[0:1, :]


def kappa_of(inner, width, left_half, right_half_row):
    scale = LOG2E * 2.0 * math.sqrt(width / 8.0)
    return jnp.exp2(inner * scale + left_half + right_half_row)


def kappa(left, right, left_half, right_half_row):
    return kappa_of(dot_nt(left, right), left.shape[-1], left_half, right_half_row)


def one_hot(chosen_row, pool):
    rank = chosen_row.shape[1]
    spread = jnp.transpose(jnp.broadcast_to(chosen_row, (128, rank)).astype(F32)).astype(jnp.int32)
    lanes = lax.broadcasted_iota(jnp.int32, (rank, 128), 1)
    pieces = [
        jnp.where(spread == lanes + 128 * j, 1.0, 0.0).astype(BF16) for j in range(pool // 128)
    ]
    return jnp.concatenate(pieces, axis=1)


def score_pieces(rows, classes, width):
    pieces = []
    for column in range(0, rows, width):
        row = rows + column * classes // width
        if rows - column >= width:
            pieces.append((column, width, 0, classes, row, 0))
        else:
            half = classes // 2
            pieces.append((column, width // 2, 0, half, row, 0))
            pieces.append((column, width // 2, half, half, row, width // 2))
    return pieces


def pack_kernel(leaf_size, first, rows, chosen, points_ref, weights_ref, out_ref, sems):
    classes = weights_ref.shape[0]
    pieces = score_pieces(rows, classes, points_ref.shape[1])
    group = lax.axis_index("grp") * out_ref.shape[0]

    def copies(j):
        start = pl.multiple_of(chosen[group + j] * leaf_size + first, 128)
        made = [
            pltpu.make_async_copy(
                points_ref.at[pl.ds(start, rows), :],
                out_ref.at[j, pl.ds(0, rows), :],
                sems.at[j, 0],
            )
        ]
        for number, (column, columns, from_class, count, row, lane) in enumerate(pieces):
            made.append(
                pltpu.make_async_copy(
                    weights_ref.at[
                        pl.ds(from_class, count),
                        pl.ds(pl.multiple_of(start + column, 128), columns),
                    ],
                    out_ref.at[j, pl.ds(row, count), pl.ds(lane, columns)],
                    sems.at[j, 1 + number],
                )
            )
        return made

    def start(j, carry):
        @pl.when(chosen[group + j] >= 0)
        def _():
            for copy in copies(j):
                copy.start()

        return carry

    def finish(j, carry):
        @pl.when(chosen[group + j] >= 0)
        def _():
            for copy in copies(j):
                copy.wait()

        return carry

    lax.fori_loop(0, out_ref.shape[0], start, 0)
    lax.fori_loop(0, out_ref.shape[0], finish, 0)


def pack(chosen, points, weights, leaf_size, first, rows):
    classes, width = weights.shape[0], points.shape[1]
    shape = (lax.axis_size("sub"), rows + rows * classes // width, width)
    return call(
        functools.partial(pack_kernel, leaf_size, first, rows),
        "pack",
        0,
        0,
        2 * math.prod(shape) * 2,
        out_shape=pltpu.HBM(shape, BF16),
        grid_spec=pltpu.PrefetchScalarGridSpec(
            num_scalar_prefetch=1,
            grid=(1,),
            in_specs=[
                pl.BlockSpec(points.shape, lambda i, c: (0, 0)),
                pl.BlockSpec(weights.shape, lambda i, c: (0, 0)),
            ],
            out_specs=pl.BlockSpec(memory_space=pltpu.HBM),
            scratch_shapes=[
                pltpu.SemaphoreType.DMA((shape[0], 1 + len(score_pieces(rows, classes, width))))
            ],
        ),
    )(chosen, in_hbm(points), in_hbm(weights))


def leaf_kernel(
    points_ref,
    weights_ref,
    chosen_ref,
    own_ref,
    skel_ref,
    up_ref,
    summary_ref,
    target_ref,
    half_ref,
):
    leaf = pl.program_id(0)
    block = points_ref[...]
    turned = jnp.transpose(block)
    target_ref[0] = turned
    leaf_size = block.shape[0]
    inverse_leaf = 1.0 / math.sqrt(leaf_size)
    half = half_exponents(block)
    half_row = as_row(half)
    half_ref[0] = half_row
    tile = kappa_of(dot(block, turned), block.shape[1], half, half_row)
    rows = lax.broadcasted_iota(jnp.int32, tile.shape, 0)
    columns = lax.broadcasted_iota(jnp.int32, tile.shape, 1)
    tile = jnp.where(rows == columns, 0.0, tile).astype(BF16)
    own = dot(weights_ref[...], tile) * inverse_leaf
    own_ref[...] = own
    chosen = chosen_ref[pl.ds(leaf, 1), :]
    rank = chosen.shape[1]
    skel_ref[0] = dot(one_hot(chosen, leaf_size), block).astype(BF16)
    places = lax.broadcasted_iota(jnp.int32, (leaf_size, rank), 0)
    columns_of = jnp.where(places == chosen, 1.0, 0.0).astype(BF16)
    up_ref[0] = dot(tile, columns_of).astype(BF16)
    summary_ref[0] = dot(own.astype(BF16), columns_of).astype(BF16)


def leaf_level(points, weights, skel_leaf):
    leaves, rank = skel_leaf.shape
    classes = weights.shape[0]
    width = points.shape[1]
    size = points.shape[0] // leaves
    return call(
        leaf_kernel,
        "leaf",
        leaves * 2 * size * (size * (width + classes + rank) + rank * width + classes * rank),
        leaves * size * size,
        8 * 2**20,
        out_shape=(
            pltpu.HBM(weights.shape, F32),
            jax.ShapeDtypeStruct((leaves, rank, width), BF16),
            pltpu.HBM((leaves, size, rank), BF16),
            jax.ShapeDtypeStruct((leaves, classes, rank), BF16),
            pltpu.HBM((leaves, width, size), BF16),
            pltpu.HBM((leaves, 1, size), F32),
        ),
        grid=(leaves,),
        in_specs=[
            pl.BlockSpec((size, width), lambda i: (i, 0)),
            pl.BlockSpec((classes, size), lambda i: (0, i)),
            pl.BlockSpec((leaves, rank), lambda i: (0, 0)),
        ],
        out_specs=(
            pl.BlockSpec((classes, size), lambda i: (0, i)),
            pl.BlockSpec((1, rank, width), lambda i: (i, 0, 0)),
            pl.BlockSpec((1, size, rank), lambda i: (i, 0, 0)),
            pl.BlockSpec((1, classes, rank), lambda i: (i, 0, 0)),
            pl.BlockSpec((1, width, size), lambda i: (i, 0, 0)),
            pl.BlockSpec((1, 1, size), lambda i: (i, 0, 0)),
        ),
    )(points, weights, skel_leaf)


def subtree_kernel(count, inner, states, rows, *refs):
    chosen_ref = refs[0]
    inputs = refs[1 : len(refs) - 5]
    lifted_ref, terms_ref, state_ref, nodes, sums = refs[len(refs) - 5 :]
    _, rank, width = nodes.shape
    classes = sums.shape[1]
    inverse_rank = 1.0 / rank
    inverse_pair = 1.0 / (math.sqrt(2.0) * rank)
    if states == 0:
        nodes[pl.ds(0, count)] = inputs[0][...]
        sums[pl.ds(0, count)] = inputs[1][...]
    else:
        for mask in range(count):
            place = lax.bitwise_xor(rows[inner], mask)
            nodes[place] = inputs[mask][pl.ds(0, rank), :]
            sums[place] = inputs[mask][pl.ds(rank, classes), :]

    def pair(i, even, odd, even_half, odd_half):
        tile = kappa(even, odd, even_half, as_row(odd_half)).astype(BF16)
        terms_ref[2 * i] = dot_nt(sums[2 * i + 1], tile) * inverse_rank
        terms_ref[2 * i + 1] = dot(sums[2 * i], tile) * inverse_rank

    def step(i, carry):
        even, odd = nodes[2 * i], nodes[2 * i + 1]
        child = jnp.concatenate([even, odd], axis=0)
        chosen = chosen_ref[pl.ds(rows[i], 1), :]
        half = half_exponents(child)
        parent = dot(one_hot(chosen, 2 * rank), child).astype(BF16)
        lifted = kappa(child, parent, half, as_row(half_exponents(parent)))
        same = lax.broadcasted_iota(jnp.int32, lifted.shape, 0) == chosen
        lifted = jnp.where(same, 0.0, lifted).astype(BF16)
        lifted_ref[i] = lifted
        summed = dot(sums[2 * i], lifted[:rank]) + dot(sums[2 * i + 1], lifted[rank:])
        nodes[count + i] = parent
        sums[count + i] = (summed * inverse_pair).astype(BF16)
        pair(i, even, odd, half[:rank], half[rank:])
        return carry

    if count > 4:
        lax.fori_loop(0, inner, step, 0)
    else:
        for i in range(inner):
            step(i, 0)
    if inner == count - 1:
        state_ref[pl.ds(0, rank), :] = nodes[count + inner - 1]
        state_ref[pl.ds(rank, classes), :] = sums[count + inner - 1]
    else:
        even, odd = nodes[2 * inner], nodes[2 * inner + 1]
        pair(inner, even, odd, half_exponents(even), half_exponents(odd))
        state_ref[...] = jnp.zeros_like(state_ref)


def subtree(name, count, inner, states, rows, table, inputs, classes):
    rank = table.shape[1]
    width = inputs[0].shape[-1]

    def whole(array):
        zeros = (0,) * len(array.shape)
        return pl.BlockSpec(array.shape, lambda i, r: zeros)

    shapes = (
        pltpu.HBM((inner, 2 * rank, rank), BF16),
        pltpu.HBM((2 * count - 2, classes, rank), F32),
        jax.ShapeDtypeStruct((rank + classes, width), BF16),
    )
    return call(
        functools.partial(subtree_kernel, count, inner, states),
        name,
        inner * 2 * rank * rank * (5 * width + 4 * classes),
        inner * 3 * rank * rank,
        6 * 2**20,
        vmem=16,
        out_shape=shapes,
        grid_spec=pltpu.PrefetchScalarGridSpec(
            num_scalar_prefetch=1,
            grid=(1,),
            in_specs=[whole(table)] + [whole(array) for array in inputs],
            out_specs=tuple(whole(shape) for shape in shapes),
            scratch_shapes=[
                pltpu.VMEM((2 * count, rank, width), BF16),
                pltpu.VMEM((2 * count, classes, rank), BF16),
            ],
        ),
    )(in_hbm(rows), in_hbm(table), *inputs)


def path_of(place, count):
    numbers = [place]
    while 2 ** len(numbers) < count:
        numbers.append(count + (numbers[-1] >> 1))
    return numbers


def place_table(steps):
    devices = 1 << sum(steps)
    table = []
    for device in range(devices):
        parts, paths, height = [], [], 0
        for number, step in enumerate(steps):
            rows = []
            for u in range(height + 1, height + step + 1):
                under = 1 << (height + step - u)
                base = devices - (devices >> u - 1) + (device >> height + step) * under
                rows += [base + i for i in range(under)]
            if number + 1 == len(steps):
                rows = rows[:-1]
            place = device >> height & (1 << step) - 1
            parts.append(rows + [place])
            paths.insert(0, path_of(place, 1 << step)[::-1])
            height += step
        parts.append([node for path in paths for node in path])
        table.append([number for part in parts for number in part])
    starts = np.cumsum([0] + [len(part) for part in parts]).tolist()
    return np.array(table, np.int32), starts, tuple(len(path) for path in paths)


def down_kernel(path, top_inner, top_rows, numbers, chosen_ref, *refs):
    top_count = top_inner + 2
    top_states = refs[:top_count]
    stages = refs[top_count : top_count + 2 * (len(path) - 1)]
    lifted_hbm, terms_hbm, up_hbm, own_hbm, out_ref = refs[top_count + len(stages) :][:5]
    lifted_ref, terms_ref, up_ref, path_lifted, path_terms, values = refs[-14:-8]
    top_lifted, top_terms, top_state, nodes, sums = refs[-8:-3]
    path_sems, up_sems, sems = refs[-3:]
    inner, _, rank = lifted_ref.shape
    leaves, size, _ = up_ref.shape
    inverse_rank = 1.0 / rank

    def child_rows(node):
        return pl.ds(pl.multiple_of((node & 1) * rank, rank), rank)

    path_copies = []
    at = path[0]
    for stage, steps in enumerate(path[1:]):
        for _ in range(steps):
            node = numbers[at]
            path_copies.append(
                [
                    pltpu.make_async_copy(
                        stages[2 * stage + 1].at[node], path_terms.at[at], path_sems.at[at, 0]
                    ),
                    pltpu.make_async_copy(
                        stages[2 * stage].at[node >> 1, child_rows(node), :],
                        path_lifted.at[at],
                        path_sems.at[at, 1],
                    ),
                ]
            )
            at += 1
    local_copies = [
        pltpu.make_async_copy(terms_hbm, terms_ref, sems.at[0]),
        pltpu.make_async_copy(lifted_hbm, lifted_ref, sems.at[1]),
    ]
    own_copy = pltpu.make_async_copy(own_hbm, out_ref, sems.at[2])
    up_copies = [
        pltpu.make_async_copy(up_hbm.at[leaf], up_ref.at[leaf], up_sems.at[leaf])
        for leaf in range(leaves)
    ]
    for copies in path_copies:
        for copy in copies:
            copy.start()
    for copy in local_copies + [own_copy] + up_copies:
        copy.start()

    subtree_kernel(
        top_count,
        top_inner,
        2,
        top_rows,
        chosen_ref,
        *top_states,
        top_lifted,
        top_terms,
        top_state,
        nodes,
        sums,
    )
    value = top_terms[numbers[0]].astype(BF16)
    for at in range(1, path[0]):
        node = numbers[at]
        child = top_lifted[node >> 1, child_rows(node), :]
        value = (top_terms[node] + dot_nt(value, child) * inverse_rank).astype(BF16)
    for at, copies in enumerate(path_copies, path[0]):
        for copy in copies:
            copy.wait()
        term = path_terms[at] + dot_nt(value, path_lifted[at]) * inverse_rank
        value = term.astype(BF16)
    values[2 * leaves - 2] = value
    for copy in local_copies:
        copy.wait()

    for i in range(inner - 1, -1, -1):
        below = dot_nt(values[leaves + i], lifted_ref[i]) * inverse_rank
        values[2 * i] = (terms_ref[2 * i] + below[:, :rank]).astype(BF16)
        values[2 * i + 1] = (terms_ref[2 * i + 1] + below[:, rank:]).astype(BF16)
    own_copy.wait()
    for leaf in range(leaves):
        up_copies[leaf].wait()
        columns = pl.ds(leaf * size, size)
        out_ref[:, columns] += dot_nt(values[leaf], up_ref[leaf]) * inverse_rank


def down(top_rows, numbers, table, path, top_states, stages, lifted, terms, up, own):
    leaves, size, rank = up.shape
    classes = own.shape[0]
    width = table.shape[1]
    count = len(top_states)
    inputs = [array for stage in stages for array in stage] + [lifted, terms, up, own]
    hbm = pl.BlockSpec(memory_space=pltpu.HBM)
    vmem = pl.BlockSpec(memory_space=pltpu.VMEM)
    smem = pl.BlockSpec(memory_space=pltpu.SMEM)
    state_width = top_states[0].shape[1]
    return call(
        functools.partial(down_kernel, path, count - 2),
        "down",
        2 * classes * rank * (sum(path) * rank + leaves * size * 2)
        + (count - 2) * 2 * rank * rank * (5 * width + 4 * classes),
        rank * rank * 6,
        8 * 2**20,
        vmem=24,
        out_shape=pltpu.HBM(own.shape, F32),
        in_specs=[smem, smem, vmem] + [vmem] * count + [hbm] * len(inputs),
        out_specs=vmem,
        scratch_shapes=[
            pltpu.VMEM(lifted.shape, BF16),
            pltpu.VMEM(terms.shape, F32),
            pltpu.VMEM(up.shape, BF16),
            pltpu.VMEM((sum(path), rank, rank), BF16),
            pltpu.VMEM((sum(path), classes, rank), F32),
            pltpu.VMEM((2 * leaves, classes, rank), BF16),
            pltpu.VMEM((count - 2, 2 * rank, rank), BF16),
            pltpu.VMEM((2 * count - 2, classes, rank), F32),
            pltpu.VMEM(top_states[0].shape, BF16),
            pltpu.VMEM((2 * count, rank, state_width), BF16),
            pltpu.VMEM((2 * count, classes, rank), BF16),
            pltpu.SemaphoreType.DMA((sum(path), 2)),
            pltpu.SemaphoreType.DMA((leaves,)),
            pltpu.SemaphoreType.DMA((3,)),
        ],
    )(
        in_hbm(top_rows),
        in_hbm(numbers),
        in_hbm(table),
        *top_states,
        *(in_hbm(array) for array in inputs),
    )


def near_kernel(
    rows, group, resident, slots, halves_ref, targets_hbm, start_hbm, block_hbm, out_ref, *refs
):
    order, leaf_state, block_state, targets_ref = refs[:4]
    leaf_sems, block_sems, start_sems = refs[-3:]
    block_ref = block_hbm if resident else refs[4]
    leaves, width, size = targets_ref.shape
    sources = block_hbm.shape[0]
    classes = out_ref.shape[0]
    inverse_leaf = 1.0 / math.sqrt(size)

    def target_copy(leaf):
        return pltpu.make_async_copy(
            targets_hbm.at[leaf], targets_ref.at[leaf], leaf_sems.at[leaf]
        )

    def start_copy(leaf):
        columns = pl.ds(pl.multiple_of(leaf * size, size), size)
        return pltpu.make_async_copy(
            start_hbm.at[:, columns], out_ref.at[:, columns], start_sems.at[leaf]
        )

    def block_copy(source):
        return pltpu.make_async_copy(
            block_hbm.at[source], block_ref.at[source], block_sems.at[source]
        )

    def clear(source, carry):
        block_state[source] = 0
        return carry

    def list_leaf(number, filled):
        target_copy(number).start()
        start_copy(number).start()
        leaf_state[number] = 1

        def list_slot(slot, carry):
            source = lax.rem(slots[number, slot] // leaves, sources)
            place = filled + (slot - 1) // 2

            @pl.when(lax.rem(slot, 2) == 1)
            def _():
                order[place, 0] = number
                order[place, 1] = source
                order[place, 2] = source
                order[place, 3] = 0

            @pl.when(lax.rem(slot, 2) == 0)
            def _():
                order[place, 2] = source
                order[place, 3] = 1

            if not resident:

                @pl.when(block_state[source] == 0)
                def _():
                    block_state[source] = 1
                    block_copy(source).start()

            return carry

        live = slots[number, slots.shape[1] - 1]
        lax.fori_loop(1, live, list_slot, 0)
        return filled + live // 2

    def repeat_last(number, carry):
        for field in range(4):
            order[number, field] = order[count - 1, field]
        return carry

    if not resident:
        lax.fori_loop(0, sources, clear, 0)
    count = lax.fori_loop(0, leaves, list_leaf, 0)
    steps = (count + group - 1) // group
    lax.fori_loop(count, steps * group, repeat_last, 0)

    def arrive(number):
        leaf = order[number, 0]

        @pl.when(leaf_state[leaf] == 1)
        def _():
            leaf_state[leaf] = 2
            target_copy(leaf).wait()
            start_copy(leaf).wait()

        for field in (1, 2) if not resident else ():
            source = order[number, field]

            @pl.when(block_state[source] == 1)
            def _():
                block_state[source] = 2
                block_copy(source).wait()

    def scores_of(source):
        found = []
        for column in range(0, rows, width):
            columns = min(width, rows - column)
            place = pl.ds(rows + column * classes // width, classes * columns // width)
            weights = block_ref[source, place, :]
            if columns < width:
                weights = jnp.concatenate(
                    [weights[:, : width // 2], weights[:, width // 2 :]], axis=0
                )
            found.append(weights)
        return found

    def contribution(number):
        leaf, one, two = order[number, 0], order[number, 1], order[number, 2]
        block = jnp.concatenate(
            [block_ref[one, pl.ds(0, rows), :], block_ref[two, pl.ds(0, rows), :]], axis=0
        )
        inner = dot(block, targets_ref[leaf])
        tile = kappa_of(inner, width, half_exponents(block), halves_ref[leaf]).astype(BF16)
        second = order[number, 3].astype(F32)
        scores = scores_of(one)
        scores += [(part.astype(F32) * second).astype(BF16) for part in scores_of(two)]
        added = dot(jnp.concatenate(scores, axis=1), tile)
        return added * jnp.where(number < count, inverse_leaf, 0.0)

    def step(first, carry):
        numbers = [first * group + k for k in range(group)]
        for number in numbers:
            arrive(number)
        added = [contribution(number) for number in numbers]
        for number, term in zip(numbers, added):
            columns = pl.ds(pl.multiple_of(order[number, 0] * size, size), size)
            out_ref[:, columns] += term
        return carry

    lax.fori_loop(0, steps, step, 0)


def near_part(rows, group, slots, targets, halves, start, blocks, resident, out_type):
    classes, columns = start.shape
    leaves, width, size = targets.shape
    tiles = 24
    whole = pl.BlockSpec(memory_space=pltpu.VMEM)
    hbm = pl.BlockSpec(memory_space=pltpu.HBM)
    scratch = [
        pltpu.SMEM((slots.size // 2 + group, 4), jnp.int32),
        pltpu.SMEM((leaves,), jnp.int32),
        pltpu.SMEM((blocks.shape[0],), jnp.int32),
        pltpu.VMEM(targets.shape, BF16),
    ]
    if not resident:
        scratch.append(pltpu.VMEM(blocks.shape, BF16))
    scratch += [
        pltpu.SemaphoreType.DMA((leaves,)),
        pltpu.SemaphoreType.DMA((blocks.shape[0],)),
        pltpu.SemaphoreType.DMA((leaves,)),
    ]
    return call(
        functools.partial(near_kernel, rows, group, resident),
        "near",
        tiles * 2 * rows * size * (width + classes),
        tiles * rows * size,
        tiles * rows * width * 2 + 4 * 2**20,
        vmem=24,
        out_shape=out_type(start.shape, F32),
        in_specs=[
            pl.BlockSpec(memory_space=pltpu.SMEM),
            whole,
            hbm,
            hbm,
            whole if resident else hbm,
        ],
        out_specs=whole,
        scratch_shapes=scratch,
    )(
        in_hbm(slots),
        in_hbm(halves),
        in_hbm(targets),
        in_hbm(start),
        blocks if resident else in_hbm(blocks),
    )


def swap(value, axis, mask):
    pairs = [(source, source ^ mask) for source in range(lax.axis_size(axis))]
    return lax.ppermute(value, axis, pairs)


def per_device(points, weights, near, counts, skel_leaf, skel_local, skel_upper):
    leaves, rank = skel_leaf.shape
    size = points.shape[0] // leaves
    classes = weights.shape[0]
    slots = near.shape[1]
    sub_count = lax.axis_size("sub")
    grp_count = lax.axis_size("grp")
    sub_index = lax.axis_index("sub")
    grp_index = lax.axis_index("grp")
    device = grp_index * sub_count + sub_index

    slot_ids = jnp.arange(slots)
    owned = (
        (near // leaves == device)
        & (slot_ids[None, :] < counts[:, None])
        & (slot_ids[None, :] > 0)
    )
    chosen = jnp.where(owned, near - device * leaves, -1)
    chosen = jnp.max(chosen.reshape(sub_count * grp_count, leaves * slots), axis=1)

    def send(block):
        return lax.all_to_all(block, "sub", split_axis=0, concat_axis=0, tiled=True)

    arrived = [send(pack(chosen, points, weights, size, 0, PARTS[0]))]

    sub_bits = sub_count.bit_length() - 1
    far_bits = (sub_bits - 1) // 2
    steps = [1, sub_bits - 1 - far_bits, far_bits, grp_count.bit_length() - 1]
    table, starts, path_lengths = place_table(steps)
    mine = lax.dynamic_slice_in_dim(jnp.asarray(table), device, 1, 0)[0]
    *stage_rows, path_nodes = (mine[low:high] for low, high in zip(starts[:-1], starts[1:]))
    near_slots = jnp.concatenate(
        [
            lax.dynamic_slice_in_dim(near, device * leaves, leaves, 0),
            lax.dynamic_slice_in_dim(counts, device * leaves, leaves, 0)[:, None],
        ],
        axis=1,
    )

    own, skel, up, summary, targets, halves = leaf_level(points, weights, skel_leaf)
    lifted, terms, state = subtree(
        "local",
        leaves,
        leaves - 1,
        0,
        jnp.arange(leaves, dtype=jnp.int32),
        skel_local,
        (skel, summary),
        classes,
    )
    state, near_slots, stage_rows, path_nodes = lax.optimization_barrier(
        (state, near_slots, stage_rows, path_nodes)
    )

    def exchange(state, stage):
        axis = "grp" if stage + 1 == len(steps) else "sub"
        low = 0 if axis == "grp" else sum(steps[:stage])
        return [state] + [swap(state, axis, mask << low) for mask in range(1, 1 << steps[stage])]

    def climb(name, states, stage, rows):
        count = 1 << steps[stage]
        inner = count - 2 if stage + 1 == len(steps) else count - 1
        *done, state = subtree(name, count, inner, 2, rows, skel_upper, states, classes)
        return done, state

    core_stage, state = climb("core_nodes", exchange(state, 0), 0, stage_rows[0])
    x_states = exchange(state, 1)
    sent = [
        pack(chosen, points, weights, size, sum(PARTS[:part]), PARTS[part]) for part in (1, 2)
    ]
    sent, x_rows, x_states = lax.optimization_barrier((sent, stage_rows[1], x_states))
    arrived.append(send(sent[0]))
    x_stage, state = climb("x_nodes", x_states, 1, x_rows)
    y_states = exchange(state, 2)

    def near_sum(part, slots, start, out_type=pltpu.HBM):
        return near_part(
            PARTS[part], GROUP, slots, targets, halves, start, arrived[part], part == 2, out_type
        )

    near_slots, _ = lax.optimization_barrier((near_slots, state))
    total = near_sum(0, near_slots, own)
    sent_last, _, _ = lax.optimization_barrier((sent[1], y_states, total))
    arrived.append(send(sent_last))
    y_stage, state = climb("y_nodes", y_states, 2, stage_rows[2])
    z_states = exchange(state, 3)
    near_slots, _ = lax.optimization_barrier((near_slots, state))
    total = near_sum(1, near_slots, total)
    stages = [y_stage, x_stage, core_stage]
    total = down(
        stage_rows[3],
        path_nodes,
        skel_upper,
        path_lengths,
        z_states,
        stages,
        lifted,
        terms,
        up,
        total,
    )
    return near_sum(2, near_slots, total, jax.ShapeDtypeStruct)


def solution(mesh):
    split = P(("grp", "sub"), None)
    columns = P(None, ("grp", "sub"))
    return jax.shard_map(
        per_device,
        mesh=mesh,
        in_specs=(split, columns, P(), P(), split, split, P()),
        out_specs=columns,
        check_vma=False,
    )
```
